32 devices in a mesh: dp: 16 (over z, y, core), mp: 2 (over x).
Axes of the slice: x: 2, y: 2, z: 4, core: 2. Of those that a mesh axis runs over, the one named last changes fastest.
Arguments:
- inputs: bfloat16 [16, 512, 768], P('dp'), may hold values from -6 to 6
- encoded: bfloat16 [16, 512, 768], P('dp'), may hold values from -6 to 6
- cotangent: bfloat16 [16, 512, 768], P('dp'), may hold values from -6 to 6
- segments: int32 [16, 512], P('dp'), may hold values from 0 to 7, never falling along the last dimension, each value on 1 to 128 neighbouring positions
- padding: int32 [16, 512], P('dp'), may hold values 0 or 1
- task_ids: int32 [16], P('dp'), may hold values from 0 to 7, as said below
- token_weights: int32 [8], replicated, may hold values from 1 to 8
- gain_self: float32 [768], replicated, may hold values from 0.5 to 1.5
- gain_cross: float32 [768], replicated, may hold values from 0.5 to 1.5
- gain_ffn: float32 [768], replicated, may hold values from 0.5 to 1.5
- self_query: bfloat16 [768, 768], P('dp', 'mp'), may hold values from -0.21875 to 0.21875
- self_key: bfloat16 [768, 768], P('dp', 'mp'), may hold values from -0.21875 to 0.21875
- self_value: bfloat16 [768, 768], P('dp', 'mp'), may hold values from -0.21875 to 0.21875
- self_out: bfloat16 [768, 768], P('dp', 'mp'), may hold values from -0.625 to 0.625
- cross_query: bfloat16 [768, 768], P('dp', 'mp'), may hold values from -0.21875 to 0.21875
- cross_key: bfloat16 [768, 768], P('dp', 'mp'), may hold values from -0.21875 to 0.21875
- cross_value: bfloat16 [768, 768], P('dp', 'mp'), may hold values from -0.21875 to 0.21875
- cross_out: bfloat16 [768, 768], P('dp', 'mp'), may hold values from -0.625 to 0.625
- ffn_in: bfloat16 [768, 3072], P('dp', 'mp'), may hold values from -0.21875 to 0.21875
- ffn_out: bfloat16 [768, 3072], P('dp', 'mp'), may hold values from -0.109375 to 0.109375
- gen_down: bfloat16 [64, 18432], P(None, 'dp'), may hold values from -0.02734375 to 0.02734375
- gen_up: bfloat16 [64, 18432], P(None, 'dp'), may hold values from -0.15625 to 0.15625
- gen_gain: float32 [64, 768], replicated, may hold values from -0.1875 to 0.1875
- task_table: float32 [8, 64], replicated, may hold values from -6 to 6
- proj_first: float32 [64, 128], replicated, may hold values from -0.75 to 0.75
- proj_second: float32 [128, 64], replicated, may hold values from -0.75 to 0.75
Outputs:
- outputs: float32 [16, 512, 768], P('dp')
- grad_inputs: float32 [16, 512, 768], P('dp')
- grad_encoded: float32 [16, 512, 768], P('dp')
- grad_gain_self: float32 [768], replicated
- grad_gain_cross: float32 [768], replicated
- grad_gain_ffn: float32 [768], replicated
- grad_self_query: float32 [768, 768], P('dp', 'mp')
- grad_self_key: float32 [768, 768], P('dp', 'mp')
- grad_self_value: float32 [768, 768], P('dp', 'mp')
- grad_self_out: float32 [768, 768], P('dp', 'mp')
- grad_cross_query: float32 [768, 768], P('dp', 'mp')
- grad_cross_key: float32 [768, 768], P('dp', 'mp')
- grad_cross_value: float32 [768, 768], P('dp', 'mp')
- grad_cross_out: float32 [768, 768], P('dp', 'mp')
- grad_ffn_in: float32 [768, 3072], P('dp', 'mp')
- grad_ffn_out: float32 [768, 3072], P('dp', 'mp')
- grad_gen_down: float32 [64, 18432], P(None, 'dp')
- grad_gen_up: float32 [64, 18432], P(None, 'dp')
- grad_gen_gain: float32 [64, 768], replicated
- grad_task_table: float32 [8, 64], replicated
- grad_proj_first: float32 [64, 128], replicated
- grad_proj_second: float32 [128, 64], replicated
The draws below stay inside these ranges and needn't reach their ends.
Inputs may be any that keep to these rules, and one draw needn't show every extreme that they name: `task_ids`: the rows of one index of dp share one task; each task holds a nonempty run of consecutive indices of dp.
All inputs are finite; a program needn't handle non-finite values. No bound on the sum of `padding` on one device may be relied on, other than what follows from the above.
Results may differ from the reference program's by a relative error of at most 0.018.
Values may be sent and summed in bfloat16 or wider, within the bound.
No kernel may reach another device: no remote copies, remote signals or barrier semaphores. Data moves between devices by JAX's collectives and lax.ppermute only.
A program may use at most 192 MiB of HBM per device.

```python
import math
import jax
import jax.numpy as jnp
import numpy as np
from jax import lax

D = 768
HEADS = 12
HD = 64
FF = 3072
ADAPT = 24
EMBED = 64
PROJ = 128
TASKS = 8
LEN = 512
ROWS_DEV = 1
ROWS = 16


def draw_task_ids(key, part):
    devices = ROWS // ROWS_DEV
    order = jax.random.permutation(key, devices - 1)
    cuts = jnp.zeros((devices,), jnp.int32).at[order[:TASKS - 1] + 1].set(1)
    owner = jnp.cumsum(cuts).astype(jnp.int32)
    return jnp.repeat(owner, ROWS_DEV)


def touch_ends(values, own_key, low, top_value):
    dims = values.shape
    index_at = [jax.random.randint(jax.random.fold_in(own_key, axis), (), 0, dims[axis]) for axis in range(len(dims))]
    values = values.at[tuple(index_at)].set(low)
    longest = dims.index(max(dims))
    index_at[longest] = (index_at[longest] + 1) % dims[longest]
    return values.at[tuple(index_at)].set(top_value)


def steps_of(own_key, dims, pieces, smallest, high):
    def one(position, blocks):
        steps = jax.random.uniform(jax.random.fold_in(jax.random.fold_in(own_key, 6), position), (blocks,), jnp.float32, smallest / len(pieces), high / len(pieces))
        return jnp.repeat(jnp.exp(steps), dims[position] // blocks).reshape((-1,) + (1,) * (len(dims) - position - 1))

    factor_of = one(*pieces[0])
    for cut in pieces[1:]:
        factor_of = factor_of * one(*cut)
    return factor_of


def profile(amount, total, most, slope):
    loads = [(1 << 20) // math.isqrt(standing ** slope) + 1 for standing in range(2, amount + 1)]
    spare, given = total - most - (amount - 1), [1] * (amount - 1)
    while spare > 0:
        candidates = [i for i in range(amount - 1) if given[i] < most]
        mass, budget = sum([loads[i] for i in candidates]), spare
        for i in candidates:
            addition = min(most - given[i], max(1, budget * loads[i] // mass), spare)
            given[i] = given[i] + addition
            spare = spare - addition
    return np.array([most] + given)


def ragged_sizes(rng, number_of, total, most, skew):
    if number_of == 2:
        one = jax.random.randint(rng, (), max(1, total - most), min(most, total - 1) + 1)
        return jnp.stack([one, total - one])
    sizes = jnp.asarray(profile(number_of, total, most, skew), jnp.int32)
    pairs = (number_of - 1) // 2
    giver, taker = sizes[1:1 + 2 * pairs:2], sizes[2:2 + 2 * pairs:2]
    margin = jnp.minimum(giver - 1, most - taker)
    moved = jax.random.randint(jax.random.fold_in(rng, 1), (pairs,), 0, 1 << 20) % (margin + 1)
    sizes = sizes.at[1:1 + 2 * pairs:2].set(giver - moved).at[2:2 + 2 * pairs:2].set(taker + moved)
    return sizes[jax.random.permutation(jax.random.fold_in(rng, 2), number_of)]


def normal_values(key, shape, spread, limit, shards=(), held_as=jnp.bfloat16):
    values = spread * jax.random.normal(key, shape, jnp.float32)
    if shards:
        values = values * steps_of(key, shape, shards, -0.22, 0.18)
    return jnp.clip(values, -limit, limit).astype(held_as)


def setup_inputs(seed: int = 0) -> dict:
    streams_of = jax.random.split(jax.random.key(seed), 27)
    return {
        "inputs": normal_values(streams_of[0], (ROWS, LEN, D), 1.0, 6.0, ((0, 16),)),
        "encoded": normal_values(streams_of[1], (ROWS, LEN, D), 1.0, 6.0, ((0, 16),)),
        "cotangent": normal_values(streams_of[2], (ROWS, LEN, D), 1.0, 6.0, ((0, 16),)),
        "segments": jax.vmap(lambda own: jnp.searchsorted(jnp.cumsum(ragged_sizes(own, 8, LEN, LEN // 4, 2)), jnp.arange(LEN), side="right"))(jax.random.split(streams_of[3], ROWS)).reshape((ROWS, LEN)).astype(jnp.int32),
        "padding": touch_ends((jax.random.randint(streams_of[4], (ROWS, LEN), 0, 8) < 7).astype(jnp.int32), jax.random.fold_in(streams_of[4], 1), 0, 1),
        "task_ids": draw_task_ids(jax.random.fold_in(streams_of[26], 71), 0),
        "token_weights": touch_ends(jax.random.randint(streams_of[6], (TASKS,), 1, 9), jax.random.fold_in(streams_of[6], 1), 1, 8).astype(jnp.int32),
        "gain_self": jnp.clip(1.0 + 0.1 * jax.random.normal(streams_of[7], (D,), jnp.float32), 0.5, 1.5),
        "gain_cross": jnp.clip(1.0 + 0.1 * jax.random.normal(streams_of[8], (D,), jnp.float32), 0.5, 1.5),
        "gain_ffn": jnp.clip(1.0 + 0.1 * jax.random.normal(streams_of[9], (D,), jnp.float32), 0.5, 1.5),
        "self_query": normal_values(streams_of[10], (D, D), D ** -0.5, 0.21875, ((0, 16), (1, 2))),
        "self_key": normal_values(streams_of[11], (D, D), D ** -0.5, 0.21875, ((0, 16), (1, 2))),
        "self_value": normal_values(streams_of[12], (D, D), D ** -0.5, 0.21875, ((0, 16), (1, 2))),
        "self_out": normal_values(streams_of[13], (D, D), (D // 8) ** -0.5, 0.625, ((0, 16), (1, 2))),
        "cross_query": normal_values(streams_of[14], (D, D), D ** -0.5, 0.21875, ((0, 16), (1, 2))),
        "cross_key": normal_values(streams_of[15], (D, D), D ** -0.5, 0.21875, ((0, 16), (1, 2))),
        "cross_value": normal_values(streams_of[16], (D, D), D ** -0.5, 0.21875, ((0, 16), (1, 2))),
        "cross_out": normal_values(streams_of[17], (D, D), (D // 8) ** -0.5, 0.625, ((0, 16), (1, 2))),
        "ffn_in": normal_values(streams_of[18], (D, FF), D ** -0.5, 0.21875, ((0, 16), (1, 2))),
        "ffn_out": normal_values(streams_of[19], (D, FF), FF ** -0.5, 0.109375, ((0, 16), (1, 2))),
        "gen_down": normal_values(streams_of[20], (EMBED, D * ADAPT), (EMBED * D) ** -0.5, 0.02734375, ((1, 16),)),
        "gen_up": normal_values(streams_of[21], (EMBED, ADAPT * D), (EMBED * ADAPT) ** -0.5, 0.15625, ((1, 16),)),
        "gen_gain": normal_values(streams_of[22], (EMBED, D), (EMBED * 16) ** -0.5, 0.1875, (), jnp.float32),
        "task_table": normal_values(streams_of[23], (TASKS, EMBED), 1.0, 6.0, (), jnp.float32),
        "proj_first": normal_values(streams_of[24], (EMBED, PROJ), EMBED ** -0.5, 0.75, (), jnp.float32),
        "proj_second": normal_values(streams_of[25], (PROJ, EMBED), (PROJ // 2) ** -0.5, 0.75, (), jnp.float32),
    }


HIGHEST = lax.Precision.HIGHEST
EPSILON = 1e-06
MASKED = -1000000000.0

@jax.custom_vjp
def low(v):
    return lax.optimization_barrier(v.astype(jnp.bfloat16)).astype(jnp.float32)

@jax.custom_vjp
def low_back(v):
    return v

def low_keep(v):
    return (low(v), None)

def low_pass(kept, grad):
    return (grad,)

def back_keep(v):
    return (v, None)

def back_low(kept, grad):
    return (low(grad),)
low.defvjp(low_keep, low_pass)
low_back.defvjp(back_keep, back_low)

def normalize(value):
    return value * lax.rsqrt(lax.optimization_barrier(jnp.mean(value * value, axis=-1, keepdims=True)) + EPSILON)

def matmul(left, right):
    return jnp.matmul(left, right, precision=HIGHEST)

def build_masks(segments, padding):
    length = segments.shape[1]
    places = jnp.arange(length)
    same = segments[:, :, None] == segments[:, None, :]
    live = padding[:, None, :] == 1
    diagonal = (places[:, None] == places[None, :])[None]
    causal = (places[None, :] <= places[:, None])[None]
    return (same & live & causal | diagonal, same & live | diagonal)

def attend(queries, keys, values, mask):
    rows, length = (queries.shape[0], queries.shape[1])
    head_q = queries.reshape(rows, length, HEADS, HD)
    head_k = keys.reshape(rows, length, HEADS, HD)
    head_v = values.reshape(rows, length, HEADS, HD)
    scores = jnp.einsum('rqhd,rkhd->rhqk', head_q, head_k, precision=HIGHEST) * HD ** (-0.5)
    scores = low_back(jnp.where(mask[:, None], scores, MASKED))
    probs = jax.nn.softmax(scores, axis=-1)
    context = jnp.einsum('rhqk,rkhd->rqhd', low(probs), head_v, precision=HIGHEST)
    return context.reshape(rows, length, HEADS * HD)

def project_task(embedding, proj_first, proj_second):
    return matmul(jax.nn.gelu(matmul(embedding, proj_first)), proj_second)

def layer(params, stream, memory, segments, padding, tasks):
    gain_self, gain_cross, gain_ffn, self_query, self_key, self_value, self_out, cross_query, cross_key, cross_value, cross_out, ffn_in, ffn_out, gen_down, gen_up, gen_gain, task_table, proj_first, proj_second = params
    rows = stream.shape[0]
    self_mask, cross_mask = build_masks(segments, padding)
    first_in = low(normalize(stream) * gain_self)
    queries = low_back(low(matmul(first_in, self_query)))
    keys = low_back(low(matmul(first_in, self_key)))
    values = low_back(low(matmul(first_in, self_value)))
    context = low_back(low(attend(queries, keys, values, self_mask)))
    after_self = stream + low_back(matmul(context, self_out.T))
    second_in = low(normalize(after_self) * gain_cross)
    cross_q = low_back(low(matmul(second_in, cross_query)))
    cross_k = low_back(low(matmul(memory, cross_key)))
    cross_v = low_back(low(matmul(memory, cross_value)))
    cross_ctx = low_back(low(attend(cross_q, cross_k, cross_v, cross_mask)))
    after_cross = after_self + low_back(matmul(cross_ctx, cross_out.T))
    third_in = low(normalize(after_cross) * gain_ffn)
    inner = low_back(matmul(third_in, ffn_in))
    active = low(jax.nn.gelu(inner))
    after_ffn = after_cross + low_back(matmul(active, ffn_out.T))
    ident = project_task(task_table[tasks], proj_first, proj_second)
    ident_low = low(ident)
    down_gen = low_back(matmul(ident_low, gen_down)).reshape(rows, D, ADAPT)
    up_gen = low_back(matmul(ident_low, gen_up)).reshape(rows, ADAPT, D)
    gain_task = 1.0 + matmul(ident, gen_gain)
    adapt_in = low(normalize(after_ffn) * gain_task[:, None, :])
    bottle = low_back(jnp.einsum('rld,rda->rla', adapt_in, low(down_gen), precision=HIGHEST))
    bottle_act = low(jax.nn.gelu(bottle))
    added = low_back(jnp.einsum('rla,rad->rld', bottle_act, low(up_gen), precision=HIGHEST))
    return after_ffn + added

def reference(inputs, encoded, cotangent, segments, padding, task_ids, token_weights, gain_self, gain_cross, gain_ffn, self_query, self_key, self_value, self_out, cross_query, cross_key, cross_value, cross_out, ffn_in, ffn_out, gen_down, gen_up, gen_gain, task_table, proj_first, proj_second):
    params = tuple((item.astype(jnp.float32) for item in (gain_self, gain_cross, gain_ffn, self_query, self_key, self_value, self_out, cross_query, cross_key, cross_value, cross_out, ffn_in, ffn_out, gen_down, gen_up, gen_gain, task_table, proj_first, proj_second)))
    rows_all = inputs.shape[0]
    block = math.gcd(rows_all, max(1, 4096 // LEN))
    blocks = rows_all // block
    weights = token_weights.astype(jnp.float32)
    row_weight = weights[task_ids] * (TASKS / jnp.sum(weights))

    def split(value):
        return value.reshape((blocks, block) + value.shape[1:])

    def step(total, item):
        stream, memory, grad_out, segs, pads, tasks, scales = item

        def forward(theta, stream_in, memory_in):
            return layer(theta, stream_in, memory_in, segs, pads, tasks)
        result, pull = jax.vjp(forward, params, stream, memory)
        weight_out = scales[:, None, None] * pads[:, :, None].astype(jnp.float32)
        grad_params, grad_stream, grad_memory = pull(grad_out * weight_out)
        total = jax.tree.map(lambda left, right: left + right, total, grad_params)
        return (total, (result, grad_stream, grad_memory))
    start = jax.tree.map(jnp.zeros_like, params)
    items = (split(inputs.astype(jnp.float32)), split(encoded.astype(jnp.float32)), split(cotangent.astype(jnp.float32)), split(segments), split(padding), split(task_ids), split(row_weight))
    totals, (results, grad_stream, grad_memory) = lax.scan(step, start, items)
    factor = 1.0 / math.sqrt(rows_all * LEN)
    shape = (rows_all, LEN, D)
    grads = tuple((item * factor for item in totals))
    return (results.reshape(shape), grad_stream.reshape(shape), grad_memory.reshape(shape), grads[0], grads[1], grads[2], grads[3], grads[4], grads[5], grads[6], grads[7], grads[8], grads[9], grads[10], grads[11], grads[12], grads[13], grads[14], grads[15], grads[16], grads[17], grads[18])
```

```python
import math

import jax
import jax.numpy as jnp
from jax import lax
from jax.sharding import Mesh
from jax.sharding import PartitionSpec as P

HD = 64
ADAPT = 24
HIGHEST = lax.Precision.HIGHEST
EPSILON = 1e-06
MASKED = -1000000000.0
LOW = jnp.bfloat16
WIDE = jnp.float32
CHIP, CORE, PAIR = "chip", "core", "mp"
ACROSS = [(0, 1), (1, 0)]


def rstd_of(value):
    return lax.rsqrt(jnp.mean(value * value, axis=-1, keepdims=True) + EPSILON)


def norm_grad(normed, rstd, grad):
    return rstd * (grad - normed * jnp.mean(grad * normed, axis=-1, keepdims=True))


def gelu_grad(value, grad):
    return jax.vjp(jax.nn.gelu, value)[1](grad)[0]


def product(left, right):
    return jnp.dot(left, right, preferred_element_type=WIDE)


def times_rows(left, right):
    return lax.dot_general(left, right, (((1,), (1,)), ((), ())), preferred_element_type=WIDE)


def inner_rows(left, right):
    return lax.dot_general(left, right, (((0,), (0,)), ((), ())), preferred_element_type=WIDE)


def exact(left, right, dims=((1,), (0,))):
    return lax.dot_general(left, right, (dims, ((), ())), precision=HIGHEST, preferred_element_type=WIDE)


def build_masks(segments, padding):
    length = segments.shape[0]
    places = jnp.arange(length)
    same = segments[:, None] == segments[None, :]
    live = padding[None, :] == 1
    diagonal = places[:, None] == places[None, :]
    causal = places[None, :] <= places[:, None]
    return (same & live & causal | diagonal, same & live | diagonal)


def masked_scores(queries, keys, mask, factor):
    scores = jnp.einsum("qhd,khd->hqk", queries, keys, preferred_element_type=WIDE) * factor
    return jnp.where(mask[None], scores, MASKED)


def attend_forward(queries, keys, values, mask, factor):
    scores = masked_scores(queries, keys, mask, factor)
    top = jnp.max(scores, axis=-1, keepdims=True)
    expos = jnp.exp(scores - top)
    total = jnp.sum(expos, axis=-1, keepdims=True)
    probs = (expos / total).astype(LOW)
    context = jnp.einsum("hqk,khd->qhd", probs, values, preferred_element_type=WIDE)
    return (context.astype(LOW), top + jnp.log(total))


def attend_backward(queries, keys, values, mask, factor, logsum, grad_ctx):
    probs = jnp.exp(masked_scores(queries, keys, mask, factor) - logsum)
    grad_probs = jnp.einsum("qhd,khd->hqk", grad_ctx, values, preferred_element_type=WIDE)
    grad_values = jnp.einsum("hqk,qhd->khd", probs.astype(LOW), grad_ctx, preferred_element_type=WIDE)
    centre = jnp.sum(probs * grad_probs, axis=-1, keepdims=True)
    grad_scores = (probs * (grad_probs - centre)).astype(LOW)
    grad_queries = jnp.einsum("hqk,khd->qhd", grad_scores, keys, preferred_element_type=WIDE) * factor
    grad_keys = jnp.einsum("hqk,qhd->khd", grad_scores, queries, preferred_element_type=WIDE) * factor
    return (grad_queries.astype(LOW), grad_keys.astype(LOW), grad_values.astype(LOW))


def swap_core(value):
    return lax.ppermute(value, CORE, ACROSS)


def swap_pair(value):
    return lax.ppermute(value, PAIR, ACROSS)


def solution(mesh):
    dp, mp = mesh.devices.shape
    chips = dp // 2
    grid = Mesh(mesh.devices.reshape(chips, 2, mp), (CHIP, CORE, PAIR))
    ring = chips == 8

    def local(
        inputs, encoded, cotangent, segments, padding, task_ids, token_weights, gain_self, gain_cross, gain_ffn,
        self_query, self_key, self_value, self_out, cross_query, cross_key, cross_value, cross_out, ffn_in, ffn_out,
        gen_down, gen_up, gen_gain, task_table, proj_first, proj_second,
    ):
        rows, length, width = inputs.shape
        half = length // 2
        core = lax.axis_index(CORE)
        chip = lax.axis_index(CHIP)
        first = core == 0
        factor = HD ** (-0.5)
        tasks_all = task_table.shape[0]
        local_rows = self_query.shape[0]
        chip_rows = 2 * local_rows
        quarter = self_query.shape[1] // 2
        heads_here = quarter // HD

        def order(mine, other, axis=0):
            return jnp.where(
                first, jnp.concatenate([mine, other], axis), jnp.concatenate([other, mine], axis)
            )

        def part_of(value, index, size, axis=0):
            return lax.dynamic_slice_in_dim(value, index * size, size, axis)

        def join(value):
            return order(value, swap_core(value))

        def pack(weights, extra=None):
            keep = [part_of(w, core, w.shape[1] // 2, 1) for w in weights]
            send = [part_of(w, 1 - core, w.shape[1] // 2, 1) for w in weights]
            if extra is not None:
                keep.append(jnp.where(first, extra[0], extra[1]))
                send.append(jnp.where(first, extra[1], extra[0]))
            keep, send = jnp.concatenate(keep, 1), jnp.concatenate(send, 1)
            return order(keep, swap_core(send))

        turn = [(k, (k + 2) % chips) for k in range(chips)]
        side = [(k, k ^ 1) for k in range(chips)]

        def gather_chips(shard):
            if not ring:
                return lax.all_gather(shard, CHIP, axis=0, tiled=True)
            held = [shard]
            for _ in range(3):
                held.append(lax.ppermute(held[-1], CHIP, turn))
            other = [lax.ppermute(h, CHIP, side) for h in held]
            rows_here = shard.shape[0]
            full = jnp.zeros((chips * rows_here, shard.shape[1]), shard.dtype)
            z, y = chip // 2, chip % 2
            for step in range(4):
                at = ((z - step) % 4) * 2
                full = lax.dynamic_update_slice_in_dim(full, held[step], (at + y) * rows_here, 0)
                full = lax.dynamic_update_slice_in_dim(full, other[step], (at + 1 - y) * rows_here, 0)
            return full

        def scatter_chips(full):
            if not ring:
                return lax.psum_scatter(full.astype(LOW), CHIP, scatter_dimension=0, tiled=True)
            z, y = chip // 2, chip % 2
            blocks = full.reshape(4, 2, chip_rows, full.shape[1])
            away = lax.dynamic_index_in_dim(blocks, 1 - y, 1, keepdims=False).astype(LOW)
            mine = lax.dynamic_index_in_dim(blocks, y, 1, keepdims=False)
            mine = (mine.astype(WIDE) + lax.ppermute(away, CHIP, side).astype(WIDE)).astype(LOW)

            def block(step):
                return lax.dynamic_index_in_dim(mine, (z - step) % 4, 0, keepdims=False)

            held = block(1)
            for step in (2, 3, 4):
                moved = lax.ppermute(held, CHIP, turn)
                held = (moved.astype(WIDE) + block(step).astype(WIDE)).astype(LOW)
            return held

        def unpack(shard, widths):
            keep = part_of(shard, core, local_rows)
            moved = swap_core(part_of(shard, 1 - core, local_rows))
            found, at = [], 0
            for size in widths:
                found.append(order(keep[:, at : at + size], moved[:, at : at + size], 1))
                at += size
            return found

        def all_sum(value):
            value = value + swap_core(value)
            bit = 1
            while bit < chips:
                value = value + lax.ppermute(value, CHIP, [(k, k ^ bit) for k in range(chips)])
                bit *= 2
            return value

        def project(table, one, two):
            return exact(jax.nn.gelu(exact(table, one)), two)

        ident_all, project_pull = jax.vjp(project, task_table, proj_first, proj_second)
        ident_low_all = ident_all.astype(LOW)
        gain_all = 1.0 + exact(ident_all, gen_gain)

        def spread(generator):
            made = product(ident_low_all, generator).astype(LOW)
            made = made.reshape(tasks_all, local_rows, ADAPT).transpose(1, 0, 2)
            return made.reshape(local_rows, tasks_all * ADAPT)

        shard_self = pack([self_query, self_key, self_value, self_out])
        shard_cross = pack([cross_query, cross_key, cross_value, cross_out])
        shard_ffn = pack([ffn_in, ffn_out], (spread(gen_down), spread(gen_up)))
        full_self = gather_chips(shard_self)
        full_cross = gather_chips(shard_cross)
        full_ffn = gather_chips(shard_ffn)
        w_qkv, w_out = full_self[:, : 3 * quarter], full_self[:, 3 * quarter :]
        c_query, c_kv, c_out = full_cross[:, :quarter], full_cross[:, quarter : 3 * quarter], full_cross[:, 3 * quarter :]
        ffn_quarter = ffn_in.shape[1] // 2
        w_inner, w_outer = full_ffn[:, :ffn_quarter], full_ffn[:, ffn_quarter : 2 * ffn_quarter]
        generated = full_ffn[:, 2 * ffn_quarter :].reshape(width, tasks_all, ADAPT)

        words = jnp.concatenate([segments, padding, jnp.broadcast_to(task_ids[:, None], (1, length))], 0)
        words_other = swap_core(words)
        words = [jnp.where(first, words, words_other), jnp.where(first, words_other, words)]
        own, memory = inputs.reshape(length, width), encoded.reshape(length, width)
        own_other, memory_other = swap_core(own), swap_core(memory)
        streams = [jnp.where(first, own, own_other), jnp.where(first, own_other, own)]
        memories = [jnp.where(first, memory, memory_other), jnp.where(first, memory_other, memory)]
        goal = cotangent.reshape(length, width)
        goal_mine = part_of(goal, core, half)
        goal_other = swap_core(part_of(goal, 1 - core, half))
        goals = [jnp.where(first, goal_mine, goal_other), jnp.where(first, goal_other, goal_mine)]
        weights = token_weights.astype(WIDE)
        onehots = [(w[2, 0] == jnp.arange(tasks_all)).astype(WIDE) for w in words]

        def pair_sum(partial):
            away = swap_core(part_of(partial, 1 - core, half).astype(LOW))
            both = (part_of(partial, core, half) + away.astype(WIDE)).astype(LOW)
            return both.astype(WIDE) + swap_pair(both).astype(WIDE)

        def heads(value):
            return value.reshape(length, heads_here, HD)

        def flat(value):
            return value.reshape(length, quarter)

        both = range(2)
        masks = [build_masks(w[0], w[1]) for w in words]
        kept = [dict() for _ in both]

        def forward_self(r):
            k = kept[r]
            x = streams[r].astype(WIDE)
            first_in = (x * rstd_of(x) * gain_self).astype(LOW)
            qkv = product(first_in, w_qkv).astype(LOW)
            q, key, v = (heads(qkv[:, i * quarter : (i + 1) * quarter]) for i in range(3))
            context, logsum = attend_forward(q, key, v, masks[r][0], factor)
            context = flat(context)
            k.update(first_in=first_in, q=q, k=key, v=v, context=context, lse=logsum)
            k["x"] = part_of(streams[r], core, half).astype(WIDE)
            k["after_self"] = k["x"] + pair_sum(times_rows(context, w_out))

        def forward_cross(r):
            k = kept[r]
            value = k["after_self"]
            k["rstd_a"] = rstd_of(value)
            k["normed_a"] = value * k["rstd_a"]
            k["second_in"] = join((k["normed_a"] * gain_cross).astype(LOW))
            kv = product(memories[r], c_kv).astype(LOW)
            ck, cv = heads(kv[:, :quarter]), heads(kv[:, quarter:])
            cq = heads(product(k["second_in"], c_query).astype(LOW))
            context, logsum = attend_forward(cq, ck, cv, masks[r][1], factor)
            context = flat(context)
            k.update(cq=cq, ck=ck, cv=cv, c_context=context, c_lse=logsum)
            k["after_cross"] = value + pair_sum(times_rows(context, c_out))

        def forward_ffn(r):
            k = kept[r]
            value = k["after_cross"]
            k["rstd_b"] = rstd_of(value)
            k["normed_b"] = value * k["rstd_b"]
            k["third_in"] = join((k["normed_b"] * gain_ffn).astype(LOW))
            k["inner"] = product(k["third_in"], w_inner)
            k["active"] = jax.nn.gelu(k["inner"]).astype(LOW)
            k["after_ffn"] = value + pair_sum(times_rows(k["active"], w_outer))

        picked = [
            lax.dynamic_index_in_dim(generated, words[r][2, 0], 1, keepdims=False) for r in both
        ]
        picked = jnp.concatenate(picked, 1)
        picked_other = swap_core(picked)
        downs = jnp.where(first, picked, picked_other)
        ups = jnp.where(first, picked_other, picked)

        def adapter(r):
            k = kept[r]
            down_gen = downs[:, r * ADAPT : (r + 1) * ADAPT]
            up_gen = ups[:, r * ADAPT : (r + 1) * ADAPT].reshape(ADAPT, width)
            gain_task = exact(onehots[r][None], gain_all)
            value = k["after_ffn"]
            rstd = rstd_of(value)
            normed = value * rstd
            adapt_in = (normed * gain_task).astype(LOW)
            bottle = product(adapt_in, down_gen)
            bottle_act = jax.nn.gelu(bottle).astype(LOW)
            k["outputs"] = value + product(bottle_act, up_gen)
            row_weight = jnp.sum(onehots[r] * weights) * (tasks_all / jnp.sum(weights))
            pads = part_of(words[r][1], core, half).astype(WIDE)
            grad_out = goals[r].astype(WIDE) * (row_weight * pads[:, None])
            out_low = grad_out.astype(LOW)
            grad_act = times_rows(out_low, up_gen)
            k["grad_up"] = inner_rows(bottle_act, out_low)
            grad_bottle = gelu_grad(bottle, grad_act).astype(LOW)
            k["grad_down"] = inner_rows(adapt_in, grad_bottle)
            grad_in = times_rows(grad_bottle, down_gen)
            k["grad_gain"] = jnp.sum(grad_in * normed, axis=0)
            k["grad_ffn"] = grad_out + norm_grad(normed, rstd, grad_in * gain_task)

        def backward_ffn(r):
            k = kept[r]
            k["ffn_low"] = join(k["grad_ffn"].astype(LOW))
            k["grad_inner"] = gelu_grad(k["inner"], product(k["ffn_low"], w_outer)).astype(LOW)
            grad_third = pair_sum(times_rows(k["grad_inner"], w_inner))
            k["g3"] = jnp.sum(grad_third * k["normed_b"], axis=0)
            k["grad_cross"] = k["grad_ffn"] + norm_grad(k["normed_b"], k["rstd_b"], grad_third * gain_ffn)

        def backward_cross(r):
            k = kept[r]
            k["cross_low"] = join(k["grad_cross"].astype(LOW))
            grad_ctx = heads(product(k["cross_low"], c_out).astype(LOW))
            gq, gk, gv = attend_backward(k["cq"], k["ck"], k["cv"], masks[r][1], factor, k["c_lse"], grad_ctx)
            gq, gk, gv = flat(gq), flat(gk), flat(gv)
            k["gcq"], k["gckv"] = gq, jnp.concatenate([gk, gv], 1)
            grad_second = pair_sum(times_rows(gq, c_query))
            k["g2"] = jnp.sum(grad_second * k["normed_a"], axis=0)
            k["grad_self"] = k["grad_cross"] + norm_grad(k["normed_a"], k["rstd_a"], grad_second * gain_cross)
            k["grad_memory"] = pair_sum(times_rows(k["gckv"], c_kv))

        def backward_self(r):
            k = kept[r]
            k["self_low"] = join(k["grad_self"].astype(LOW))
            grad_ctx = heads(product(k["self_low"], w_out).astype(LOW))
            gq, gk, gv = attend_backward(k["q"], k["k"], k["v"], masks[r][0], factor, k["lse"], grad_ctx)
            k["gqkv"] = jnp.concatenate([flat(gq), flat(gk), flat(gv)], 1)
            grad_first = pair_sum(times_rows(k["gqkv"], w_qkv))
            rstd = rstd_of(k["x"])
            normed = k["x"] * rstd
            k["g1"] = jnp.sum(grad_first * normed, axis=0)
            k["grad_x"] = k["grad_self"] + norm_grad(normed, rstd, grad_first * gain_self)

        for stage in (forward_self, forward_cross, forward_ffn, adapter, backward_ffn):
            for r in both:
                stage(r)

        def over_rows(left, right):
            return sum(inner_rows(kept[r][left], kept[r][right]) for r in both)

        def by_task(name, shape):
            stacked = [
                kept[r][name].reshape(width, 1, ADAPT) * onehots[r][None, :, None] for r in both
            ]
            return (stacked[0] + stacked[1]).reshape(width, tasks_all * ADAPT).astype(LOW)

        tasks_down, tasks_up = by_task("grad_down", None), by_task("grad_up", None)
        tasks_here = jnp.where(first, tasks_down, tasks_up).astype(WIDE)
        tasks_here = tasks_here + swap_core(jnp.where(first, tasks_up, tasks_down)).astype(WIDE)
        sum_ffn = scatter_chips(
            jnp.concatenate(
                [over_rows("third_in", "grad_inner"), over_rows("ffn_low", "active"), tasks_here], 1
            )
        )
        for r in both:
            backward_cross(r)
        for r in both:
            kept[r]["memory"] = memories[r]
        sum_cross = scatter_chips(
            jnp.concatenate(
                [over_rows("second_in", "gcq"), over_rows("memory", "gckv"), over_rows("cross_low", "c_context")], 1
            )
        )
        for r in both:
            backward_self(r)
        sum_self = scatter_chips(
            jnp.concatenate([over_rows("first_in", "gqkv"), over_rows("self_low", "context")], 1)
        )
        scale = 1.0 / math.sqrt(rows * dp * length)

        grads_self = unpack(sum_self, [quarter] * 4)
        grads_cross = unpack(sum_cross, [quarter] * 4)
        tasks_wide = tasks_all * ADAPT
        grad_in, grad_outer, found = unpack(sum_ffn, [ffn_quarter, ffn_quarter, tasks_wide])

        def narrow(value):
            value = value.reshape(local_rows, tasks_all, ADAPT).transpose(1, 0, 2)
            return value.reshape(tasks_all, local_rows * ADAPT)

        found_down, found_up = narrow(found[:, :tasks_wide]), narrow(found[:, tasks_wide:])
        grad_gen_down = inner_rows(ident_low_all, found_down)
        grad_gen_up = inner_rows(ident_low_all, found_up)
        ident_part = times_rows(found_down, gen_down) + times_rows(found_up, gen_up)
        gain_part = sum(onehots[r][:, None] * kept[r]["grad_gain"][None] for r in both)
        norms = [sum(kept[r][name] for r in both)[None] for name in ("g1", "g2", "g3")]
        early = all_sum(jnp.concatenate([gain_part, jnp.pad(ident_part, ((0, 0), (0, width - ident_part.shape[1])))], 0))
        gain_sum, ident_sum = early[:tasks_all], early[tasks_all:, : ident_part.shape[1]]
        norm_sums = all_sum(jnp.concatenate(norms, 0)) * scale
        grad_gen_gain = exact(ident_all, gain_sum, ((0,), (0,))) * scale
        grad_ident = ident_sum + exact(gain_sum, gen_gain, ((1,), (1,)))
        grad_table, grad_first_m, grad_second_m = project_pull(grad_ident)

        def place(name):
            one, two = kept[0][name], kept[1][name]
            moved = swap_core(jnp.where(first, two, one))
            return order(jnp.where(first, one, two), moved).reshape(rows, length, width)

        def out(value):
            return value.astype(WIDE) * scale

        return (
            place("outputs"), place("grad_x"), place("grad_memory"),
            norm_sums[0], norm_sums[1], norm_sums[2],
            *(out(g) for g in grads_self), *(out(g) for g in grads_cross),
            out(grad_in), out(grad_outer), out(grad_gen_down), out(grad_gen_up),
            grad_gen_gain, grad_table * scale, grad_first_m * scale, grad_second_m * scale,
        )

    data = (CHIP, CORE)
    three, matrix = P(data, None, None), P(data, PAIR)
    in_specs = (
        three, three, three, P(data, None), P(data, None), P(data), P(), P(), P(), P(),
        *(matrix,) * 10, P(None, data), P(None, data), P(), P(), P(), P(),
    )
    out_specs = (
        three, three, three, P(), P(), P(), *(matrix,) * 10, P(None, data), P(None, data), P(), P(), P(), P(),
    )
    return jax.shard_map(local, mesh=grid, in_specs=in_specs, out_specs=out_specs, check_vma=False)
```

```python
import functools
import math

import jax
import jax.numpy as jnp
from jax import lax
from jax.experimental import pallas as pl
from jax.experimental.pallas import tpu as pltpu
from jax.sharding import Mesh
from jax.sharding import PartitionSpec as P

HD = 64
ADAPT = 24
HIGHEST = lax.Precision.HIGHEST
EPSILON = 1e-06
MASKED = -1000000000.0
LOW = jnp.bfloat16
WIDE = jnp.float32
CHIP, CORE, PAIR = "chip", "core", "mp"
ACROSS = [(0, 1), (1, 0)]
SPAN = 128
ROOT = math.sqrt(2.0 / math.pi)


def dot(left, right):
    return lax.dot_general(left, right, (((1,), (0,)), ((), ())), preferred_element_type=WIDE)


def dot_rows(left, right):
    return lax.dot_general(left, right, (((1,), (1,)), ((), ())), preferred_element_type=WIDE)


def dot_inner(left, right):
    return lax.dot_general(left, right, (((0,), (0,)), ((), ())), preferred_element_type=WIDE)


def exact(left, right, dims=((1,), (0,))):
    return lax.dot_general(left, right, (dims, ((), ())), precision=HIGHEST, preferred_element_type=WIDE)


def rstd_of(value):
    return lax.rsqrt(jnp.mean(value * value, axis=-1, keepdims=True) + EPSILON)


def gelu_parts(value):
    square = value * value
    slope = jnp.tanh(ROOT * (value + 0.044715 * square * value))
    half = 0.5 * (1.0 + slope)
    return value * half, half + 0.5 * value * (1.0 - slope * slope) * ROOT * (1.0 + 0.134145 * square)


def shape(dims, dtype):
    return jax.ShapeDtypeStruct(dims, dtype)


class Cols:
    def __init__(self, array, start, stop):
        self.array, self.start, self.stop = array, start, stop


class Pick:
    def __init__(self, row, own, other):
        self.row, self.own, self.other = row, own, other


class Pieces:
    def __init__(self, held, other):
        self.blocks = [*held, *other]
        self.size = held[0].shape[0]
        self.shape = (len(self.blocks) * self.size, held[0].shape[1])
        self.dtype = held[0].dtype

    def places(self, where):
        part = self.size // 2
        for index in range(len(self.blocks)):
            z = lax.rem(where[1] + 4 - index % 4, 4)
            y = where[2] if index < 4 else 1 - where[2]
            for side in range(2):
                turn = where[0] if side == 0 else 1 - where[0]
                at = pl.multiple_of((2 * z + y) * self.size + turn * part, 16)
                yield index, slice(side * part, (side + 1) * part), pl.ds(at, part)


class Owned:
    def __init__(self, row, aval, into):
        self.row, self.aval, self.into = row, aval, into


class Routed:
    def __init__(self, row, aval, into):
        self.row, self.aval, self.into = row, aval, into


class Box:
    def __init__(self, ref, copies):
        self.ref, self.copies, self.pending = ref, copies, False

    def each(self, act):
        for condition, copy in self.copies:
            if condition is None:
                act(copy)
            else:
                pl.when(condition)(functools.partial(act, copy))

    def start(self):
        self.each(lambda copy: copy.start())
        self.pending = True

    def wait(self):
        if self.pending:
            self.each(lambda copy: copy.wait())
            self.pending = False

    def get(self):
        self.wait()
        return self.ref

    def put(self, value):
        self.ref[...] = value
        self.start()


VMEM_LIMIT = 60 * 1024 * 1024


def call(body, outs, where, *args, after=(), flops=0, scratch=()):
    inputs, buffers, loads = [], [], []
    for arg in args:
        if isinstance(arg, Pick):
            loads.append((arg, len(inputs)))
            inputs += [arg.own, arg.other]
            buffers.append((arg.own.shape, arg.own.dtype))
        elif isinstance(arg, Cols):
            loads.append((arg, len(inputs)))
            inputs.append(arg.array)
            buffers.append(((arg.array.shape[0], arg.stop - arg.start), arg.array.dtype))
        elif isinstance(arg, Pieces):
            loads.append((arg, len(inputs)))
            inputs += arg.blocks
            buffers.append((arg.shape, arg.dtype))
        else:
            loads.append((arg, len(inputs)))
            inputs.append(arg)
            buffers.append((arg.shape, arg.dtype))
    avals, stores, aliases = [], [], {}
    for out in outs:
        special = isinstance(out, (Owned, Routed))
        aval = out.aval if special else out
        stores.append((out, len(avals)))
        buffers.append((aval.shape, aval.dtype))
        if special and out.into is not None:
            for array in out.into:
                aliases[1 + len(inputs)] = len(avals)
                inputs.append(array)
                avals.append(aval)
        else:
            avals += [aval] * (2 if isinstance(out, Routed) else 1)
    many = sum(2 * len(a.blocks) for a in args if isinstance(a, Pieces))
    moved = sum(math.prod(dims) * jnp.dtype(dtype).itemsize for dims, dtype in buffers)
    inputs += after

    def kernel(where_ref, *refs):
        in_refs, refs = refs[: len(inputs)], refs[len(inputs) :]
        out_refs, refs = refs[: len(avals)], refs[len(avals) :]
        own, refs = refs[: len(scratch)], refs[len(scratch) :]
        held, sems = refs[:-1], refs[-1]
        boxes, extra = [], len(buffers)
        for n, (arg, at) in enumerate(loads):
            if isinstance(arg, Pieces):
                copies = []
                for index, rows, place in arg.places(where_ref):
                    source, target = in_refs[at + index].at[rows, :], held[n].at[place, :]
                    copies.append((None, pltpu.make_async_copy(source, target, sems.at[extra])))
                    extra += 1
                boxes.append(Box(held[n], copies))
                boxes[-1].start()
                continue
            if isinstance(arg, Pick):
                mine = where_ref[0] == arg.row
                pairs = [(mine, in_refs[at]), (jnp.logical_not(mine), in_refs[at + 1])]
            elif isinstance(arg, Cols):
                pairs = [(None, in_refs[at].at[:, arg.start : arg.stop])]
            else:
                pairs = [(None, in_refs[at])]
            boxes.append(Box(held[n], [(c, pltpu.make_async_copy(s, held[n], sems.at[n])) for c, s in pairs]))
            boxes[-1].start()
        for n, (out, at) in enumerate(stores, len(loads)):
            pairs = [(None, out_refs[at])]
            if isinstance(out, (Owned, Routed)):
                mine = where_ref[0] == out.row
                pairs = [(mine, out_refs[at])]
                if isinstance(out, Routed):
                    pairs.append((jnp.logical_not(mine), out_refs[at + 1]))
            boxes.append(Box(held[n], [(c, pltpu.make_async_copy(held[n], d, sems.at[n])) for c, d in pairs]))
        body(where_ref, *boxes, *own)
        for box in boxes:
            box.wait()

    hbm = pl.BlockSpec(memory_space=pltpu.HBM)
    return pl.pallas_call(
        kernel,
        out_shape=tuple(avals),
        in_specs=[pl.BlockSpec(memory_space=pltpu.SMEM)] + [hbm] * len(inputs),
        out_specs=tuple(hbm for _ in avals),
        scratch_shapes=[*scratch, *(pltpu.VMEM(*b) for b in buffers), pltpu.SemaphoreType.DMA((len(buffers) + many,))],
        input_output_aliases=aliases,
        compiler_params=pltpu.CompilerParams(vmem_limit_bytes=VMEM_LIMIT),
        cost_estimate=pl.CostEstimate(flops=flops, bytes_accessed=moved, transcendentals=0),
    )(where, *inputs)


def at_half(core, half):
    return pl.ds(pl.multiple_of(core * half, half), half)


def windows(length, causal):
    for lo in range(0, length, SPAN):
        yield lo, max(lo - SPAN, 0), lo + SPAN if causal else min(lo + 2 * SPAN, length)


def mask_of(segq_ref, segk_ref, lo, start, stop, causal):
    dims = (stop - start, SPAN)
    keys = start + lax.broadcasted_iota(jnp.int32, dims, 0)
    queries = lo + lax.broadcasted_iota(jnp.int32, dims, 1)
    same = segk_ref[start:stop, :] == segq_ref[:, lo : lo + SPAN]
    if causal:
        same = same & (keys <= queries)
    return same | (keys == queries)


def beside(parts):
    return jnp.concatenate(parts, axis=1)


def lanes(value, count):
    return [value[:, i * SPAN : (i + 1) * SPAN] for i in range(count)]


def attend(q_at, k_at, v_at, segq_ref, segk_ref, context_ref, lse_ref, causal, heads, factor):
    for lo, start, stop in windows(context_ref.shape[0], causal):
        mask = beside([mask_of(segq_ref, segk_ref, lo, start, stop, causal)] * heads)
        scores = beside([dot_rows(k_at(h, start, stop), q_at(h, lo, lo + SPAN) * LOW(factor)) for h in range(heads)])
        scores = jnp.where(mask, scores, MASKED)
        top = jnp.max(scores, axis=0, keepdims=True)
        expos = jnp.exp(scores - top)
        total = jnp.sum(expos, axis=0, keepdims=True)
        probs = (expos * (1.0 / total)).astype(LOW)
        logs = lanes(top + jnp.log(total), heads)
        for h, part in enumerate(lanes(probs, heads)):
            context_ref[lo : lo + SPAN, h * HD : (h + 1) * HD] = dot_inner(part, v_at(h, start, stop)).astype(LOW)
            lse_ref[h : h + 1, lo : lo + SPAN] = logs[h]


def attend_back(q_at, k_at, v_at, g_at, segq_ref, segk_ref, lse_ref, gq_ref, gk_ref, gv_ref, causal, heads, factor):
    gk_ref[...] = jnp.zeros_like(gk_ref)
    gv_ref[...] = jnp.zeros_like(gv_ref)
    for lo, start, stop in windows(lse_ref.shape[1], causal):
        mask = beside([mask_of(segq_ref, segk_ref, lo, start, stop, causal)] * heads)
        queries = [q_at(h, lo, lo + SPAN) * LOW(factor) for h in range(heads)]
        keys = [k_at(h, start, stop) for h in range(heads)]
        grads = [g_at(h, lo, lo + SPAN) for h in range(heads)]
        scores = beside([dot_rows(keys[h], queries[h]) for h in range(heads)])
        logs = beside([lse_ref[h : h + 1, lo : lo + SPAN] for h in range(heads)])
        probs = jnp.exp(jnp.where(mask, scores, MASKED) - logs)
        grad_probs = beside([dot_rows(v_at(h, start, stop), grads[h]) for h in range(heads)])
        centre = jnp.sum(probs * grad_probs, axis=0, keepdims=True)
        grad_scores = lanes((probs * (grad_probs - centre)).astype(LOW), heads)
        for h, part in enumerate(lanes(probs.astype(LOW), heads)):
            cols = slice(h * HD, (h + 1) * HD)
            gv_ref[start:stop, cols] += dot(part, grads[h])
            gk_ref[start:stop, cols] += dot(grad_scores[h], queries[h])
            gq_ref[lo : lo + SPAN, cols] = (dot_inner(grad_scores[h], keys[h]) * factor).astype(LOW)


def columns(ref, at):
    return lambda h, lo, hi: ref[lo:hi, at + h * HD : at + (h + 1) * HD]


def branch(core, pack, total_ref):
    mine, other, far, far_other = pack
    total_ref[...] = (mine.get()[...].astype(WIDE) + other.get()[...].astype(WIDE)).astype(LOW).astype(WIDE)
    half = far.ref.shape[0]
    total_ref[at_half(core, half), :] += far.get()[...].astype(WIDE)
    total_ref[at_half(1 - core, half), :] += far_other.get()[...].astype(WIDE)
    return total_ref[...]


def wide(box):
    return box.get()[...].astype(WIDE)


def self_forward(heads, factor, where, own, gain, w, segq, segk, first, qkv, context, lse, part, *whole):
    third = heads * HD
    value = wide(own)
    first.put((value * rstd_of(value) * gain.get()[...]).astype(LOW))
    w_ref = w.get()
    qkv.put(dot(first.ref[...], w_ref[:, : 3 * third]).astype(LOW))
    attend(columns(qkv.ref, 0), columns(qkv.ref, third), columns(qkv.ref, 2 * third), segq.get(), segk.get(),
           context.ref, lse.ref, True, heads, factor)
    context.start()
    lse.start()
    part.put(dot_rows(context.ref[...], w_ref[:, 3 * third :]).astype(LOW))
    hand_on(w, whole)


def cross_forward(heads, factor, where, memory, w, before, mine, theirs, far, far_other, gain, segq, segk,
                  after, second, cq, ckv, context, lse, part, total_ref):
    third = heads * HD
    memory_ref, w_ref = memory.get(), w.get()
    ckv.put(dot(memory_ref[...], w_ref[:, third : 3 * third]).astype(LOW))
    value = wide(before) + branch(where[0], (mine, theirs, far, far_other), total_ref)
    after.put(value.astype(LOW))
    value = after.ref[...].astype(WIDE)
    second.put((value * rstd_of(value) * gain.get()[...]).astype(LOW))
    cq.put(dot(second.ref[...], w_ref[:, :third]).astype(LOW))
    attend(columns(cq.ref, 0), columns(ckv.ref, 0), columns(ckv.ref, third), segq.get(), segk.get(),
           context.ref, lse.ref, False, heads, factor)
    context.start()
    lse.start()
    part.put(dot_rows(context.ref[...], w_ref[:, 3 * third :]).astype(LOW))


def ffn_forward(hidden, where, before, mine, theirs, far, far_other, gain, w, after, third, slope, active, part, total_ref):
    value = branch(where[0], (mine, theirs, far, far_other), total_ref) + wide(before)
    after.put(value.astype(LOW))
    value = after.ref[...].astype(WIDE)
    third.put((value * rstd_of(value) * gain.get()[...]).astype(LOW))
    w_ref = w.get()
    act, rate = gelu_parts(dot(third.ref[...], w_ref[:, :hidden]))
    active.put(act.astype(LOW))
    slope.put(rate.astype(LOW))
    part.put(dot_rows(active.ref[...], w_ref[:, hidden : 2 * hidden]).astype(LOW))


def adapt_backward(where, before, mine, theirs, far, far_other, gain, down, up, goal, weight, w_out, slope, w_in,
                   low, inner, part, outputs, down_grad, up_grad, gain_grad, total_ref):
    value = branch(where[0], (mine, theirs, far, far_other), total_ref) + wide(before)
    rstd = rstd_of(value)
    normed = value * rstd
    gain_ref, down_ref, up_ref = gain.get(), down.get(), up.get()
    adapt_in = (normed * gain_ref[...]).astype(LOW)
    act, rate = gelu_parts(dot(adapt_in, down_ref[...]))
    act = act.astype(LOW)
    outputs.put(value + dot(act, up_ref[...]))
    grad_out = wide(goal) * weight.get()[...]
    out_low = grad_out.astype(LOW)
    grad_bottle = (dot_rows(out_low, up_ref[...]) * rate).astype(LOW)
    grad_in = dot_rows(grad_bottle, down_ref[...])
    gain_grad.put(jnp.sum(grad_in * normed, axis=0, keepdims=True))
    scaled = grad_in * gain_ref[...]
    total = grad_out + rstd * (scaled - normed * jnp.mean(scaled * normed, axis=-1, keepdims=True))
    low.put(total.astype(LOW))
    inner.put((dot(low.ref[...], w_out.get()[...]) * wide(slope)).astype(LOW))
    part.put(dot_rows(inner.ref[...], w_in.get()[...]).astype(LOW))
    up_grad.put(dot_inner(act, out_low).astype(LOW))
    down_grad.put(dot_inner(adapt_in, grad_bottle).astype(LOW))


def norm_back(moved, value, gain, gain_grad):
    rstd = rstd_of(value)
    normed = value * rstd
    gain_grad.put(jnp.sum(moved * normed, axis=0, keepdims=True))
    scaled = moved * gain
    return rstd * (scaled - normed * jnp.mean(scaled * normed, axis=-1, keepdims=True))


def cross_backward(heads, factor, where, mine, theirs, far, far_other, value, before, gain, w, cq, ckv, lse, segq, segk,
                   low, gain_grad, gq, gkv, part, memory, total_ref, g_ref, gk_ref, gv_ref):
    third = heads * HD
    moved = branch(where[0], (mine, theirs, far, far_other), total_ref)
    low.put((norm_back(moved, wide(value), gain.get()[...], gain_grad) + wide(before)).astype(LOW))
    w_ref = w.get()
    g_ref[...] = dot(low.ref[...], w_ref[:, 3 * third :]).astype(LOW)
    attend_back(columns(cq.get(), 0), columns(ckv.get(), 0), columns(ckv.get(), third), columns(g_ref, 0), segq.get(), segk.get(),
                lse.get(), gq.ref, gk_ref, gv_ref, False, heads, factor)
    gq.start()
    part.put(dot_rows(gq.ref[...], w_ref[:, :third]).astype(LOW))
    gkv.ref[:, :third] = gk_ref[...].astype(LOW)
    gkv.ref[:, third:] = gv_ref[...].astype(LOW)
    gkv.start()
    memory.put(dot_rows(gkv.ref[...], w_ref[:, third : 3 * third]).astype(LOW))


def self_backward(heads, factor, where, mine, theirs, far, far_other, value, before, gain, w, qkv, lse, segq, segk,
                  low, gain_grad, gqkv, part, total_ref, g_ref, gk_ref, gv_ref):
    third = heads * HD
    moved = branch(where[0], (mine, theirs, far, far_other), total_ref)
    low.put((norm_back(moved, wide(value), gain.get()[...], gain_grad) + wide(before)).astype(LOW))
    w_ref = w.get()
    g_ref[...] = dot(low.ref[...], w_ref[:, 3 * third :]).astype(LOW)
    qkv_ref = qkv.get()
    attend_back(columns(qkv_ref, 0), columns(qkv_ref, third), columns(qkv_ref, 2 * third), columns(g_ref, 0),
                segq.get(), segk.get(), lse.get(), gqkv.ref, gk_ref, gv_ref, True, heads, factor)
    gqkv.ref[:, third : 2 * third] = gk_ref[...].astype(LOW)
    gqkv.ref[:, 2 * third :] = gv_ref[...].astype(LOW)
    gqkv.start()
    part.put(dot_rows(gqkv.ref[...], w_ref[:, : 3 * third]).astype(LOW))


def input_backward(where, mine, theirs, far, far_other, own, before, gain, grad, gain_grad, total_ref):
    moved = branch(where[0], (mine, theirs, far, far_other), total_ref)
    grad.put(norm_back(moved, wide(own), gain.get()[...], gain_grad) + wide(before))


def pair_dot(left0, left1, right0, right1):
    return (dot_inner(left0.get()[...], right0.get()[...]) + dot_inner(left1.get()[...], right1.get()[...])).astype(LOW)


def weights_grad(widths, where, *refs):
    *boxes, out = refs
    at = 0
    for index, size in enumerate(widths):
        out.ref[:, at : at + size] = pair_dot(*boxes[4 * index : 4 * index + 4])
        at += size
    for box in boxes[4 * len(widths) :]:
        out.ref[:, at : at + box.ref.shape[1]] = box.get()[...]
    out.start()


def emit(widths, scale, where, keep, moved, *outs):
    keep_ref, moved_ref = keep.get(), moved.get()

    def put_in(first, second):
        at = 0
        for size, out in zip(widths, outs, strict=True):
            out.ref[:, :size] = first[:, at : at + size].astype(WIDE) * scale
            out.ref[:, size:] = second[:, at : at + size].astype(WIDE) * scale
            at += size

    @pl.when(where[0] == 0)
    def _():
        put_in(keep_ref, moved_ref)

    @pl.when(where[0] != 0)
    def _():
        put_in(moved_ref, keep_ref)

    for out in outs:
        out.start()


def hand_on(weight, outs):
    for out in outs:
        out.put(weight.ref[...])


def pack_rows(where, *refs):
    *weights, keep, send = refs
    for weight in weights:
        weight.wait()

    def put_in(core):
        at = 0
        for weight in weights:
            size = weight.ref.shape[1] // 2
            send.ref[:, at : at + size] = weight.ref[:, (1 - core) * size : (2 - core) * size]
            keep.ref[:, at : at + size] = weight.ref[:, core * size : (core + 1) * size]
            at += size

    @pl.when(where[0] == 0)
    def _():
        put_in(0)

    @pl.when(where[0] != 0)
    def _():
        put_in(1)

    send.start()
    keep.start()


def swap_core(value):
    return lax.ppermute(value, CORE, ACROSS)


def swap_pair(value):
    return lax.ppermute(value, PAIR, ACROSS)


def solution(mesh):
    dp, mp = mesh.devices.shape
    chips = dp // 2
    grid = Mesh(mesh.devices.reshape(chips, 2, mp), (CHIP, CORE, PAIR))
    ring = chips == 8

    def local(
        inputs, encoded, cotangent, segments, padding, task_ids, token_weights, gain_self, gain_cross, gain_ffn,
        self_query, self_key, self_value, self_out, cross_query, cross_key, cross_value, cross_out, ffn_in, ffn_out,
        gen_down, gen_up, gen_gain, task_table, proj_first, proj_second,
    ):
        rows, length, width = inputs.shape
        half = length // 2
        core = lax.axis_index(CORE)
        chip = lax.axis_index(CHIP)
        z, y = chip // 2, chip % 2
        where = jnp.stack([core, z, y]).astype(jnp.int32)
        first = core == 0
        factor = HD ** (-0.5)
        tasks_all = task_table.shape[0]
        local_rows = self_query.shape[0]
        chip_rows = 2 * local_rows
        quarter = self_query.shape[1] // 2
        heads = quarter // HD
        hidden = ffn_in.shape[1] // 2
        tasks_wide = tasks_all * ADAPT
        both = range(2)

        def order(mine, other, axis=0):
            return jnp.where(
                first, jnp.concatenate([mine, other], axis), jnp.concatenate([other, mine], axis)
            )

        def part_of(value, index, size, axis=0):
            return lax.dynamic_slice_in_dim(value, index * size, size, axis)

        turn = [(k, (k + 2) % chips) for k in range(chips)]
        side = [(k, k ^ 1) for k in range(chips)]

        def gather(weights, soon):
            total = sum(w.shape[1] // 2 for w in weights)
            if ring:
                keep, send = call(pack_rows, [shape((local_rows, total), LOW)] * 2, where, *weights)
            else:
                keep = jnp.concatenate([part_of(w, core, w.shape[1] // 2, 1) for w in weights], 1)
                send = jnp.concatenate([part_of(w, 1 - core, w.shape[1] // 2, 1) for w in weights], 1)
            moved = swap_core(send)
            if not (ring and soon):
                return lax.all_gather(order(keep, moved), CHIP, axis=0, tiled=True)
            held = [jnp.concatenate([keep, moved], 0)]
            for _ in range(3):
                held.append(lax.ppermute(held[-1], CHIP, turn))
            return Pieces(held, [lax.ppermute(h, CHIP, side) for h in held])

        def behind(value, gate):
            return value if gate is None else lax.optimization_barrier((value, gate))[0]

        def scatter(full, widths, soon, gates=(None,) * 4):
            total = sum(widths)
            if ring and soon:
                blocks = full.reshape(4, 2, chip_rows, total)
                moved = lax.ppermute(lax.dynamic_index_in_dim(blocks, 1 - y, 1, keepdims=False), CHIP, side)
                mine = lax.dynamic_index_in_dim(blocks, y, 1, keepdims=False)
                moved = behind(moved, gates[0])

                def block(step):
                    at = (z - step) % 4
                    return sum(lax.dynamic_index_in_dim(v, at, 0, keepdims=False).astype(WIDE) for v in (mine, moved))

                held = block(1)
                for step in (2, 3, 4):
                    held = behind(lax.ppermute(held.astype(LOW), CHIP, turn), gates[step - 1]).astype(WIDE) + block(step)
            else:
                held = lax.psum_scatter(full, CHIP, scatter_dimension=0, tiled=True)
            send = swap_core(part_of(held, 1 - core, local_rows).astype(LOW))
            scale = 1.0 / math.sqrt(rows * dp * length)
            return call(
                functools.partial(emit, widths, scale), [shape((local_rows, 2 * w), WIDE) for w in widths],
                where, part_of(held, core, local_rows), send,
            )

        def all_sum(value):
            bit = 1
            while bit < chips:
                value = value + lax.ppermute(value, CHIP, [(k, k ^ bit) for k in range(chips)])
                bit *= 2
            return value

        def project(table, one, two):
            return exact(jax.nn.gelu(exact(table, one)), two)

        w_self = gather([self_query, self_key, self_value, self_out], True)

        ident_all, project_pull = jax.vjp(project, task_table, proj_first, proj_second)
        ident_low_all = ident_all.astype(LOW)
        gain_all = 1.0 + exact(ident_all, gen_gain)

        def spread(generator):
            made = dot(ident_low_all, generator).astype(LOW)
            made = made.reshape(tasks_all, local_rows, ADAPT).transpose(1, 0, 2)
            return made.reshape(local_rows, tasks_wide)

        w_rest = gather(
            [cross_query, cross_key, cross_value, cross_out, ffn_in, ffn_out,
             jnp.concatenate([spread(gen_down), spread(gen_up)], 1)],
            False,
        )
        w_cross = Cols(w_rest, 0, 4 * quarter)
        w_ffn = Cols(w_rest, 4 * quarter, 4 * quarter + 2 * hidden)
        generated = w_rest[:, 4 * quarter + 2 * hidden :]

        words = jnp.concatenate([segments, padding, jnp.broadcast_to(task_ids[:, None], (1, length))], 0)
        words_other = swap_core(words)
        words = [jnp.where(first, words, words_other), jnp.where(first, words_other, words)]
        own, memory, goal = (v.reshape(length, width) for v in (inputs, encoded, cotangent))
        own_other, memory_other, goal_other = swap_core(own), swap_core(memory), swap_core(goal)
        streams = [Pick(r, own, own_other) for r in both]
        memories = [Pick(r, memory, memory_other) for r in both]
        goals = [Pick(r, goal, goal_other) for r in both]
        weights = token_weights.astype(WIDE)
        onehots = [(w[2, 0] == jnp.arange(tasks_all)).astype(WIDE) for w in words]
        segqs = [w[:1] for w in words]
        segks = [jnp.where(w[1] == 1, w[0], -1)[:, None] for w in words]
        row_weights = [jnp.sum(o * weights) * (tasks_all / jnp.sum(weights)) for o in onehots]
        token_scales = [row_weights[r] * words[r][1].astype(WIDE)[:, None] for r in both]
        gains_task = [exact(o[None], gain_all) for o in onehots]
        g_self, g_cross, g_ffn = (g[None] for g in (gain_self, gain_cross, gain_ffn))

        line = shape((1, width), WIDE)
        lse = shape((heads, length), WIDE)
        total_scratch = pltpu.VMEM((length, width), WIDE)
        unit = 2 * length * width

        def low(columns_wide):
            return shape((length, columns_wide), LOW)

        full_low = low(width)
        kept = [dict() for _ in both]
        chain, last, found = [], [], []

        def share(part):
            if last:
                part, _ = lax.optimization_barrier((part, last[0]))
            other = swap_core(part)
            here = (part_of(part, core, half).astype(WIDE) + part_of(other, core, half).astype(WIDE)).astype(LOW)
            far = swap_pair(here)
            chain[:], last[:] = [here], [far]
            return part, other, far, swap_core(far)

        def stage(body, outs, *args, extra=(), **options):
            return call(body, outs, where, *args, after=(*chain, *extra), **options)

        def forward_self(r):
            k = kept[r]
            whole = [shape(w_self.shape, LOW)] if ring and r == 0 else []
            k["first"], k["qkv"], k["context"], k["lse"], part, *more = stage(
                functools.partial(self_forward, heads, factor),
                [full_low, low(3 * quarter), low(quarter), lse, full_low, *whole],
                streams[r], g_self, *(found or [w_self]), segqs[r], segks[r], flops=5 * unit * quarter,
            )
            found[:] = more or found
            k["y"] = share(part)

        def forward_cross(r):
            k = kept[r]
            k["after_self"], k["second"], k["cq"], k["ckv"], k["c_context"], k["c_lse"], part = stage(
                functools.partial(cross_forward, heads, factor),
                [full_low, full_low, low(quarter), low(2 * quarter), low(quarter), lse, full_low],
                memories[r], w_cross, streams[r], *k["y"], g_cross, segqs[r], segks[r],
                flops=5 * unit * quarter, scratch=[total_scratch],
            )
            k["y"] = share(part)

        def forward_ffn(r):
            k = kept[r]
            k["after_cross"], k["third"], k["slope"], k["active"], part = stage(
                functools.partial(ffn_forward, hidden), [full_low, full_low, low(hidden), low(hidden), full_low],
                k["after_self"], *k["y"], g_ffn, w_ffn,
                flops=2 * unit * hidden, scratch=[total_scratch],
            )
            k["y"] = share(part)

        def into(r, name):
            return (kept[0][name],) if r else None

        def backward_ffn(r):
            k = kept[r]
            down = downs[:, r * ADAPT : (r + 1) * ADAPT]
            up = ups[:, r * ADAPT : (r + 1) * ADAPT].reshape(ADAPT, width)
            k["ffn_low"], k["grad_inner"], part, k["outputs"], k["grad_down"], k["grad_up"], k["grad_gain"] = stage(
                adapt_backward,
                [full_low, low(hidden), full_low, Owned(r, shape((length, width), WIDE), into(r, "outputs")),
                 shape((width, ADAPT), LOW), shape((ADAPT, width), LOW), line],
                k["after_cross"], *k["y"], gains_task[r], down, up, goals[r], token_scales[r],
                Cols(w_rest, w_ffn.start + hidden, w_ffn.stop), k["slope"], Cols(w_rest, w_ffn.start, w_ffn.start + hidden),
                flops=2 * unit * hidden + 5 * unit * 128, scratch=[total_scratch],
            )
            k["y"] = share(part)

        grads_scratch = [total_scratch, pltpu.VMEM((length, quarter), LOW)] + [pltpu.VMEM((length, quarter), WIDE)] * 2

        def backward_cross(r):
            k = kept[r]
            k["cross_low"], k["g3"], k["gcq"], k["gckv"], part, *k["memory"] = stage(
                functools.partial(cross_backward, heads, factor),
                [full_low, line, low(quarter), low(2 * quarter), full_low, Routed(r, full_low, kept[0]["memory"] if r else None)],
                *k["y"], k["after_cross"], k["ffn_low"], g_ffn, w_cross, k["cq"], k["ckv"], k["c_lse"], segqs[r], segks[r],
                flops=7 * unit * quarter, scratch=grads_scratch,
            )
            k["y"] = share(part)

        def backward_self(r):
            k = kept[r]
            k["self_low"], k["g2"], k["gqkv"], part = stage(
                functools.partial(self_backward, heads, factor), [full_low, line, low(3 * quarter), full_low],
                *k["y"], k["after_self"], k["cross_low"], g_cross, w_self, k["qkv"], k["lse"], segqs[r], segks[r],
                flops=7 * unit * quarter, scratch=grads_scratch,
            )
            k["y"] = share(part)
            k["far"] = k["y"][2]

        def backward_input(r):
            k = kept[r]
            k["grad_x"], k["g1"] = call(
                input_backward, [Owned(r, shape((length, width), WIDE), into(r, "grad_x")), line],
                where, *k["y"], streams[r], k["self_low"], g_self, after=(sum_self,), scratch=[total_scratch],
            )

        def pairs(*names):
            return [kept[r][name] for name in names for r in both]

        for step in (forward_self, forward_cross, forward_ffn):
            for r in both:
                step(r)
        w_self = (found or [w_self])[0]

        slots = lax.broadcasted_iota(jnp.int32, (tasks_wide, 2 * ADAPT), 0)
        places = lax.broadcasted_iota(jnp.int32, (tasks_wide, 2 * ADAPT), 1)
        wanted = jnp.where(places < ADAPT, words[0][2, 0], words[1][2, 0]) * ADAPT + places % ADAPT
        select = (slots == wanted).astype(LOW)
        picked = dot(generated, select).astype(LOW)
        picked_other = swap_core(picked)
        downs = jnp.where(first, picked, picked_other)
        ups = jnp.where(first, picked_other, picked)

        for r in both:
            backward_ffn(r)
        tasks_here = dot_rows(
            jnp.concatenate([jnp.where(first, kept[r]["grad_down"], kept[r]["grad_up"].reshape(width, ADAPT)) for r in both], 1),
            select,
        ).astype(LOW)
        grad_in, grad_outer, found = scatter(
            call(
                functools.partial(weights_grad, [hidden, hidden]), [shape((width, 2 * hidden + tasks_wide), LOW)], where,
                *pairs("third", "grad_inner", "ffn_low", "active"), tasks_here, after=tuple(chain), flops=4 * unit * hidden,
            )[0],
            [hidden, hidden, tasks_wide], False,
        )
        for r in both:
            backward_cross(r)
        sum_cross = (
            call(
                functools.partial(weights_grad, [quarter, 2 * quarter, quarter]), [shape((width, 4 * quarter), LOW)], where,
                *pairs("second", "gcq"), *memories, *pairs("gckv", "cross_low", "c_context"), after=tuple(chain),
                flops=8 * unit * quarter,
            )[0]
        )
        chain.append(sum_cross)
        for r in both:
            backward_self(r)
        sum_self = (
            call(
                functools.partial(weights_grad, [3 * quarter, quarter]), [shape((width, 4 * quarter), LOW)], where,
                *pairs("first", "gqkv", "self_low", "context"), after=tuple(chain), flops=8 * unit * quarter,
            )[0]
        )
        for r in both:
            backward_input(r)
        grads_cross = scatter(
            sum_cross, [quarter] * 4, True, (kept[0]["self_low"], kept[1]["self_low"], sum_self, kept[0]["g1"])
        )
        grads_self = scatter(sum_self, [quarter] * 4, True)
        scale = 1.0 / math.sqrt(rows * dp * length)

        keep, send = kept[1]["memory"]
        memory_part = (keep.astype(WIDE) + swap_core(send).astype(WIDE)).astype(LOW)
        memory_part = behind(memory_part, kept[0]["far"])
        grad_memory = memory_part.astype(WIDE) + swap_pair(memory_part).astype(WIDE)

        def narrow(value):
            value = value.reshape(local_rows, tasks_all, ADAPT).transpose(1, 0, 2)
            return value.reshape(tasks_all, local_rows * ADAPT).astype(LOW)

        found_down, found_up = narrow(found[:, :tasks_wide]), narrow(found[:, tasks_wide:])
        grad_gen_down = dot_inner(ident_low_all, found_down)
        grad_gen_up = dot_inner(ident_low_all, found_up)
        ident_part = dot_rows(found_down, gen_down) + dot_rows(found_up, gen_up)
        ident_part = ident_part + swap_core(ident_part)
        gain_part = sum(onehots[r][:, None] * kept[r]["grad_gain"] for r in both) * scale
        early = all_sum(jnp.concatenate([gain_part, jnp.pad(ident_part, ((0, 0), (0, width - ident_part.shape[1])))], 0))
        gain_sum, ident_sum = early[:tasks_all], early[tasks_all:, : ident_part.shape[1]]
        norms = [sum(kept[r][name] for r in both) for name in ("g1", "g2", "g3")]
        norm_sums = all_sum(jnp.concatenate(norms, 0)) * scale
        grad_gen_gain = exact(ident_all, gain_sum, ((0,), (0,)))
        grad_ident = ident_sum + exact(gain_sum, gen_gain, ((1,), (1,)))
        grad_table, grad_first_m, grad_second_m = project_pull(grad_ident)

        def shaped(value):
            return value.reshape(rows, length, width)

        return (
            shaped(kept[1]["outputs"]), shaped(kept[1]["grad_x"]), shaped(grad_memory), norm_sums[0], norm_sums[1], norm_sums[2],
            *grads_self, *grads_cross, grad_in, grad_outer, grad_gen_down, grad_gen_up,
            grad_gen_gain, grad_table, grad_first_m, grad_second_m,
        )

    data = (CHIP, CORE)
    three, matrix = P(data, None, None), P(data, PAIR)
    in_specs = (
        three, three, three, P(data, None), P(data, None), P(data), P(), P(), P(), P(),
        *(matrix,) * 10, P(None, data), P(None, data), P(), P(), P(), P(),
    )
    out_specs = (
        three, three, three, P(), P(), P(), *(matrix,) * 10, P(None, data), P(None, data), P(), P(), P(), P(),
    )
    return jax.shard_map(local, mesh=grid, in_specs=in_specs, out_specs=out_specs, check_vma=False)
```

```python
import functools
import math

import jax
import jax.numpy as jnp
from jax import lax
from jax.experimental import pallas as pl
from jax.experimental.pallas import tpu as pltpu
from jax.sharding import Mesh
from jax.sharding import PartitionSpec as P

HD = 64
ADAPT = 24
HIGHEST = lax.Precision.HIGHEST
EPSILON = 1e-06
MASKED = -1000000000.0
LOW = jnp.bfloat16
WIDE = jnp.float32
CHIP, CORE, PAIR = "chip", "core", "mp"
ACROSS = [(0, 1), (1, 0)]
SPAN = 128
ROOT = math.sqrt(2.0 / math.pi)


def dot(left, right):
    return lax.dot_general(left, right, (((1,), (0,)), ((), ())), preferred_element_type=WIDE)


def dot_rows(left, right):
    return lax.dot_general(left, right, (((1,), (1,)), ((), ())), preferred_element_type=WIDE)


def dot_inner(left, right):
    return lax.dot_general(left, right, (((0,), (0,)), ((), ())), preferred_element_type=WIDE)


def exact(left, right, dims=((1,), (0,))):
    return lax.dot_general(left, right, (dims, ((), ())), precision=HIGHEST, preferred_element_type=WIDE)


def rstd_of(value):
    return lax.rsqrt(jnp.mean(value * value, axis=-1, keepdims=True) + EPSILON)


def gelu_parts(value):
    square = value * value
    slope = jnp.tanh(ROOT * (value + 0.044715 * square * value))
    half = 0.5 * (1.0 + slope)
    return value * half, half + 0.5 * value * (1.0 - slope * slope) * ROOT * (1.0 + 0.134145 * square)


def shape(dims, dtype):
    return jax.ShapeDtypeStruct(dims, dtype)


class Cols:
    def __init__(self, array, start, stop):
        self.array, self.start, self.stop = array, start, stop


class Pick:
    def __init__(self, row, own, other):
        self.row, self.own, self.other = row, own, other


class Pieces:
    def __init__(self, held, other):
        self.blocks = [*held, *other]
        self.size = held[0].shape[0]
        self.shape = (len(self.blocks) * self.size, held[0].shape[1])
        self.dtype = held[0].dtype

    def places(self, where):
        part = self.size // 2
        for index in range(len(self.blocks)):
            z = lax.rem(where[1] + 4 - index % 4, 4)
            y = where[2] if index < 4 else 1 - where[2]
            for side in range(2):
                turn = where[0] if side == 0 else 1 - where[0]
                at = pl.multiple_of((2 * z + y) * self.size + turn * part, 16)
                yield index, slice(side * part, (side + 1) * part), pl.ds(at, part)


class Owned:
    def __init__(self, row, aval, into):
        self.row, self.aval, self.into = row, aval, into


class Routed:
    def __init__(self, row, aval, into):
        self.row, self.aval, self.into = row, aval, into


class Box:
    def __init__(self, ref, copies):
        self.ref, self.copies, self.pending = ref, copies, False

    def each(self, act):
        for condition, copy in self.copies:
            if condition is None:
                act(copy)
            else:
                pl.when(condition)(functools.partial(act, copy))

    def start(self):
        self.each(lambda copy: copy.start())
        self.pending = True

    def wait(self):
        if self.pending:
            self.each(lambda copy: copy.wait())
            self.pending = False

    def get(self):
        self.wait()
        return self.ref

    def put(self, value):
        self.ref[...] = value
        self.start()


VMEM_LIMIT = 60 * 1024 * 1024


def call(body, outs, where, *args, after=(), flops=0, scratch=()):
    inputs, buffers, loads = [], [], []
    for arg in args:
        if isinstance(arg, Pick):
            loads.append((arg, len(inputs)))
            inputs += [arg.own, arg.other]
            buffers.append((arg.own.shape, arg.own.dtype))
        elif isinstance(arg, Cols):
            loads.append((arg, len(inputs)))
            inputs.append(arg.array)
            buffers.append(((arg.array.shape[0], arg.stop - arg.start), arg.array.dtype))
        elif isinstance(arg, Pieces):
            loads.append((arg, len(inputs)))
            inputs += arg.blocks
            buffers.append((arg.shape, arg.dtype))
        else:
            loads.append((arg, len(inputs)))
            inputs.append(arg)
            buffers.append((arg.shape, arg.dtype))
    avals, stores, aliases = [], [], {}
    for out in outs:
        special = isinstance(out, (Owned, Routed))
        aval = out.aval if special else out
        stores.append((out, len(avals)))
        buffers.append((aval.shape, aval.dtype))
        if special and out.into is not None:
            for array in out.into:
                aliases[1 + len(inputs)] = len(avals)
                inputs.append(array)
                avals.append(aval)
        else:
            avals += [aval] * (2 if isinstance(out, Routed) else 1)
    many = sum(2 * len(a.blocks) for a in args if isinstance(a, Pieces))
    moved = sum(math.prod(dims) * jnp.dtype(dtype).itemsize for dims, dtype in buffers)
    inputs += after

    def kernel(where_ref, *refs):
        in_refs, refs = refs[: len(inputs)], refs[len(inputs) :]
        out_refs, refs = refs[: len(avals)], refs[len(avals) :]
        own, refs = refs[: len(scratch)], refs[len(scratch) :]
        held, sems = refs[:-1], refs[-1]
        boxes, extra = [], len(buffers)
        for n, (arg, at) in enumerate(loads):
            if isinstance(arg, Pieces):
                copies = []
                for index, rows, place in arg.places(where_ref):
                    source, target = in_refs[at + index].at[rows, :], held[n].at[place, :]
                    copies.append((None, pltpu.make_async_copy(source, target, sems.at[extra])))
                    extra += 1
                boxes.append(Box(held[n], copies))
                boxes[-1].start()
                continue
            if isinstance(arg, Pick):
                mine = where_ref[0] == arg.row
                pairs = [(mine, in_refs[at]), (jnp.logical_not(mine), in_refs[at + 1])]
            elif isinstance(arg, Cols):
                pairs = [(None, in_refs[at].at[:, arg.start : arg.stop])]
            else:
                pairs = [(None, in_refs[at])]
            boxes.append(Box(held[n], [(c, pltpu.make_async_copy(s, held[n], sems.at[n])) for c, s in pairs]))
            boxes[-1].start()
        for n, (out, at) in enumerate(stores, len(loads)):
            pairs = [(None, out_refs[at])]
            if isinstance(out, (Owned, Routed)):
                mine = where_ref[0] == out.row
                pairs = [(mine, out_refs[at])]
                if isinstance(out, Routed):
                    pairs.append((jnp.logical_not(mine), out_refs[at + 1]))
            boxes.append(Box(held[n], [(c, pltpu.make_async_copy(held[n], d, sems.at[n])) for c, d in pairs]))
        body(where_ref, *boxes, *own)
        for box in boxes:
            box.wait()

    hbm = pl.BlockSpec(memory_space=pltpu.HBM)
    return pl.pallas_call(
        kernel,
        out_shape=tuple(avals),
        in_specs=[pl.BlockSpec(memory_space=pltpu.SMEM)] + [hbm] * len(inputs),
        out_specs=tuple(hbm for _ in avals),
        scratch_shapes=[*scratch, *(pltpu.VMEM(*b) for b in buffers), pltpu.SemaphoreType.DMA((len(buffers) + many,))],
        input_output_aliases=aliases,
        compiler_params=pltpu.CompilerParams(vmem_limit_bytes=VMEM_LIMIT),
        cost_estimate=pl.CostEstimate(flops=flops, bytes_accessed=moved, transcendentals=0),
    )(where, *inputs)


def at_half(core, half):
    return pl.ds(pl.multiple_of(core * half, half), half)


def windows(length, causal):
    for lo in range(0, length, SPAN):
        yield lo, max(lo - SPAN, 0), lo + SPAN if causal else min(lo + 2 * SPAN, length)


def mask_of(segq_ref, segk_ref, lo, start, stop, causal):
    dims = (stop - start, SPAN)
    keys = start + lax.broadcasted_iota(jnp.int32, dims, 0)
    queries = lo + lax.broadcasted_iota(jnp.int32, dims, 1)
    same = segk_ref[start:stop, :] == segq_ref[:, lo : lo + SPAN]
    if causal:
        same = same & (keys <= queries)
    return same | (keys == queries)


def beside(parts):
    return jnp.concatenate(parts, axis=1)


def lanes(value, count):
    return [value[:, i * SPAN : (i + 1) * SPAN] for i in range(count)]


def attend(q_at, k_at, v_at, segq_ref, segk_ref, context_ref, lse_ref, causal, heads, factor):
    for lo, start, stop in windows(context_ref.shape[0], causal):
        mask = beside([mask_of(segq_ref, segk_ref, lo, start, stop, causal)] * heads)
        scores = beside([dot_rows(k_at(h, start, stop), q_at(h, lo, lo + SPAN) * LOW(factor)) for h in range(heads)])
        scores = jnp.where(mask, scores, MASKED)
        top = jnp.max(scores, axis=0, keepdims=True)
        expos = jnp.exp(scores - top)
        total = jnp.sum(expos, axis=0, keepdims=True)
        probs = (expos * (1.0 / total)).astype(LOW)
        logs = lanes(top + jnp.log(total), heads)
        for h, part in enumerate(lanes(probs, heads)):
            context_ref[lo : lo + SPAN, h * HD : (h + 1) * HD] = dot_inner(part, v_at(h, start, stop)).astype(LOW)
            lse_ref[h : h + 1, lo : lo + SPAN] = logs[h]


def attend_back(q_at, k_at, v_at, g_at, segq_ref, segk_ref, lse_ref, gq_ref, gk_ref, gv_ref, causal, heads, factor):
    gk_ref[...] = jnp.zeros_like(gk_ref)
    gv_ref[...] = jnp.zeros_like(gv_ref)
    for lo, start, stop in windows(lse_ref.shape[1], causal):
        mask = beside([mask_of(segq_ref, segk_ref, lo, start, stop, causal)] * heads)
        queries = [q_at(h, lo, lo + SPAN) * LOW(factor) for h in range(heads)]
        keys = [k_at(h, start, stop) for h in range(heads)]
        grads = [g_at(h, lo, lo + SPAN) for h in range(heads)]
        scores = beside([dot_rows(keys[h], queries[h]) for h in range(heads)])
        logs = beside([lse_ref[h : h + 1, lo : lo + SPAN] for h in range(heads)])
        probs = jnp.exp(jnp.where(mask, scores, MASKED) - logs)
        grad_probs = beside([dot_rows(v_at(h, start, stop), grads[h]) for h in range(heads)])
        centre = jnp.sum(probs * grad_probs, axis=0, keepdims=True)
        grad_scores = lanes((probs * (grad_probs - centre)).astype(LOW), heads)
        for h, part in enumerate(lanes(probs.astype(LOW), heads)):
            cols = slice(h * HD, (h + 1) * HD)
            gv_ref[start:stop, cols] += dot(part, grads[h])
            gk_ref[start:stop, cols] += dot(grad_scores[h], queries[h])
            gq_ref[lo : lo + SPAN, cols] = (dot_inner(grad_scores[h], keys[h]) * factor).astype(LOW)


def columns(ref, at):
    return lambda h, lo, hi: ref[lo:hi, at + h * HD : at + (h + 1) * HD]


def branch(core, pack, total_ref):
    mine, other, far, far_other = pack
    total_ref[...] = (mine.get()[...].astype(WIDE) + other.get()[...].astype(WIDE)).astype(LOW).astype(WIDE)
    half = far.ref.shape[0]
    total_ref[at_half(core, half), :] += far.get()[...].astype(WIDE)
    total_ref[at_half(1 - core, half), :] += far_other.get()[...].astype(WIDE)
    return total_ref[...]


def wide(box):
    return box.get()[...].astype(WIDE)


def self_forward(heads, factor, where, own, gain, w, segq, segk, first, qkv, context, lse, part, *whole):
    third = heads * HD
    value = wide(own)
    first.put((value * rstd_of(value) * gain.get()[...]).astype(LOW))
    w_ref = w.get()
    qkv.put(dot(first.ref[...], w_ref[:, : 3 * third]).astype(LOW))
    attend(columns(qkv.ref, 0), columns(qkv.ref, third), columns(qkv.ref, 2 * third), segq.get(), segk.get(),
           context.ref, lse.ref, True, heads, factor)
    context.start()
    lse.start()
    part.put(dot_rows(context.ref[...], w_ref[:, 3 * third : 4 * third]).astype(LOW))
    hand_on(w, whole)


def cross_forward(heads, factor, where, memory, w, before, mine, theirs, far, far_other, gain, segq, segk,
                  after, second, cq, ckv, context, lse, part, total_ref):
    third = heads * HD
    memory_ref, w_ref = memory.get(), w.get()
    ckv.put(dot(memory_ref[...], w_ref[:, third : 3 * third]).astype(LOW))
    value = wide(before) + branch(where[0], (mine, theirs, far, far_other), total_ref)
    after.put(value.astype(LOW))
    value = after.ref[...].astype(WIDE)
    second.put((value * rstd_of(value) * gain.get()[...]).astype(LOW))
    cq.put(dot(second.ref[...], w_ref[:, :third]).astype(LOW))
    attend(columns(cq.ref, 0), columns(ckv.ref, 0), columns(ckv.ref, third), segq.get(), segk.get(),
           context.ref, lse.ref, False, heads, factor)
    context.start()
    lse.start()
    part.put(dot_rows(context.ref[...], w_ref[:, 3 * third : 4 * third]).astype(LOW))


def ffn_forward(hidden, where, before, mine, theirs, far, far_other, gain, w, after, third, slope, active, part, total_ref):
    value = branch(where[0], (mine, theirs, far, far_other), total_ref) + wide(before)
    after.put(value.astype(LOW))
    value = after.ref[...].astype(WIDE)
    third.put((value * rstd_of(value) * gain.get()[...]).astype(LOW))
    w_ref = w.get()
    act, rate = gelu_parts(dot(third.ref[...], w_ref[:, :hidden]))
    active.put(act.astype(LOW))
    slope.put(rate.astype(LOW))
    part.put(dot_rows(active.ref[...], w_ref[:, hidden : 2 * hidden]).astype(LOW))


def adapt_backward(where, before, mine, theirs, far, far_other, gain, down, up, goal, weight, segk, w_out, slope, w_in,
                   low, inner, part, outputs, down_grad, up_grad, gain_grad, total_ref):
    value = branch(where[0], (mine, theirs, far, far_other), total_ref) + wide(before)
    rstd = rstd_of(value)
    normed = value * rstd
    gain_ref, down_ref, up_ref = gain.get(), down.get(), up.get()
    adapt_in = (normed * gain_ref[...]).astype(LOW)
    act, rate = gelu_parts(dot(adapt_in, down_ref[...]))
    act = act.astype(LOW)
    outputs.put(value + dot(act, up_ref[...]))
    grad_out = wide(goal) * jnp.where(segk.get()[...] >= 0, weight.get()[...], 0.0)
    out_low = grad_out.astype(LOW)
    grad_bottle = (dot_rows(out_low, up_ref[...]) * rate).astype(LOW)
    grad_in = dot_rows(grad_bottle, down_ref[...])
    gain_grad.put(jnp.sum(grad_in * normed, axis=0, keepdims=True))
    scaled = grad_in * gain_ref[...]
    total = grad_out + rstd * (scaled - normed * jnp.mean(scaled * normed, axis=-1, keepdims=True))
    low.put(total.astype(LOW))
    inner.put((dot(low.ref[...], w_out.get()[...]) * wide(slope)).astype(LOW))
    part.put(dot_rows(inner.ref[...], w_in.get()[...]).astype(LOW))
    up_grad.put(dot_inner(act, out_low).astype(LOW))
    down_grad.put(dot_inner(adapt_in, grad_bottle).astype(LOW))


def norm_back(moved, value, gain, gain_grad):
    rstd = rstd_of(value)
    normed = value * rstd
    gain_grad.put(jnp.sum(moved * normed, axis=0, keepdims=True))
    scaled = moved * gain
    return rstd * (scaled - normed * jnp.mean(scaled * normed, axis=-1, keepdims=True))


def cross_backward(heads, factor, where, mine, theirs, far, far_other, value, before, gain, w, cq, ckv, lse, segq, segk,
                   low, gain_grad, gq, gkv, part, memory, total_ref, g_ref, gk_ref, gv_ref):
    third = heads * HD
    moved = branch(where[0], (mine, theirs, far, far_other), total_ref)
    low.put((norm_back(moved, wide(value), gain.get()[...], gain_grad) + wide(before)).astype(LOW))
    w_ref = w.get()
    g_ref[...] = dot(low.ref[...], w_ref[:, 3 * third : 4 * third]).astype(LOW)
    attend_back(columns(cq.get(), 0), columns(ckv.get(), 0), columns(ckv.get(), third), columns(g_ref, 0), segq.get(), segk.get(),
                lse.get(), gq.ref, gk_ref, gv_ref, False, heads, factor)
    gq.start()
    part.put(dot_rows(gq.ref[...], w_ref[:, :third]).astype(LOW))
    gkv.ref[:, :third] = gk_ref[...].astype(LOW)
    gkv.ref[:, third:] = gv_ref[...].astype(LOW)
    gkv.start()
    memory.put(dot_rows(gkv.ref[...], w_ref[:, third : 3 * third]).astype(LOW))


def self_backward(heads, factor, where, mine, theirs, far, far_other, value, before, gain, w, qkv, lse, segq, segk,
                  low, gain_grad, gqkv, part, total_ref, g_ref, gk_ref, gv_ref):
    third = heads * HD
    moved = branch(where[0], (mine, theirs, far, far_other), total_ref)
    low.put((norm_back(moved, wide(value), gain.get()[...], gain_grad) + wide(before)).astype(LOW))
    w_ref = w.get()
    g_ref[...] = dot(low.ref[...], w_ref[:, 3 * third : 4 * third]).astype(LOW)
    qkv_ref = qkv.get()
    attend_back(columns(qkv_ref, 0), columns(qkv_ref, third), columns(qkv_ref, 2 * third), columns(g_ref, 0),
                segq.get(), segk.get(), lse.get(), gqkv.ref, gk_ref, gv_ref, True, heads, factor)
    gqkv.ref[:, third : 2 * third] = gk_ref[...].astype(LOW)
    gqkv.ref[:, 2 * third :] = gv_ref[...].astype(LOW)
    gqkv.start()
    part.put(dot_rows(gqkv.ref[...], w_ref[:, : 3 * third]).astype(LOW))


def input_backward(where, mine, theirs, far, far_other, own, before, gain, grad, gain_grad, total_ref):
    moved = branch(where[0], (mine, theirs, far, far_other), total_ref)
    grad.put(norm_back(moved, wide(own), gain.get()[...], gain_grad) + wide(before))


def pair_dot(left0, left1, right0, right1):
    return (dot_inner(left0.get()[...], right0.get()[...]) + dot_inner(left1.get()[...], right1.get()[...])).astype(LOW)


def weights_grad(widths, where, *refs):
    *boxes, out = refs
    at = 0
    for index, size in enumerate(widths):
        out.ref[:, at : at + size] = pair_dot(*boxes[4 * index : 4 * index + 4])
        at += size
    for box in boxes[4 * len(widths) :]:
        out.ref[:, at : at + box.ref.shape[1]] = box.get()[...]
    out.start()


def emit(widths, scale, where, *refs):
    count = len(refs) // (2 + len(widths))
    sums, outs = refs[: 2 * count], refs[2 * count :]
    for box in sums:
        box.wait()

    def put_in(index, first, second):
        at = 0
        for size, out in zip(widths, outs[index * len(widths) :], strict=False):
            out.ref[:, :size] = first[:, at : at + size].astype(WIDE) * scale
            out.ref[:, size:] = second[:, at : at + size].astype(WIDE) * scale
            at += size

    @pl.when(where[0] == 0)
    def _():
        for index in range(count):
            put_in(index, sums[2 * index].ref, sums[2 * index + 1].ref)

    @pl.when(where[0] != 0)
    def _():
        for index in range(count):
            put_in(index, sums[2 * index + 1].ref, sums[2 * index].ref)

    for out in outs:
        out.start()


def pick(where, generated, select, out):
    out.put(dot(generated.get()[...], select.get()[...]).astype(LOW))


def hand_on(weight, outs):
    for out in outs:
        out.put(weight.ref[...])


def pack_rows(where, *refs):
    *weights, keep, send = refs
    for weight in weights:
        weight.wait()

    def put_in(core):
        at = 0
        for weight in weights:
            size = weight.ref.shape[1] // 2
            send.ref[:, at : at + size] = weight.ref[:, (1 - core) * size : (2 - core) * size]
            keep.ref[:, at : at + size] = weight.ref[:, core * size : (core + 1) * size]
            at += size

    @pl.when(where[0] == 0)
    def _():
        put_in(0)

    @pl.when(where[0] != 0)
    def _():
        put_in(1)

    send.start()
    keep.start()


def swap_core(value):
    return lax.ppermute(value, CORE, ACROSS)


def swap_pair(value):
    return lax.ppermute(value, PAIR, ACROSS)


def solution(mesh):
    dp, mp = mesh.devices.shape
    chips = dp // 2
    grid = Mesh(mesh.devices.reshape(chips, 2, mp), (CHIP, CORE, PAIR))
    ring = chips == 8

    def local(
        inputs, encoded, cotangent, segments, padding, task_ids, token_weights, gain_self, gain_cross, gain_ffn,
        self_query, self_key, self_value, self_out, cross_query, cross_key, cross_value, cross_out, ffn_in, ffn_out,
        gen_down, gen_up, gen_gain, task_table, proj_first, proj_second,
    ):
        rows, length, width = inputs.shape
        half = length // 2
        core = lax.axis_index(CORE)
        chip = lax.axis_index(CHIP)
        z, y = chip // 2, chip % 2
        where = jnp.stack([core, z, y]).astype(jnp.int32)
        first = core == 0
        factor = HD ** (-0.5)
        tasks_all = task_table.shape[0]
        local_rows = self_query.shape[0]
        chip_rows = 2 * local_rows
        quarter = self_query.shape[1] // 2
        heads = quarter // HD
        hidden = ffn_in.shape[1] // 2
        tasks_wide = tasks_all * ADAPT
        both = range(2)

        def order(mine, other, axis=0):
            return jnp.where(
                first, jnp.concatenate([mine, other], axis), jnp.concatenate([other, mine], axis)
            )

        def part_of(value, index, size, axis=0):
            return lax.dynamic_slice_in_dim(value, index * size, size, axis)

        turns = [[(k, (k + 2 * step) % chips) for k in range(chips)] for step in (1, 2, 3)]
        side = [(k, k ^ 1) for k in range(chips)]

        def behind(value, gate):
            return value if gate is None else lax.optimization_barrier((value, gate))[0]

        def gather(weights, soon, after=()):
            total = sum(w.shape[1] // 2 for w in weights)
            if ring:
                keep, send = call(pack_rows, [shape((local_rows, total), LOW)] * 2, where, *weights, after=after)
            else:
                keep = jnp.concatenate([part_of(w, core, w.shape[1] // 2, 1) for w in weights], 1)
                send = jnp.concatenate([part_of(w, 1 - core, w.shape[1] // 2, 1) for w in weights], 1)
            moved = swap_core(send)
            if not (ring and soon):
                shard = order(keep, moved)
                return lax.all_gather(shard, CHIP, axis=0, tiled=True), shard
            shard = jnp.concatenate([keep, moved], 0)
            held = [shard]
            for _ in range(3):
                held.append(lax.ppermute(held[-1], CHIP, turns[0]))
            return Pieces(held, [lax.ppermute(h, CHIP, side) for h in held]), shard

        def sides(full):
            blocks = full.reshape(4, 2, chip_rows, full.shape[1])
            return [lax.dynamic_index_in_dim(blocks, at, 1, keepdims=False) for at in (1 - y, y)]

        def blocks_of(mine, moved):
            def block(step):
                at = (z + step) % 4
                return sum(lax.dynamic_index_in_dim(v, at, 0, keepdims=False).astype(WIDE) for v in (mine, moved))

            return block(0), [block(step).astype(LOW) for step in (1, 2, 3)]

        def away_blocks(sent):
            return [lax.ppermute(b, CHIP, turn) for b, turn in zip(sent, turns, strict=True)]

        def meet(own_block, sent, gate):
            far = away_blocks(sent)
            return own_block + sum(behind(f, gate).astype(WIDE) for f in far)

        def scatter(full):
            return lax.psum_scatter(full, CHIP, scatter_dimension=0, tiled=True)

        def halves(held):
            send = swap_core(part_of(held, 1 - core, local_rows).astype(LOW))
            return part_of(held, core, local_rows), send

        def give(widths, *sums):
            scale = 1.0 / math.sqrt(rows * dp * length)
            return call(
                functools.partial(emit, widths, scale),
                [shape((local_rows, 2 * w), WIDE) for _ in range(len(sums) // 2) for w in widths], where, *sums,
            )

        def all_sum(value):
            bit = 1
            while bit < chips:
                value = value + lax.ppermute(value, CHIP, [(k, k ^ bit) for k in range(chips)])
                bit *= 2
            return value

        def project(table, one, two):
            return exact(jax.nn.gelu(exact(table, one)), two)


        w_rest, shard_rest = gather([cross_query, cross_key, cross_value, cross_out, ffn_in, ffn_out], False)
        w_cross = Cols(w_rest, 0, 4 * quarter)
        w_ffn = Cols(w_rest, 4 * quarter, 4 * quarter + 2 * hidden)
        w_self, shard_self = gather([self_query, self_key, self_value, self_out], True, (shard_rest,))
        gate = w_self.blocks[1] if ring else shard_self
        ident_all, project_pull = jax.vjp(project, behind(task_table, gate), proj_first, proj_second)
        ident_low_all = ident_all.astype(LOW)
        gain_all = 1.0 + exact(ident_all, gen_gain)

        def spread(generator):
            made = dot(ident_low_all, generator).astype(LOW)
            made = made.reshape(tasks_all, local_rows, ADAPT).transpose(1, 0, 2)
            return made.reshape(local_rows, tasks_wide)

        down_here, up_here = spread(gen_down), spread(gen_up)
        keep, send = jnp.where(first, down_here, up_here), jnp.where(first, up_here, down_here)
        if ring:
            shard = jnp.concatenate([keep, swap_core(send)], 0)
            held = [shard, *(lax.ppermute(shard, CHIP, turn) for turn in turns)]
            generated = Pieces(held, [lax.ppermute(h, CHIP, side) for h in held])
        else:
            generated = lax.all_gather(order(keep, swap_core(send)), CHIP, axis=0, tiled=True)

        words = jnp.concatenate([segments, padding, jnp.broadcast_to(task_ids[:, None], (1, length))], 0)
        words = behind(words, gate)
        words_other = swap_core(words)
        words = [jnp.where(first, words, words_other), jnp.where(first, words_other, words)]
        own, memory, goal = (v.reshape(length, width) for v in (inputs, encoded, cotangent))
        own_other, memory_other, goal_other = swap_core(own), swap_core(memory), swap_core(goal)
        streams = [Pick(r, own, own_other) for r in both]
        memories = [Pick(r, memory, memory_other) for r in both]
        goals = [Pick(r, goal, goal_other) for r in both]
        weights = token_weights.astype(WIDE)
        onehots = [(w[2, 0] == jnp.arange(tasks_all)).astype(WIDE) for w in words]
        segqs = [w[:1] for w in words]
        segks = [jnp.where(w[1] == 1, w[0], -1)[:, None] for w in words]
        row_weights = [jnp.sum(o * weights) * (tasks_all / jnp.sum(weights)) for o in onehots]
        row_weights = [w.reshape(1, 1) for w in row_weights]
        gains_task = [exact(o[None], gain_all) for o in onehots]
        slots = lax.broadcasted_iota(jnp.int32, (tasks_wide, 2 * ADAPT), 0)
        places = lax.broadcasted_iota(jnp.int32, (tasks_wide, 2 * ADAPT), 1)
        wanted = jnp.where(places < ADAPT, words[0][2, 0], words[1][2, 0]) * ADAPT + places % ADAPT
        select = (slots == wanted).astype(LOW)
        g_self, g_cross, g_ffn = (g[None] for g in (gain_self, gain_cross, gain_ffn))

        ready = (*gains_task, *row_weights, *segks, select, g_self, g_cross, g_ffn)
        sent_early = tuple(generated.blocks[1:4]) if ring else ()
        picked = call(pick, [shape((width, 2 * ADAPT), LOW)], where, generated, select)[0]
        line = shape((1, width), WIDE)
        lse = shape((heads, length), WIDE)
        total_scratch = pltpu.VMEM((length, width), WIDE)
        unit = 2 * length * width

        def low(columns_wide):
            return shape((length, columns_wide), LOW)

        full_low = low(width)
        kept = [dict() for _ in both]
        chain, last = [], []

        def share(part, between=None):
            if last:
                part, _ = lax.optimization_barrier((part, last[0]))
            other = behind(swap_core(part), between)
            here = (part_of(part, core, half).astype(WIDE) + part_of(other, core, half).astype(WIDE)).astype(LOW)
            far = swap_pair(here)
            chain[:], last[:] = [here], [far]
            return part, other, far, swap_core(far)

        def stage(body, outs, *args, extra=(), **options):
            return call(body, outs, where, *args, after=(*chain, *extra), **options)

        def whole(weight):
            return [shape(weight.shape, LOW)] if isinstance(weight, Pieces) else []

        def forward_self(r):
            nonlocal w_self
            k = kept[r]
            k["first"], k["qkv"], k["context"], k["lse"], part, *more = stage(
                functools.partial(self_forward, heads, factor),
                [full_low, low(3 * quarter), low(quarter), lse, full_low, *whole(w_self)],
                streams[r], g_self, w_self, segqs[r], segks[r], extra=(*ready, *sent_early), flops=5 * unit * quarter,
            )
            w_self = (more or [w_self])[0]
            k["y"] = share(part)

        def forward_cross(r):
            k = kept[r]
            k["after_self"], k["second"], k["cq"], k["ckv"], k["c_context"], k["c_lse"], part = stage(
                functools.partial(cross_forward, heads, factor),
                [full_low, full_low, low(quarter), low(2 * quarter), low(quarter), lse, full_low],
                memories[r], w_cross, streams[r], *k["y"], g_cross, segqs[r], segks[r], extra=ready if r else (),
                flops=5 * unit * quarter, scratch=[total_scratch],
            )
            k["y"] = share(part)

        def forward_ffn(r):
            k = kept[r]
            k["after_cross"], k["third"], k["slope"], k["active"], part = stage(
                functools.partial(ffn_forward, hidden), [full_low, full_low, low(hidden), low(hidden), full_low],
                k["after_self"], *k["y"], g_ffn, w_ffn, extra=ready,
                flops=2 * unit * hidden, scratch=[total_scratch],
            )
            k["y"] = share(part)

        def into(r, name):
            return (kept[0][name],) if r else None

        def backward_ffn(r):
            k = kept[r]
            k["ffn_low"], k["grad_inner"], part, k["outputs"], k["grad_down"], k["grad_up"], k["grad_gain"] = stage(
                adapt_backward,
                [full_low, low(hidden), full_low, Owned(r, shape((length, width), WIDE), into(r, "outputs")),
                 shape((width, ADAPT), LOW), shape((ADAPT, width), LOW), line],
                k["after_cross"], *k["y"], gains_task[r], *made[r], goals[r], row_weights[r], segks[r],
                Cols(w_rest, w_ffn.start + hidden, w_ffn.stop), k["slope"], Cols(w_rest, w_ffn.start, w_ffn.start + hidden),
                flops=2 * unit * hidden + 5 * unit * 128, scratch=[total_scratch],
            )
            k["y"] = share(part)

        grads_scratch = [total_scratch, pltpu.VMEM((length, quarter), LOW)] + [pltpu.VMEM((length, quarter), WIDE)] * 2

        def backward_cross(r):
            k = kept[r]
            k["cross_low"], k["g3"], k["gcq"], k["gckv"], part, *k["memory"] = stage(
                functools.partial(cross_backward, heads, factor),
                [full_low, line, low(quarter), low(2 * quarter), full_low, Routed(r, full_low, kept[0]["memory"] if r else None)],
                *k["y"], k["after_cross"], k["ffn_low"], g_ffn, w_cross, k["cq"], k["ckv"], k["c_lse"], segqs[r], segks[r],
                flops=7 * unit * quarter, scratch=grads_scratch,
            )
            k["y"] = share(part)

        def backward_self(r, work=None):
            k = kept[r]
            k["self_low"], k["g2"], k["gqkv"], part = stage(
                functools.partial(self_backward, heads, factor), [full_low, line, low(3 * quarter), full_low],
                *k["y"], k["after_self"], k["cross_low"], g_cross, w_self, k["qkv"], k["lse"], segqs[r], segks[r],
                flops=7 * unit * quarter, scratch=grads_scratch,
            )
            if work is not None:
                k["sum"] = work()
            k["y"] = share(part, k.get("sum"))
            k["far"] = k["y"][2]

        def backward_input(r, after):
            k = kept[r]
            k["grad_x"], k["g1"] = call(
                input_backward, [Owned(r, shape((length, width), WIDE), into(r, "grad_x")), line],
                where, *k["y"], streams[r], k["self_low"], g_self, after=after, scratch=[total_scratch],
            )

        def pairs(*names):
            return [kept[r][name] for name in names for r in both]

        for r in both:
            forward_self(r)

        picked_other = swap_core(picked)
        downs = jnp.where(first, picked, picked_other)
        ups = jnp.where(first, picked_other, picked)
        made = [(downs[:, r * ADAPT : (r + 1) * ADAPT], ups[:, r * ADAPT : (r + 1) * ADAPT].reshape(ADAPT, width)) for r in both]
        ready = tuple(m for pair in made for m in pair)
        for r in both:
            forward_cross(r)
        for r in both:
            forward_ffn(r)
        for r in both:
            backward_ffn(r)
        tasks_here = dot_rows(
            jnp.concatenate([jnp.where(first, kept[r]["grad_down"], kept[r]["grad_up"].reshape(width, ADAPT)) for r in both], 1),
            select,
        ).astype(LOW)
        sum_ffn = call(
            functools.partial(weights_grad, [hidden, hidden]), [shape((width, 2 * hidden + tasks_wide), LOW)], where,
            *pairs("third", "grad_inner", "ffn_low", "active"), tasks_here, after=tuple(chain), flops=4 * unit * hidden,
        )[0]
        held_ffn = scatter(sum_ffn)
        for r in both:
            backward_cross(r)
        sum_cross = (
            call(
                functools.partial(weights_grad, [quarter, 2 * quarter, quarter]), [shape((width, 4 * quarter), LOW)], where,
                *pairs("second", "gcq"), *memories, *pairs("gckv", "cross_low", "c_context"), after=tuple(chain),
                flops=8 * unit * quarter,
            )[0]
        )
        if ring:
            away, mine = sides(sum_cross)
            moved = lax.ppermute(away, CHIP, side)
        chain += [away] if ring else [sum_cross]
        backward_self(0)
        sent_cross = []
        if ring:
            own_cross, sent_cross = blocks_of(mine, moved)

        def self_sum():
            return call(
                functools.partial(weights_grad, [3 * quarter, quarter]), [shape((width, 4 * quarter), LOW)], where,
                *pairs("first", "gqkv", "self_low", "context"), after=tuple(sent_cross), flops=8 * unit * quarter,
            )[0]

        backward_self(1, self_sum)
        sum_self = kept[1]["sum"]
        if ring:
            away, mine = sides(sum_self)
            backward_input(0, (*chain, away, *sent_cross))
            moved = behind(lax.ppermute(away, CHIP, side), kept[1]["far"])
            own_self, sent_self = blocks_of(mine, moved)
            backward_input(1, tuple(sent_self))
            held_cross = meet(own_cross, sent_cross, kept[0]["g1"])
            held_self = meet(own_self, sent_self, kept[1]["g1"])
        else:
            backward_input(0, ())
            backward_input(1, ())
            held_cross, held_self = scatter(sum_cross), scatter(sum_self)
        parts_ffn = halves(behind(held_ffn, sent_self[2] if ring else chain[0]))
        grad_in, grad_outer = give([hidden, hidden], *parts_ffn)
        found_mine, found_other = (p[:, 2 * hidden :].astype(WIDE) * (1.0 / math.sqrt(rows * dp * length)) for p in parts_ffn)
        found = order(found_mine, found_other, 1)
        given = give([quarter] * 4, *halves(held_cross), *halves(held_self))
        grads_cross, grads_self = given[:4], given[4:]
        scale = 1.0 / math.sqrt(rows * dp * length)

        keep, send = kept[1]["memory"]
        memory_part = (keep.astype(WIDE) + swap_core(send).astype(WIDE)).astype(LOW)
        memory_part = behind(memory_part, kept[0]["far"])
        grad_memory = memory_part.astype(WIDE) + swap_pair(memory_part).astype(WIDE)

        def narrow(value):
            value = value.reshape(local_rows, tasks_all, ADAPT).transpose(1, 0, 2)
            return value.reshape(tasks_all, local_rows * ADAPT).astype(LOW)

        found_down, found_up = narrow(found[:, :tasks_wide]), narrow(found[:, tasks_wide:])
        grad_gen_down = dot_inner(ident_low_all, found_down)
        grad_gen_up = dot_inner(ident_low_all, found_up)
        ident_part = dot_rows(found_down, gen_down) + dot_rows(found_up, gen_up)
        ident_part = ident_part + swap_core(ident_part)
        gain_part = sum(onehots[r][:, None] * behind(kept[r]["grad_gain"], sum_self) for r in both) * scale
        early = all_sum(jnp.concatenate([gain_part, jnp.pad(ident_part, ((0, 0), (0, width - ident_part.shape[1])))], 0))
        gain_sum, ident_sum = early[:tasks_all], early[tasks_all:, : ident_part.shape[1]]
        norms = [sum(kept[r][name] for r in both) for name in ("g1", "g2", "g3")]
        norm_sums = all_sum(jnp.concatenate(norms, 0)) * scale
        grad_gen_gain = exact(ident_all, gain_sum, ((0,), (0,)))
        grad_ident = ident_sum + exact(gain_sum, gen_gain, ((1,), (1,)))
        grad_table, grad_first_m, grad_second_m = project_pull(grad_ident)

        def shaped(value):
            return value.reshape(rows, length, width)

        return (
            shaped(kept[1]["outputs"]), shaped(kept[1]["grad_x"]), shaped(grad_memory), norm_sums[0], norm_sums[1], norm_sums[2],
            *grads_self, *grads_cross, grad_in, grad_outer, grad_gen_down, grad_gen_up,
            grad_gen_gain, grad_table, grad_first_m, grad_second_m,
        )

    data = (CHIP, CORE)
    three, matrix = P(data, None, None), P(data, PAIR)
    in_specs = (
        three, three, three, P(data, None), P(data, None), P(data), P(), P(), P(), P(),
        *(matrix,) * 10, P(None, data), P(None, data), P(), P(), P(), P(),
    )
    out_specs = (
        three, three, three, P(), P(), P(), *(matrix,) * 10, P(None, data), P(None, data), P(), P(), P(), P(),
    )
    return jax.shard_map(local, mesh=grid, in_specs=in_specs, out_specs=out_specs, check_vma=False)
```

```python
import functools
import math

import jax
import jax.numpy as jnp
from jax import lax
from jax.experimental import pallas as pl
from jax.experimental.pallas import tpu as pltpu
from jax.sharding import Mesh
from jax.sharding import PartitionSpec as P

HD = 64
ADAPT = 24
HIGHEST = lax.Precision.HIGHEST
EPSILON = 1e-06
MASKED = -1000000000.0
LOW = jnp.bfloat16
WIDE = jnp.float32
CHIP, CORE, PAIR = "chip", "core", "mp"
ACROSS = [(0, 1), (1, 0)]
SPAN = 128
ROOT = math.sqrt(2.0 / math.pi)


def dot(left, right):
    return lax.dot_general(left, right, (((1,), (0,)), ((), ())), preferred_element_type=WIDE)


def dot_rows(left, right):
    return lax.dot_general(left, right, (((1,), (1,)), ((), ())), preferred_element_type=WIDE)


def dot_inner(left, right):
    return lax.dot_general(left, right, (((0,), (0,)), ((), ())), preferred_element_type=WIDE)


def exact(left, right, dims=((1,), (0,))):
    return lax.dot_general(left, right, (dims, ((), ())), precision=HIGHEST, preferred_element_type=WIDE)


def rstd_of(value):
    return lax.rsqrt(jnp.mean(value * value, axis=-1, keepdims=True) + EPSILON)


def gelu_parts(value):
    square = value * value
    slope = jnp.tanh(ROOT * (value + 0.044715 * square * value))
    half = 0.5 * (1.0 + slope)
    return value * half, half + 0.5 * value * (1.0 - slope * slope) * ROOT * (1.0 + 0.134145 * square)


def shape(dims, dtype):
    return jax.ShapeDtypeStruct(dims, dtype)


class Cols:
    def __init__(self, array, start, stop):
        self.array, self.start, self.stop = array, start, stop


class Pick:
    def __init__(self, row, own, other):
        self.row, self.own, self.other = row, own, other


class Pieces:
    def __init__(self, held, other):
        self.blocks = [*held, *other]
        self.size = held[0].shape[0]
        self.shape = (len(self.blocks) * self.size, held[0].shape[1])
        self.dtype = held[0].dtype

    def places(self, where):
        part = self.size // 2
        for index in range(len(self.blocks)):
            z = lax.rem(where[1] + 4 - index % 4, 4)
            y = where[2] if index < 4 else 1 - where[2]
            for side in range(2):
                turn = where[0] if side == 0 else 1 - where[0]
                at = pl.multiple_of((2 * z + y) * self.size + turn * part, 16)
                yield index, slice(side * part, (side + 1) * part), pl.ds(at, part)


class Owned:
    def __init__(self, row, aval, into):
        self.row, self.aval, self.into = row, aval, into


class Halved:
    def __init__(self, aval):
        self.aval = aval


class Routed:
    def __init__(self, row, aval, into):
        self.row, self.aval, self.into = row, aval, into


class Box:
    def __init__(self, ref, copies):
        self.ref, self.copies, self.pending = ref, copies, False

    def each(self, act):
        for condition, copy in self.copies:
            if condition is None:
                act(copy)
            else:
                pl.when(condition)(functools.partial(act, copy))

    def start(self):
        self.each(lambda copy: copy.start())
        self.pending = True

    def wait(self):
        if self.pending:
            self.each(lambda copy: copy.wait())
            self.pending = False

    def get(self):
        self.wait()
        return self.ref

    def put(self, value):
        self.ref[...] = value
        self.start()

    def put_halves(self, make):
        middle = self.ref.shape[0] // 2
        for index, (_, copy) in enumerate(self.copies):
            rows = slice(index * middle, (index + 1) * middle)
            self.ref[rows, :] = make(rows)
            copy.start()
        self.pending = True


VMEM_LIMIT = 60 * 1024 * 1024


def call(body, outs, where, *args, after=(), flops=0, scratch=()):
    inputs, buffers, loads = [], [], []
    for arg in args:
        if isinstance(arg, Pick):
            loads.append((arg, len(inputs)))
            inputs += [arg.own, arg.other]
            buffers.append((arg.own.shape, arg.own.dtype))
        elif isinstance(arg, Cols):
            loads.append((arg, len(inputs)))
            inputs.append(arg.array)
            buffers.append(((arg.array.shape[0], arg.stop - arg.start), arg.array.dtype))
        elif isinstance(arg, Pieces):
            loads.append((arg, len(inputs)))
            inputs += arg.blocks
            buffers.append((arg.shape, arg.dtype))
        else:
            loads.append((arg, len(inputs)))
            inputs.append(arg)
            buffers.append((arg.shape, arg.dtype))
    avals, stores, aliases = [], [], {}
    for out in outs:
        special = isinstance(out, (Owned, Routed))
        aval = out.aval if special or isinstance(out, Halved) else out
        stores.append((out, len(avals)))
        buffers.append((aval.shape, aval.dtype))
        if special and out.into is not None:
            for array in out.into:
                aliases[1 + len(inputs)] = len(avals)
                inputs.append(array)
                avals.append(aval)
        else:
            avals += [aval] * (2 if isinstance(out, Routed) else 1)
    many = sum(2 * len(a.blocks) for a in args if isinstance(a, Pieces)) + sum(isinstance(o, Halved) for o in outs)
    moved = sum(math.prod(dims) * jnp.dtype(dtype).itemsize for dims, dtype in buffers)
    inputs += after

    def kernel(where_ref, *refs):
        in_refs, refs = refs[: len(inputs)], refs[len(inputs) :]
        out_refs, refs = refs[: len(avals)], refs[len(avals) :]
        own, refs = refs[: len(scratch)], refs[len(scratch) :]
        held, sems = refs[:-1], refs[-1]
        boxes, extra = [], len(buffers)
        for n, (arg, at) in enumerate(loads):
            if isinstance(arg, Pieces):
                copies = []
                for index, rows, place in arg.places(where_ref):
                    source, target = in_refs[at + index].at[rows, :], held[n].at[place, :]
                    copies.append((None, pltpu.make_async_copy(source, target, sems.at[extra])))
                    extra += 1
                boxes.append(Box(held[n], copies))
                boxes[-1].start()
                continue
            if isinstance(arg, Pick):
                mine = where_ref[0] == arg.row
                pairs = [(mine, in_refs[at]), (jnp.logical_not(mine), in_refs[at + 1])]
            elif isinstance(arg, Cols):
                pairs = [(None, in_refs[at].at[:, arg.start : arg.stop])]
            else:
                pairs = [(None, in_refs[at])]
            boxes.append(Box(held[n], [(c, pltpu.make_async_copy(s, held[n], sems.at[n])) for c, s in pairs]))
            boxes[-1].start()
        for n, (out, at) in enumerate(stores, len(loads)):
            pairs = [(None, out_refs[at])]
            if isinstance(out, Halved):
                middle = out.aval.shape[0] // 2
                copies = []
                for rows, sem in ((pl.ds(0, middle), n), (pl.ds(middle, middle), extra)):
                    copies.append((None, pltpu.make_async_copy(held[n].at[rows, :], out_refs[at].at[rows, :], sems.at[sem])))
                extra += 1
                boxes.append(Box(held[n], copies))
                continue
            if isinstance(out, (Owned, Routed)):
                mine = where_ref[0] == out.row
                pairs = [(mine, out_refs[at])]
                if isinstance(out, Routed):
                    pairs.append((jnp.logical_not(mine), out_refs[at + 1]))
            boxes.append(Box(held[n], [(c, pltpu.make_async_copy(held[n], d, sems.at[n])) for c, d in pairs]))
        body(where_ref, *boxes, *own)
        for box in boxes:
            box.wait()

    hbm = pl.BlockSpec(memory_space=pltpu.HBM)
    return pl.pallas_call(
        kernel,
        out_shape=tuple(avals),
        in_specs=[pl.BlockSpec(memory_space=pltpu.SMEM)] + [hbm] * len(inputs),
        out_specs=tuple(hbm for _ in avals),
        scratch_shapes=[*scratch, *(pltpu.VMEM(*b) for b in buffers), pltpu.SemaphoreType.DMA((len(buffers) + many,))],
        input_output_aliases=aliases,
        compiler_params=pltpu.CompilerParams(vmem_limit_bytes=VMEM_LIMIT),
        cost_estimate=pl.CostEstimate(flops=flops, bytes_accessed=moved, transcendentals=0),
    )(where, *inputs)


def at_half(core, half):
    return pl.ds(pl.multiple_of(core * half, half), half)


def windows(length, causal):
    for lo in range(0, length, SPAN):
        yield lo, max(lo - SPAN, 0), lo + SPAN if causal else min(lo + 2 * SPAN, length)


def mask_of(segq_ref, segk_ref, lo, start, stop, causal):
    dims = (stop - start, SPAN)
    keys = start + lax.broadcasted_iota(jnp.int32, dims, 0)
    queries = lo + lax.broadcasted_iota(jnp.int32, dims, 1)
    same = segk_ref[start:stop, :] == segq_ref[:, lo : lo + SPAN]
    if causal:
        same = same & (keys <= queries)
    return same | (keys == queries)


def beside(parts):
    return jnp.concatenate(parts, axis=1)


def lanes(value, count):
    return [value[:, i * SPAN : (i + 1) * SPAN] for i in range(count)]


def attend(q_at, k_at, v_at, segq_ref, segk_ref, context_ref, lse_ref, causal, heads, factor):
    for lo, start, stop in windows(context_ref.shape[0], causal):
        mask = beside([mask_of(segq_ref, segk_ref, lo, start, stop, causal)] * heads)
        scores = beside([dot_rows(k_at(h, start, stop), q_at(h, lo, lo + SPAN) * LOW(factor)) for h in range(heads)])
        scores = jnp.where(mask, scores, MASKED)
        top = jnp.max(scores, axis=0, keepdims=True)
        expos = jnp.exp(scores - top)
        total = jnp.sum(expos, axis=0, keepdims=True)
        probs = (expos * (1.0 / total)).astype(LOW)
        logs = lanes(top + jnp.log(total), heads)
        for h, part in enumerate(lanes(probs, heads)):
            context_ref[lo : lo + SPAN, h * HD : (h + 1) * HD] = dot_inner(part, v_at(h, start, stop)).astype(LOW)
            lse_ref[h : h + 1, lo : lo + SPAN] = logs[h]


def attend_back(q_at, k_at, v_at, g_at, segq_ref, segk_ref, lse_ref, gq_ref, gk_ref, gv_ref, causal, heads, factor):
    gk_ref[...] = jnp.zeros_like(gk_ref)
    gv_ref[...] = jnp.zeros_like(gv_ref)
    for lo, start, stop in windows(lse_ref.shape[1], causal):
        mask = beside([mask_of(segq_ref, segk_ref, lo, start, stop, causal)] * heads)
        queries = [q_at(h, lo, lo + SPAN) * LOW(factor) for h in range(heads)]
        keys = [k_at(h, start, stop) for h in range(heads)]
        grads = [g_at(h, lo, lo + SPAN) for h in range(heads)]
        scores = beside([dot_rows(keys[h], queries[h]) for h in range(heads)])
        logs = beside([lse_ref[h : h + 1, lo : lo + SPAN] for h in range(heads)])
        probs = jnp.exp(jnp.where(mask, scores, MASKED) - logs)
        grad_probs = beside([dot_rows(v_at(h, start, stop), grads[h]) for h in range(heads)])
        centre = jnp.sum(probs * grad_probs, axis=0, keepdims=True)
        grad_scores = lanes((probs * (grad_probs - centre)).astype(LOW), heads)
        for h, part in enumerate(lanes(probs.astype(LOW), heads)):
            cols = slice(h * HD, (h + 1) * HD)
            gv_ref[start:stop, cols] += dot(part, grads[h])
            gk_ref[start:stop, cols] += dot(grad_scores[h], queries[h])
            gq_ref[lo : lo + SPAN, cols] = (dot_inner(grad_scores[h], keys[h]) * factor).astype(LOW)


def columns(ref, at):
    return lambda h, lo, hi: ref[lo:hi, at + h * HD : at + (h + 1) * HD]


def branch(core, pack):
    mine, other, *far = pack
    half = far[0].ref.shape[0]
    for index, box in zip((core, 1 - core), far, strict=True):
        rows = at_half(index, half)
        here = (mine.get()[rows, :].astype(WIDE) + other.get()[rows, :].astype(WIDE)).astype(LOW)
        yield rows, here.astype(WIDE) + box.get()[...].astype(WIDE)


def wide(box):
    return box.get()[...].astype(WIDE)


def norm_next(core, pack, before, gain, after, normed):
    for rows, moved in branch(core, pack):
        value = (moved + before.get()[rows, :].astype(WIDE)).astype(LOW)
        after.ref[rows, :] = value
        value = value.astype(WIDE)
        normed.ref[rows, :] = (value * rstd_of(value) * gain.get()[...]).astype(LOW)
    after.start()
    normed.start()


def self_forward(heads, factor, where, own, gain, w, segq, segk, first, qkv, context, lse, part, *whole):
    third = heads * HD
    value = wide(own)
    first.put((value * rstd_of(value) * gain.get()[...]).astype(LOW))
    w_ref = w.get()
    qkv.put(dot(first.ref[...], w_ref[:, : 3 * third]).astype(LOW))
    attend(columns(qkv.ref, 0), columns(qkv.ref, third), columns(qkv.ref, 2 * third), segq.get(), segk.get(),
           context.ref, lse.ref, True, heads, factor)
    context.start()
    lse.start()
    part.put_halves(lambda rows: dot_rows(context.ref[rows, :], w_ref[:, 3 * third : 4 * third]).astype(LOW))
    hand_on(w, whole)


def cross_forward(heads, factor, where, memory, w, before, mine, theirs, far, far_other, gain, segq, segk,
                  after, second, cq, ckv, context, lse, part):
    third = heads * HD
    memory_ref, w_ref = memory.get(), w.get()
    ckv.put(dot(memory_ref[...], w_ref[:, third : 3 * third]).astype(LOW))
    norm_next(where[0], (mine, theirs, far, far_other), before, gain, after, second)
    cq.put(dot(second.ref[...], w_ref[:, :third]).astype(LOW))
    attend(columns(cq.ref, 0), columns(ckv.ref, 0), columns(ckv.ref, third), segq.get(), segk.get(),
           context.ref, lse.ref, False, heads, factor)
    context.start()
    lse.start()
    part.put_halves(lambda rows: dot_rows(context.ref[rows, :], w_ref[:, 3 * third : 4 * third]).astype(LOW))


def ffn_forward(hidden, where, before, mine, theirs, far, far_other, gain, w, after, third, slope, active, part):
    norm_next(where[0], (mine, theirs, far, far_other), before, gain, after, third)
    w_ref = w.get()
    act, rate = gelu_parts(dot(third.ref[...], w_ref[:, :hidden]))
    active.put(act.astype(LOW))
    slope.put(rate.astype(LOW))
    part.put_halves(lambda rows: dot_rows(active.ref[rows, :], w_ref[:, hidden : 2 * hidden]).astype(LOW))


def adapt_backward(where, before, mine, theirs, far, far_other, gain, down, up, goal, weight, segk, w_out, slope, w_in,
                   low, inner, part, outputs, down_grad, up_grad, gain_grad, total_ref):
    for rows, moved in branch(where[0], (mine, theirs, far, far_other)):
        total_ref[rows, :] = moved + before.get()[rows, :].astype(WIDE)
    value = total_ref[...]
    rstd = rstd_of(value)
    normed = value * rstd
    gain_ref, down_ref, up_ref = gain.get(), down.get(), up.get()
    adapt_in = (normed * gain_ref[...]).astype(LOW)
    act, rate = gelu_parts(dot(adapt_in, down_ref[...]))
    act = act.astype(LOW)
    outputs.put(value + dot(act, up_ref[...]))
    grad_out = wide(goal) * jnp.where(segk.get()[...] >= 0, weight.get()[...], 0.0)
    out_low = grad_out.astype(LOW)
    grad_bottle = (dot_rows(out_low, up_ref[...]) * rate).astype(LOW)
    grad_in = dot_rows(grad_bottle, down_ref[...])
    gain_grad.put(jnp.sum(grad_in * normed, axis=0, keepdims=True))
    scaled = grad_in * gain_ref[...]
    total = grad_out + rstd * (scaled - normed * jnp.mean(scaled * normed, axis=-1, keepdims=True))
    low.put(total.astype(LOW))
    inner.put((dot(low.ref[...], w_out.get()[...]) * wide(slope)).astype(LOW))
    part.put(dot_rows(inner.ref[...], w_in.get()[...]).astype(LOW))
    up_grad.put(dot_inner(act, out_low).astype(LOW))
    down_grad.put(dot_inner(adapt_in, grad_bottle).astype(LOW))


def norm_back(core, pack, value, before, gain, grad, gain_grad):
    total = 0.0
    for rows, moved in branch(core, pack):
        here = value.get()[rows, :].astype(WIDE)
        rstd = rstd_of(here)
        normed = here * rstd
        total = total + jnp.sum(moved * normed, axis=0, keepdims=True)
        scaled = moved * gain.get()[...]
        here = rstd * (scaled - normed * jnp.mean(scaled * normed, axis=-1, keepdims=True))
        grad.ref[rows, :] = (here + before.get()[rows, :].astype(WIDE)).astype(grad.ref.dtype)
    grad.start()
    gain_grad.put(total)


def cross_backward(heads, factor, where, mine, theirs, far, far_other, value, before, gain, w, cq, ckv, lse, segq, segk,
                   low, gain_grad, gq, gkv, part, memory, g_ref, gk_ref, gv_ref):
    third = heads * HD
    norm_back(where[0], (mine, theirs, far, far_other), value, before, gain, low, gain_grad)
    w_ref = w.get()
    g_ref[...] = dot(low.ref[...], w_ref[:, 3 * third : 4 * third]).astype(LOW)
    attend_back(columns(cq.get(), 0), columns(ckv.get(), 0), columns(ckv.get(), third), columns(g_ref, 0), segq.get(), segk.get(),
                lse.get(), gq.ref, gk_ref, gv_ref, False, heads, factor)
    gq.start()
    part.put(dot_rows(gq.ref[...], w_ref[:, :third]).astype(LOW))
    gkv.ref[:, :third] = gk_ref[...].astype(LOW)
    gkv.ref[:, third:] = gv_ref[...].astype(LOW)
    gkv.start()
    memory.put(dot_rows(gkv.ref[...], w_ref[:, third : 3 * third]).astype(LOW))


def self_backward(heads, factor, where, mine, theirs, far, far_other, value, before, gain, w, qkv, lse, segq, segk,
                  low, gain_grad, gqkv, part, g_ref, gk_ref, gv_ref):
    third = heads * HD
    norm_back(where[0], (mine, theirs, far, far_other), value, before, gain, low, gain_grad)
    w_ref = w.get()
    g_ref[...] = dot(low.ref[...], w_ref[:, 3 * third : 4 * third]).astype(LOW)
    qkv_ref = qkv.get()
    attend_back(columns(qkv_ref, 0), columns(qkv_ref, third), columns(qkv_ref, 2 * third), columns(g_ref, 0),
                segq.get(), segk.get(), lse.get(), gqkv.ref, gk_ref, gv_ref, True, heads, factor)
    gqkv.ref[:, third : 2 * third] = gk_ref[...].astype(LOW)
    gqkv.ref[:, 2 * third :] = gv_ref[...].astype(LOW)
    gqkv.start()
    part.put_halves(lambda rows: dot_rows(gqkv.ref[rows, :], w_ref[:, : 3 * third]).astype(LOW))


def input_backward(where, mine, theirs, far, far_other, own, before, gain, grad, gain_grad):
    norm_back(where[0], (mine, theirs, far, far_other), own, before, gain, grad, gain_grad)


def pair_dot(left0, left1, right0, right1):
    return (dot_inner(left0.get()[...], right0.get()[...]) + dot_inner(left1.get()[...], right1.get()[...])).astype(LOW)


def weights_grad(widths, where, *refs):
    *boxes, out = refs
    at = 0
    for index, size in enumerate(widths):
        out.ref[:, at : at + size] = pair_dot(*boxes[4 * index : 4 * index + 4])
        at += size
    for box in boxes[4 * len(widths) :]:
        out.ref[:, at : at + box.ref.shape[1]] = box.get()[...]
    out.start()


def emit(widths, scale, where, *refs):
    count = len(refs) // (2 + len(widths))
    sums, outs = refs[: 2 * count], refs[2 * count :]
    for box in sums:
        box.wait()

    def put_in(index, first, second):
        at = 0
        for size, out in zip(widths, outs[index * len(widths) :], strict=False):
            out.ref[:, :size] = first[:, at : at + size].astype(WIDE) * scale
            out.ref[:, size:] = second[:, at : at + size].astype(WIDE) * scale
            at += size

    @pl.when(where[0] == 0)
    def _():
        for index in range(count):
            put_in(index, sums[2 * index].ref, sums[2 * index + 1].ref)

    @pl.when(where[0] != 0)
    def _():
        for index in range(count):
            put_in(index, sums[2 * index + 1].ref, sums[2 * index].ref)

    for out in outs:
        out.start()


def pick(where, generated, select, out):
    out.put(dot(generated.get()[...], select.get()[...]).astype(LOW))


def hand_on(weight, outs):
    for out in outs:
        out.put(weight.ref[...])


def pack_rows(where, *refs):
    *weights, keep, send = refs
    for weight in weights:
        weight.wait()

    def put_in(core):
        at = 0
        for weight in weights:
            size = weight.ref.shape[1] // 2
            send.ref[:, at : at + size] = weight.ref[:, (1 - core) * size : (2 - core) * size]
            keep.ref[:, at : at + size] = weight.ref[:, core * size : (core + 1) * size]
            at += size

    @pl.when(where[0] == 0)
    def _():
        put_in(0)

    @pl.when(where[0] != 0)
    def _():
        put_in(1)

    send.start()
    keep.start()


def swap_core(value):
    return lax.ppermute(value, CORE, ACROSS)


def swap_pair(value):
    return lax.ppermute(value, PAIR, ACROSS)


def solution(mesh):
    dp, mp = mesh.devices.shape
    chips = dp // 2
    grid = Mesh(mesh.devices.reshape(chips, 2, mp), (CHIP, CORE, PAIR))
    ring = chips == 8

    def local(
        inputs, encoded, cotangent, segments, padding, task_ids, token_weights, gain_self, gain_cross, gain_ffn,
        self_query, self_key, self_value, self_out, cross_query, cross_key, cross_value, cross_out, ffn_in, ffn_out,
        gen_down, gen_up, gen_gain, task_table, proj_first, proj_second,
    ):
        rows, length, width = inputs.shape
        half = length // 2
        core = lax.axis_index(CORE)
        chip = lax.axis_index(CHIP)
        z, y = chip // 2, chip % 2
        where = jnp.stack([core, z, y]).astype(jnp.int32)
        first = core == 0
        factor = HD ** (-0.5)
        tasks_all = task_table.shape[0]
        local_rows = self_query.shape[0]
        chip_rows = 2 * local_rows
        quarter = self_query.shape[1] // 2
        heads = quarter // HD
        hidden = ffn_in.shape[1] // 2
        tasks_wide = tasks_all * ADAPT
        both = range(2)

        def order(mine, other, axis=0):
            return jnp.where(
                first, jnp.concatenate([mine, other], axis), jnp.concatenate([other, mine], axis)
            )

        def part_of(value, index, size, axis=0):
            return lax.dynamic_slice_in_dim(value, index * size, size, axis)

        turns = [[(k, (k + 2 * step) % chips) for k in range(chips)] for step in (1, 2, 3)]
        side = [(k, k ^ 1) for k in range(chips)]

        def behind(value, gate):
            return value if gate is None else lax.optimization_barrier((value, gate))[0]

        def gather(weights, soon, after=()):
            total = sum(w.shape[1] // 2 for w in weights)
            if ring:
                keep, send = call(pack_rows, [shape((local_rows, total), LOW)] * 2, where, *weights, after=after)
            else:
                keep = jnp.concatenate([part_of(w, core, w.shape[1] // 2, 1) for w in weights], 1)
                send = jnp.concatenate([part_of(w, 1 - core, w.shape[1] // 2, 1) for w in weights], 1)
            moved = swap_core(send)
            if not (ring and soon):
                shard = order(keep, moved)
                return lax.all_gather(shard, CHIP, axis=0, tiled=True), shard
            shard = jnp.concatenate([keep, moved], 0)
            held = [shard]
            for _ in range(3):
                held.append(lax.ppermute(held[-1], CHIP, turns[0]))
            return Pieces(held, [lax.ppermute(h, CHIP, side) for h in held]), shard

        def sides(full):
            blocks = full.reshape(4, 2, chip_rows, full.shape[1])
            return [lax.dynamic_index_in_dim(blocks, at, 1, keepdims=False) for at in (1 - y, y)]

        def blocks_of(mine, moved):
            def block(step):
                at = (z + step) % 4
                return sum(lax.dynamic_index_in_dim(v, at, 0, keepdims=False).astype(WIDE) for v in (mine, moved))

            return block(0), [block(step).astype(LOW) for step in (1, 2, 3)]

        def away_blocks(sent):
            return [lax.ppermute(b, CHIP, turn) for b, turn in zip(sent, turns, strict=True)]

        def meet(own_block, sent, gate):
            far = away_blocks(sent)
            return own_block + sum(behind(f, gate).astype(WIDE) for f in far)

        def scatter(full):
            return lax.psum_scatter(full, CHIP, scatter_dimension=0, tiled=True)

        def halves(held):
            send = swap_core(part_of(held, 1 - core, local_rows).astype(LOW))
            return part_of(held, core, local_rows), send

        def give(widths, *sums, after=()):
            scale = 1.0 / math.sqrt(rows * dp * length)
            return call(
                functools.partial(emit, widths, scale),
                [shape((local_rows, 2 * w), WIDE) for _ in range(len(sums) // 2) for w in widths], where, *sums, after=after,
            )

        def all_sum(value):
            bit = 1
            while bit < chips:
                value = value + lax.ppermute(value, CHIP, [(k, k ^ bit) for k in range(chips)])
                bit *= 2
            return value

        def project(table, one, two):
            return exact(jax.nn.gelu(exact(table, one)), two)


        w_rest, shard_rest = gather([cross_query, cross_key, cross_value, cross_out, ffn_in, ffn_out], False)
        w_cross = Cols(w_rest, 0, 4 * quarter)
        w_ffn = Cols(w_rest, 4 * quarter, 4 * quarter + 2 * hidden)
        w_self, shard_self = gather([self_query, self_key, self_value, self_out], True, (shard_rest,))
        gate = w_self.blocks[1] if ring else shard_self
        ident_all, project_pull = jax.vjp(project, behind(task_table, gate), proj_first, proj_second)
        ident_low_all = ident_all.astype(LOW)
        gain_all = 1.0 + exact(ident_all, gen_gain)

        def spread(generator):
            made = dot(ident_low_all, generator).astype(LOW)
            made = made.reshape(tasks_all, local_rows, ADAPT).transpose(1, 0, 2)
            return made.reshape(local_rows, tasks_wide)

        down_here, up_here = spread(gen_down), spread(gen_up)
        keep, send = jnp.where(first, down_here, up_here), jnp.where(first, up_here, down_here)
        if ring:
            shard = jnp.concatenate([keep, swap_core(send)], 0)
            held = [shard, *(lax.ppermute(shard, CHIP, turn) for turn in turns)]
            generated = Pieces(held, [lax.ppermute(h, CHIP, side) for h in held])
        else:
            generated = lax.all_gather(order(keep, swap_core(send)), CHIP, axis=0, tiled=True)

        words = jnp.concatenate([segments, padding, jnp.broadcast_to(task_ids[:, None], (1, length))], 0)
        words = behind(words, gate)
        words_other = swap_core(words)
        words = [jnp.where(first, words, words_other), jnp.where(first, words_other, words)]
        own, memory, goal = (v.reshape(length, width) for v in (inputs, encoded, cotangent))
        own_other, memory_other, goal_other = swap_core(own), swap_core(memory), swap_core(goal)
        streams = [Pick(r, own, own_other) for r in both]
        memories = [Pick(r, memory, memory_other) for r in both]
        goals = [Pick(r, goal, goal_other) for r in both]
        weights = token_weights.astype(WIDE)
        onehots = [(w[2, 0] == jnp.arange(tasks_all)).astype(WIDE) for w in words]
        segqs = [w[:1] for w in words]
        segks = [jnp.where(w[1] == 1, w[0], -1)[:, None] for w in words]
        row_weights = [jnp.sum(o * weights) * (tasks_all / jnp.sum(weights)) for o in onehots]
        row_weights = [w.reshape(1, 1) for w in row_weights]
        gains_task = [exact(o[None], gain_all) for o in onehots]
        slots = lax.broadcasted_iota(jnp.int32, (tasks_wide, 2 * ADAPT), 0)
        places = lax.broadcasted_iota(jnp.int32, (tasks_wide, 2 * ADAPT), 1)
        wanted = jnp.where(places < ADAPT, words[0][2, 0], words[1][2, 0]) * ADAPT + places % ADAPT
        select = (slots == wanted).astype(LOW)
        g_self, g_cross, g_ffn = (g[None] for g in (gain_self, gain_cross, gain_ffn))

        ready = (*gains_task, *row_weights, *segks, select, g_self, g_cross, g_ffn)
        sent_early = tuple(generated.blocks[1:4]) if ring else ()
        picked = call(pick, [shape((width, 2 * ADAPT), LOW)], where, generated, select)[0]
        line = shape((1, width), WIDE)
        lse = shape((heads, length), WIDE)
        total_scratch = pltpu.VMEM((length, width), WIDE)
        unit = 2 * length * width

        def low(columns_wide):
            return shape((length, columns_wide), LOW)

        full_low = low(width)
        kept = [dict() for _ in both]
        chain, last = [], []

        def share(part, between=None):
            if last:
                part, _ = lax.optimization_barrier((part, last[0]))
            other = behind(swap_core(part), between)
            here = (part_of(part, core, half).astype(WIDE) + part_of(other, core, half).astype(WIDE)).astype(LOW)
            far = swap_pair(here)
            chain[:], last[:] = [here], [far]
            return part, other, far, swap_core(far)

        def stage(body, outs, *args, extra=(), **options):
            return call(body, outs, where, *args, after=(*chain, *extra), **options)

        def whole(weight):
            return [shape(weight.shape, LOW)] if isinstance(weight, Pieces) else []

        def forward_self(r):
            nonlocal w_self
            k = kept[r]
            k["first"], k["qkv"], k["context"], k["lse"], part, *more = stage(
                functools.partial(self_forward, heads, factor),
                [full_low, low(3 * quarter), low(quarter), lse, Halved(full_low), *whole(w_self)],
                streams[r], g_self, w_self, segqs[r], segks[r], extra=(picked,) if r else (*ready, *sent_early), flops=5 * unit * quarter,
            )
            w_self = (more or [w_self])[0]
            k["y"] = share(part)

        def forward_cross(r):
            k = kept[r]
            k["after_self"], k["second"], k["cq"], k["ckv"], k["c_context"], k["c_lse"], part = stage(
                functools.partial(cross_forward, heads, factor),
                [full_low, full_low, low(quarter), low(2 * quarter), low(quarter), lse, Halved(full_low)],
                memories[r], w_cross, streams[r], *k["y"], g_cross, segqs[r], segks[r], extra=ready if r else (),
                flops=5 * unit * quarter,
            )
            k["y"] = share(part)

        def forward_ffn(r):
            k = kept[r]
            k["after_cross"], k["third"], k["slope"], k["active"], part = stage(
                functools.partial(ffn_forward, hidden), [full_low, full_low, low(hidden), low(hidden), Halved(full_low)],
                k["after_self"], *k["y"], g_ffn, w_ffn, extra=ready,
                flops=2 * unit * hidden,
            )
            k["y"] = share(part)

        def into(r, name):
            return (kept[0][name],) if r else None

        def backward_ffn(r):
            k = kept[r]
            k["ffn_low"], k["grad_inner"], part, k["outputs"], k["grad_down"], k["grad_up"], k["grad_gain"] = stage(
                adapt_backward,
                [full_low, low(hidden), full_low, Owned(r, shape((length, width), WIDE), into(r, "outputs")),
                 shape((width, ADAPT), LOW), shape((ADAPT, width), LOW), line],
                k["after_cross"], *k["y"], gains_task[r], *made[r], goals[r], row_weights[r], segks[r],
                Cols(w_rest, w_ffn.start + hidden, w_ffn.stop), k["slope"], Cols(w_rest, w_ffn.start, w_ffn.start + hidden),
                flops=2 * unit * hidden + 5 * unit * 128, scratch=[total_scratch],
            )
            k["y"] = share(part)

        grads_scratch = [pltpu.VMEM((length, quarter), LOW)] + [pltpu.VMEM((length, quarter), WIDE)] * 2

        def backward_cross(r):
            k = kept[r]
            k["cross_low"], k["g3"], k["gcq"], k["gckv"], part, *k["memory"] = stage(
                functools.partial(cross_backward, heads, factor),
                [full_low, line, low(quarter), low(2 * quarter), full_low, Routed(r, full_low, kept[0]["memory"] if r else None)],
                *k["y"], k["after_cross"], k["ffn_low"], g_ffn, w_cross, k["cq"], k["ckv"], k["c_lse"], segqs[r], segks[r],
                flops=7 * unit * quarter, scratch=grads_scratch,
            )
            k["y"] = share(part)

        def backward_self(r, work=None):
            k = kept[r]
            k["self_low"], k["g2"], k["gqkv"], part = stage(
                functools.partial(self_backward, heads, factor), [full_low, line, low(3 * quarter), Halved(full_low)],
                *k["y"], k["after_self"], k["cross_low"], g_cross, w_self, k["qkv"], k["lse"], segqs[r], segks[r],
                flops=7 * unit * quarter, scratch=grads_scratch,
            )
            if work is not None:
                k["sum"] = work()
            k["y"] = share(part, k.get("sum"))
            k["far"] = k["y"][2]

        def backward_input(r, after):
            k = kept[r]
            k["grad_x"], k["g1"] = call(
                input_backward, [Owned(r, shape((length, width), WIDE), into(r, "grad_x")), line],
                where, *k["y"], streams[r], k["self_low"], g_self, after=after,
            )

        def pairs(*names):
            return [kept[r][name] for name in names for r in both]

        for r in both:
            forward_self(r)

        picked_other = swap_core(picked)
        downs = jnp.where(first, picked, picked_other)
        ups = jnp.where(first, picked_other, picked)
        made = [(downs[:, r * ADAPT : (r + 1) * ADAPT], ups[:, r * ADAPT : (r + 1) * ADAPT].reshape(ADAPT, width)) for r in both]
        ready = tuple(m for pair in made for m in pair)
        for r in both:
            forward_cross(r)
        for r in both:
            forward_ffn(r)
        for r in both:
            backward_ffn(r)
        tasks_here = dot_rows(
            jnp.concatenate([jnp.where(first, kept[r]["grad_down"], kept[r]["grad_up"].reshape(width, ADAPT)) for r in both], 1),
            select,
        ).astype(LOW)
        sum_ffn = call(
            functools.partial(weights_grad, [hidden, hidden]), [shape((width, 2 * hidden + tasks_wide), LOW)], where,
            *pairs("third", "grad_inner", "ffn_low", "active"), tasks_here, after=tuple(chain), flops=4 * unit * hidden,
        )[0]
        held_ffn = scatter(sum_ffn)
        for r in both:
            backward_cross(r)
        sum_cross = (
            call(
                functools.partial(weights_grad, [quarter, 2 * quarter, quarter]), [shape((width, 4 * quarter), LOW)], where,
                *pairs("second", "gcq"), *memories, *pairs("gckv", "cross_low", "c_context"), after=tuple(chain),
                flops=8 * unit * quarter,
            )[0]
        )
        if ring:
            away, mine = sides(sum_cross)
            moved = lax.ppermute(away, CHIP, side)
        chain += [away] if ring else [sum_cross]
        backward_self(0)
        cross = (mine, moved) if ring else ()

        def self_sum():
            return call(
                functools.partial(weights_grad, [3 * quarter, quarter]), [shape((width, 4 * quarter), LOW)], where,
                *pairs("first", "gqkv", "self_low", "context"), after=cross[1:], flops=8 * unit * quarter,
            )[0]

        backward_self(1, self_sum)
        sum_self = kept[1]["sum"]
        if ring:
            away, mine = sides(sum_self)
            own_cross, sent_cross = blocks_of(cross[0], behind(cross[1], away))
            backward_input(0, (*chain, away, *sent_cross))
            moved = behind(lax.ppermute(away, CHIP, side), kept[0]["g1"])
            own_self, sent_self = blocks_of(mine, moved)
            backward_input(1, tuple(sent_self))
            held_cross = meet(own_cross, sent_cross, kept[0]["g1"])
            far_self = away_blocks(sent_self)
            held_self = own_self + sum(behind(f, kept[1]["g1"]).astype(WIDE) for f in far_self)
        else:
            backward_input(0, ())
            backward_input(1, ())
            held_cross, held_self = scatter(sum_cross), scatter(sum_self)
        parts_ffn = halves(behind(held_ffn, sent_self[2] if ring else chain[0]))
        found_mine, found_other = (p[:, 2 * hidden :].astype(WIDE) * (1.0 / math.sqrt(rows * dp * length)) for p in parts_ffn)
        found = order(found_mine, found_other, 1)
        given = give([quarter] * 4, *halves(held_cross), *halves(held_self))
        grads_cross, grads_self = given[:4], given[4:]
        scale = 1.0 / math.sqrt(rows * dp * length)

        keep, send = kept[1]["memory"]
        memory_part = (behind(keep, sum_self).astype(WIDE) + swap_core(send).astype(WIDE)).astype(LOW)
        memory_part = behind(memory_part, kept[0]["far"])
        grad_memory = memory_part.astype(WIDE) + swap_pair(memory_part).astype(WIDE)

        def narrow(value):
            value = value.reshape(local_rows, tasks_all, ADAPT).transpose(1, 0, 2)
            return value.reshape(tasks_all, local_rows * ADAPT).astype(LOW)

        found_down, found_up = narrow(found[:, :tasks_wide]), narrow(found[:, tasks_wide:])
        grad_gen_down = dot_inner(ident_low_all, found_down)
        grad_gen_up = dot_inner(ident_low_all, found_up)
        ident_part = dot_rows(found_down, gen_down) + dot_rows(found_up, gen_up)
        ident_part = ident_part + swap_core(ident_part)
        ident_pad = jnp.pad(ident_part, ((0, 0), (0, width - ident_part.shape[1])))
        grad_in, grad_outer = give([hidden, hidden], *parts_ffn, after=(ident_pad,))
        gain_part = sum(onehots[r][:, None] * behind(kept[r]["grad_gain"], sum_self) for r in both) * scale
        norms = [sum(kept[r][name] for r in both) for name in ("g1", "g2", "g3")]
        sums = all_sum(jnp.concatenate([gain_part, ident_pad, *norms], 0))
        gain_sum, ident_sum = sums[:tasks_all], sums[tasks_all : 2 * tasks_all, : ident_part.shape[1]]
        norm_sums = sums[2 * tasks_all :] * scale
        grad_gen_gain = exact(ident_all, gain_sum, ((0,), (0,)))
        grad_ident = ident_sum + exact(gain_sum, gen_gain, ((1,), (1,)))
        grad_table, grad_first_m, grad_second_m = project_pull(grad_ident)

        def shaped(value):
            return value.reshape(rows, length, width)

        return (
            shaped(kept[1]["outputs"]), shaped(kept[1]["grad_x"]), shaped(grad_memory), norm_sums[0], norm_sums[1], norm_sums[2],
            *grads_self, *grads_cross, grad_in, grad_outer, grad_gen_down, grad_gen_up,
            grad_gen_gain, grad_table, grad_first_m, grad_second_m,
        )

    data = (CHIP, CORE)
    three, matrix = P(data, None, None), P(data, PAIR)
    in_specs = (
        three, three, three, P(data, None), P(data, None), P(data), P(), P(), P(), P(),
        *(matrix,) * 10, P(None, data), P(None, data), P(), P(), P(), P(),
    )
    out_specs = (
        three, three, three, P(), P(), P(), *(matrix,) * 10, P(None, data), P(None, data), P(), P(), P(), P(),
    )
    return jax.shard_map(local, mesh=grid, in_specs=in_specs, out_specs=out_specs, check_vma=False)
```

```python
import functools
import math

import jax
import jax.numpy as jnp
from jax import lax
from jax.experimental import pallas as pl
from jax.experimental.pallas import tpu as pltpu
from jax.sharding import Mesh
from jax.sharding import PartitionSpec as P

HD = 64
ADAPT = 24
HIGHEST = lax.Precision.HIGHEST
EPSILON = 1e-06
MASKED = -1000000000.0
LOW = jnp.bfloat16
WIDE = jnp.float32
CHIP, CORE, PAIR = "chip", "core", "mp"
ACROSS = [(0, 1), (1, 0)]
SPAN = 128
ROOT = math.sqrt(2.0 / math.pi)


def dot(left, right):
    return lax.dot_general(left, right, (((1,), (0,)), ((), ())), preferred_element_type=WIDE)


def dot_rows(left, right):
    return lax.dot_general(left, right, (((1,), (1,)), ((), ())), preferred_element_type=WIDE)


def dot_inner(left, right):
    return lax.dot_general(left, right, (((0,), (0,)), ((), ())), preferred_element_type=WIDE)


def exact(left, right, dims=((1,), (0,))):
    return lax.dot_general(left, right, (dims, ((), ())), precision=HIGHEST, preferred_element_type=WIDE)


def rstd_of(value):
    return lax.rsqrt(jnp.mean(value * value, axis=-1, keepdims=True) + EPSILON)


def gelu_parts(value):
    square = value * value
    slope = jnp.tanh(ROOT * (value + 0.044715 * square * value))
    half = 0.5 * (1.0 + slope)
    return value * half, half + 0.5 * value * (1.0 - slope * slope) * ROOT * (1.0 + 0.134145 * square)


def shape(dims, dtype):
    return jax.ShapeDtypeStruct(dims, dtype)


class Cols:
    def __init__(self, array, start, stop):
        self.array, self.start, self.stop = array, start, stop


class Pick:
    def __init__(self, row, own, other):
        self.row, self.own, self.other = row, own, other


class Pieces:
    def __init__(self, held, other):
        self.blocks = [*held, *other]
        self.size = held[0].shape[0]
        self.shape = (len(self.blocks) * self.size, held[0].shape[1])
        self.dtype = held[0].dtype

    def places(self, where):
        part = self.size // 2
        for index in range(len(self.blocks)):
            z = lax.rem(where[1] + 4 - index % 4, 4)
            y = where[2] if index < 4 else 1 - where[2]
            for side in range(2):
                turn = where[0] if side == 0 else 1 - where[0]
                at = pl.multiple_of((2 * z + y) * self.size + turn * part, 16)
                yield index, slice(side * part, (side + 1) * part), pl.ds(at, part)


class Owned:
    def __init__(self, row, aval, into):
        self.row, self.aval, self.into = row, aval, into


class Halved:
    def __init__(self, aval):
        self.aval = aval


class Routed:
    def __init__(self, row, aval, into):
        self.row, self.aval, self.into = row, aval, into


class Box:
    def __init__(self, ref, copies):
        self.ref, self.copies, self.pending = ref, copies, False

    def each(self, act):
        for condition, copy in self.copies:
            if condition is None:
                act(copy)
            else:
                pl.when(condition)(functools.partial(act, copy))

    def start(self):
        self.each(lambda copy: copy.start())
        self.pending = True

    def wait(self):
        if self.pending:
            self.each(lambda copy: copy.wait())
            self.pending = False

    def get(self):
        self.wait()
        return self.ref

    def put(self, value):
        self.ref[...] = value
        self.start()

    def put_halves(self, make):
        middle = self.ref.shape[0] // 2
        for index, (_, copy) in enumerate(self.copies):
            rows = slice(index * middle, (index + 1) * middle)
            self.ref[rows, :] = make(rows)
            copy.start()
        self.pending = True


VMEM_LIMIT = 60 * 1024 * 1024


def call(body, outs, where, *args, after=(), flops=0, scratch=()):
    inputs, buffers, loads = [], [], []
    for arg in args:
        if isinstance(arg, Pick):
            loads.append((arg, len(inputs)))
            inputs += [arg.own, arg.other]
            buffers.append((arg.own.shape, arg.own.dtype))
        elif isinstance(arg, Cols):
            loads.append((arg, len(inputs)))
            inputs.append(arg.array)
            buffers.append(((arg.array.shape[0], arg.stop - arg.start), arg.array.dtype))
        elif isinstance(arg, Pieces):
            loads.append((arg, len(inputs)))
            inputs += arg.blocks
            buffers.append((arg.shape, arg.dtype))
        else:
            loads.append((arg, len(inputs)))
            inputs.append(arg)
            buffers.append((arg.shape, arg.dtype))
    avals, stores, aliases = [], [], {}
    for out in outs:
        special = isinstance(out, (Owned, Routed))
        aval = out.aval if special or isinstance(out, Halved) else out
        stores.append((out, len(avals)))
        buffers.append((aval.shape, aval.dtype))
        if special and out.into is not None:
            for array in out.into:
                aliases[1 + len(inputs)] = len(avals)
                inputs.append(array)
                avals.append(aval)
        else:
            avals += [aval] * (2 if isinstance(out, Routed) else 1)
    many = sum(2 * len(a.blocks) for a in args if isinstance(a, Pieces)) + sum(isinstance(o, Halved) for o in outs)
    moved = sum(math.prod(dims) * jnp.dtype(dtype).itemsize for dims, dtype in buffers)
    inputs += after

    def kernel(where_ref, *refs):
        in_refs, refs = refs[: len(inputs)], refs[len(inputs) :]
        out_refs, refs = refs[: len(avals)], refs[len(avals) :]
        own, refs = refs[: len(scratch)], refs[len(scratch) :]
        held, sems = refs[:-1], refs[-1]
        boxes, extra = [], len(buffers)
        for n, (arg, at) in enumerate(loads):
            if isinstance(arg, Pieces):
                copies = []
                for index, rows, place in arg.places(where_ref):
                    source, target = in_refs[at + index].at[rows, :], held[n].at[place, :]
                    copies.append((None, pltpu.make_async_copy(source, target, sems.at[extra])))
                    extra += 1
                boxes.append(Box(held[n], copies))
                boxes[-1].start()
                continue
            if isinstance(arg, Pick):
                mine = where_ref[0] == arg.row
                pairs = [(mine, in_refs[at]), (jnp.logical_not(mine), in_refs[at + 1])]
            elif isinstance(arg, Cols):
                pairs = [(None, in_refs[at].at[:, arg.start : arg.stop])]
            else:
                pairs = [(None, in_refs[at])]
            boxes.append(Box(held[n], [(c, pltpu.make_async_copy(s, held[n], sems.at[n])) for c, s in pairs]))
            boxes[-1].start()
        for n, (out, at) in enumerate(stores, len(loads)):
            pairs = [(None, out_refs[at])]
            if isinstance(out, Halved):
                middle = out.aval.shape[0] // 2
                copies = []
                for rows, sem in ((pl.ds(0, middle), n), (pl.ds(middle, middle), extra)):
                    copies.append((None, pltpu.make_async_copy(held[n].at[rows, :], out_refs[at].at[rows, :], sems.at[sem])))
                extra += 1
                boxes.append(Box(held[n], copies))
                continue
            if isinstance(out, (Owned, Routed)):
                mine = where_ref[0] == out.row
                pairs = [(mine, out_refs[at])]
                if isinstance(out, Routed):
                    pairs.append((jnp.logical_not(mine), out_refs[at + 1]))
            boxes.append(Box(held[n], [(c, pltpu.make_async_copy(held[n], d, sems.at[n])) for c, d in pairs]))
        body(where_ref, *boxes, *own)
        for box in boxes:
            box.wait()

    hbm = pl.BlockSpec(memory_space=pltpu.HBM)
    return pl.pallas_call(
        kernel,
        out_shape=tuple(avals),
        in_specs=[pl.BlockSpec(memory_space=pltpu.SMEM)] + [hbm] * len(inputs),
        out_specs=tuple(hbm for _ in avals),
        scratch_shapes=[*scratch, *(pltpu.VMEM(*b) for b in buffers), pltpu.SemaphoreType.DMA((len(buffers) + many,))],
        input_output_aliases=aliases,
        compiler_params=pltpu.CompilerParams(vmem_limit_bytes=VMEM_LIMIT),
        cost_estimate=pl.CostEstimate(flops=flops, bytes_accessed=moved, transcendentals=0),
    )(where, *inputs)


def at_half(core, half):
    return pl.ds(pl.multiple_of(core * half, half), half)


def windows(length, causal):
    for lo in range(0, length, SPAN):
        yield lo, max(lo - SPAN, 0), lo + SPAN if causal else min(lo + 2 * SPAN, length)


def mask_of(segq_ref, segk_ref, lo, start, stop, causal):
    dims = (stop - start, SPAN)
    keys = start + lax.broadcasted_iota(jnp.int32, dims, 0)
    queries = lo + lax.broadcasted_iota(jnp.int32, dims, 1)
    same = segk_ref[start:stop, :] == segq_ref[:, lo : lo + SPAN]
    if causal:
        same = same & (keys <= queries)
    return same | (keys == queries)


def beside(parts):
    return jnp.concatenate(parts, axis=1)


def lanes(value, count):
    return [value[:, i * SPAN : (i + 1) * SPAN] for i in range(count)]


def attend(q_at, k_at, v_at, segq_ref, segk_ref, context_ref, lse_ref, causal, heads, factor):
    for lo, start, stop in windows(context_ref.shape[0], causal):
        mask = beside([mask_of(segq_ref, segk_ref, lo, start, stop, causal)] * heads)
        scores = beside([dot_rows(k_at(h, start, stop), q_at(h, lo, lo + SPAN) * LOW(factor)) for h in range(heads)])
        scores = jnp.where(mask, scores, MASKED)
        top = jnp.max(scores, axis=0, keepdims=True)
        expos = jnp.exp(scores - top)
        total = jnp.sum(expos, axis=0, keepdims=True)
        probs = (expos * (1.0 / total)).astype(LOW)
        logs = lanes(top + jnp.log(total), heads)
        for h, part in enumerate(lanes(probs, heads)):
            context_ref[lo : lo + SPAN, h * HD : (h + 1) * HD] = dot_inner(part, v_at(h, start, stop)).astype(LOW)
            lse_ref[h : h + 1, lo : lo + SPAN] = logs[h]


def attend_back(q_at, k_at, v_at, g_at, segq_ref, segk_ref, lse_ref, gq_ref, gk_ref, gv_ref, causal, heads, factor):
    gk_ref[...] = jnp.zeros_like(gk_ref)
    gv_ref[...] = jnp.zeros_like(gv_ref)
    for lo, start, stop in windows(lse_ref.shape[1], causal):
        mask = beside([mask_of(segq_ref, segk_ref, lo, start, stop, causal)] * heads)
        queries = [q_at(h, lo, lo + SPAN) * LOW(factor) for h in range(heads)]
        keys = [k_at(h, start, stop) for h in range(heads)]
        grads = [g_at(h, lo, lo + SPAN) for h in range(heads)]
        scores = beside([dot_rows(keys[h], queries[h]) for h in range(heads)])
        logs = beside([lse_ref[h : h + 1, lo : lo + SPAN] for h in range(heads)])
        probs = jnp.exp(jnp.where(mask, scores, MASKED) - logs)
        grad_probs = beside([dot_rows(v_at(h, start, stop), grads[h]) for h in range(heads)])
        centre = jnp.sum(probs * grad_probs, axis=0, keepdims=True)
        grad_scores = lanes((probs * (grad_probs - centre)).astype(LOW), heads)
        for h, part in enumerate(lanes(probs.astype(LOW), heads)):
            cols = slice(h * HD, (h + 1) * HD)
            gv_ref[start:stop, cols] += dot(part, grads[h])
            gk_ref[start:stop, cols] += dot(grad_scores[h], queries[h])
            gq_ref[lo : lo + SPAN, cols] = (dot_inner(grad_scores[h], keys[h]) * factor).astype(LOW)


def columns(ref, at):
    return lambda h, lo, hi: ref[lo:hi, at + h * HD : at + (h + 1) * HD]


def branch(core, pack):
    mine, other, *far = pack
    half = far[0].ref.shape[0]
    for index, box in zip((core, 1 - core), far, strict=True):
        rows = at_half(index, half)
        here = (mine.get()[rows, :].astype(WIDE) + other.get()[rows, :].astype(WIDE)).astype(LOW)
        yield rows, here.astype(WIDE) + box.get()[...].astype(WIDE)


def wide(box):
    return box.get()[...].astype(WIDE)


def norm_next(core, pack, before, gain, after, normed):
    for rows, moved in branch(core, pack):
        value = (moved + before.get()[rows, :].astype(WIDE)).astype(LOW)
        after.ref[rows, :] = value
        value = value.astype(WIDE)
        normed.ref[rows, :] = (value * rstd_of(value) * gain.get()[...]).astype(LOW)
    after.start()
    normed.start()


def self_forward(heads, factor, where, own, gain, w, segq, segk, first, qkv, context, lse, part, *whole):
    third = heads * HD
    value = wide(own)
    first.put((value * rstd_of(value) * gain.get()[...]).astype(LOW))
    w_ref = w.get()
    qkv.put(dot(first.ref[...], w_ref[:, : 3 * third]).astype(LOW))
    attend(columns(qkv.ref, 0), columns(qkv.ref, third), columns(qkv.ref, 2 * third), segq.get(), segk.get(),
           context.ref, lse.ref, True, heads, factor)
    context.start()
    lse.start()
    part.put_halves(lambda rows: dot_rows(context.ref[rows, :], w_ref[:, 3 * third : 4 * third]).astype(LOW))
    hand_on(w, whole)


def cross_forward(heads, factor, where, memory, w, before, mine, theirs, far, far_other, gain, segq, segk,
                  after, second, cq, ckv, context, lse, part):
    third = heads * HD
    memory_ref, w_ref = memory.get(), w.get()
    ckv.put(dot(memory_ref[...], w_ref[:, third : 3 * third]).astype(LOW))
    norm_next(where[0], (mine, theirs, far, far_other), before, gain, after, second)
    cq.put(dot(second.ref[...], w_ref[:, :third]).astype(LOW))
    attend(columns(cq.ref, 0), columns(ckv.ref, 0), columns(ckv.ref, third), segq.get(), segk.get(),
           context.ref, lse.ref, False, heads, factor)
    context.start()
    lse.start()
    part.put_halves(lambda rows: dot_rows(context.ref[rows, :], w_ref[:, 3 * third : 4 * third]).astype(LOW))


def ffn_forward(hidden, where, before, mine, theirs, far, far_other, gain, w, after, third, slope, active, part):
    norm_next(where[0], (mine, theirs, far, far_other), before, gain, after, third)
    w_ref = w.get()
    act, rate = gelu_parts(dot(third.ref[...], w_ref[:, :hidden]))
    active.put(act.astype(LOW))
    slope.put(rate.astype(LOW))
    part.put_halves(lambda rows: dot_rows(active.ref[rows, :], w_ref[:, hidden : 2 * hidden]).astype(LOW))


def adapt_backward(where, before, mine, theirs, far, far_other, gain, down, up, goal, weight, segk, w_out, slope, w_in,
                   low, inner, part, outputs, down_grad, up_grad, gain_grad, total_ref):
    for rows, moved in branch(where[0], (mine, theirs, far, far_other)):
        total_ref[rows, :] = moved + before.get()[rows, :].astype(WIDE)
    value = total_ref[...]
    rstd = rstd_of(value)
    normed = value * rstd
    gain_ref, down_ref, up_ref = gain.get(), down.get(), up.get()
    adapt_in = (normed * gain_ref[...]).astype(LOW)
    act, rate = gelu_parts(dot(adapt_in, down_ref[...]))
    act = act.astype(LOW)
    outputs.put(value + dot(act, up_ref[...]))
    grad_out = wide(goal) * jnp.where(segk.get()[...] >= 0, weight.get()[...], 0.0)
    out_low = grad_out.astype(LOW)
    grad_bottle = (dot_rows(out_low, up_ref[...]) * rate).astype(LOW)
    grad_in = dot_rows(grad_bottle, down_ref[...])
    gain_grad.put(jnp.sum(grad_in * normed, axis=0, keepdims=True))
    scaled = grad_in * gain_ref[...]
    total = grad_out + rstd * (scaled - normed * jnp.mean(scaled * normed, axis=-1, keepdims=True))
    low.put(total.astype(LOW))
    inner.put((dot(low.ref[...], w_out.get()[...]) * wide(slope)).astype(LOW))
    part.put(dot_rows(inner.ref[...], w_in.get()[...]).astype(LOW))
    up_grad.put(dot_inner(act, out_low).astype(LOW))
    down_grad.put(dot_inner(adapt_in, grad_bottle).astype(LOW))


def norm_back(core, pack, value, before, gain, grad, gain_grad):
    total = 0.0
    for rows, moved in branch(core, pack):
        here = value.get()[rows, :].astype(WIDE)
        rstd = rstd_of(here)
        normed = here * rstd
        total = total + jnp.sum(moved * normed, axis=0, keepdims=True)
        scaled = moved * gain.get()[...]
        here = rstd * (scaled - normed * jnp.mean(scaled * normed, axis=-1, keepdims=True))
        grad.ref[rows, :] = (here + before.get()[rows, :].astype(WIDE)).astype(grad.ref.dtype)
    grad.start()
    gain_grad.put(total)


def cross_backward(heads, factor, where, mine, theirs, far, far_other, value, before, gain, w, cq, ckv, lse, segq, segk,
                   low, gain_grad, gq, gkv, part, memory, g_ref, gk_ref, gv_ref):
    third = heads * HD
    norm_back(where[0], (mine, theirs, far, far_other), value, before, gain, low, gain_grad)
    w_ref = w.get()
    g_ref[...] = dot(low.ref[...], w_ref[:, 3 * third : 4 * third]).astype(LOW)
    attend_back(columns(cq.get(), 0), columns(ckv.get(), 0), columns(ckv.get(), third), columns(g_ref, 0), segq.get(), segk.get(),
                lse.get(), gq.ref, gk_ref, gv_ref, False, heads, factor)
    gq.start()
    part.put(dot_rows(gq.ref[...], w_ref[:, :third]).astype(LOW))
    gkv.ref[:, :third] = gk_ref[...].astype(LOW)
    gkv.ref[:, third:] = gv_ref[...].astype(LOW)
    gkv.start()
    memory.put(dot_rows(gkv.ref[...], w_ref[:, third : 3 * third]).astype(LOW))


def self_backward(heads, factor, where, mine, theirs, far, far_other, value, before, gain, w, qkv, lse, segq, segk,
                  low, gain_grad, gqkv, part, g_ref, gk_ref, gv_ref):
    third = heads * HD
    norm_back(where[0], (mine, theirs, far, far_other), value, before, gain, low, gain_grad)
    w_ref = w.get()
    g_ref[...] = dot(low.ref[...], w_ref[:, 3 * third : 4 * third]).astype(LOW)
    qkv_ref = qkv.get()
    attend_back(columns(qkv_ref, 0), columns(qkv_ref, third), columns(qkv_ref, 2 * third), columns(g_ref, 0),
                segq.get(), segk.get(), lse.get(), gqkv.ref, gk_ref, gv_ref, True, heads, factor)
    gqkv.ref[:, third : 2 * third] = gk_ref[...].astype(LOW)
    gqkv.ref[:, 2 * third :] = gv_ref[...].astype(LOW)
    gqkv.start()
    part.put_halves(lambda rows: dot_rows(gqkv.ref[rows, :], w_ref[:, : 3 * third]).astype(LOW))


def input_backward(where, mine, theirs, far, far_other, own, before, gain, grad, gain_grad):
    norm_back(where[0], (mine, theirs, far, far_other), own, before, gain, grad, gain_grad)


def pair_dot(left0, left1, right0, right1):
    return (dot_inner(left0.get()[...], right0.get()[...]) + dot_inner(left1.get()[...], right1.get()[...])).astype(LOW)


def weights_grad(widths, where, *refs):
    *boxes, out = refs
    at = 0
    for index, size in enumerate(widths):
        out.ref[:, at : at + size] = pair_dot(*boxes[4 * index : 4 * index + 4])
        at += size
    for box in boxes[4 * len(widths) :]:
        out.ref[:, at : at + box.ref.shape[1]] = box.get()[...]
    out.start()


def emit(widths, scale, where, *refs):
    count = len(refs) // (2 + len(widths))
    sums, outs = refs[: 2 * count], refs[2 * count :]
    for box in sums:
        box.wait()

    def put_in(index, first, second):
        at = 0
        for size, out in zip(widths, outs[index * len(widths) :], strict=False):
            out.ref[:, :size] = first[:, at : at + size].astype(WIDE) * scale
            out.ref[:, size:] = second[:, at : at + size].astype(WIDE) * scale
            at += size

    @pl.when(where[0] == 0)
    def _():
        for index in range(count):
            put_in(index, sums[2 * index].ref, sums[2 * index + 1].ref)

    @pl.when(where[0] != 0)
    def _():
        for index in range(count):
            put_in(index, sums[2 * index + 1].ref, sums[2 * index].ref)

    for out in outs:
        out.start()


def pick(where, generated, select, out):
    out.put(dot(generated.get()[...], select.get()[...]).astype(LOW))


def hand_on(weight, outs):
    for out in outs:
        out.put(weight.ref[...])


def pack_rows(where, *refs):
    *weights, keep, send = refs
    for weight in weights:
        weight.wait()

    def put_in(core):
        at = 0
        for weight in weights:
            size = weight.ref.shape[1] // 2
            send.ref[:, at : at + size] = weight.ref[:, (1 - core) * size : (2 - core) * size]
            keep.ref[:, at : at + size] = weight.ref[:, core * size : (core + 1) * size]
            at += size

    @pl.when(where[0] == 0)
    def _():
        put_in(0)

    @pl.when(where[0] != 0)
    def _():
        put_in(1)

    send.start()
    keep.start()


def swap_core(value):
    return lax.ppermute(value, CORE, ACROSS)


def swap_pair(value):
    return lax.ppermute(value, PAIR, ACROSS)


def solution(mesh):
    dp, mp = mesh.devices.shape
    chips = dp // 2
    grid = Mesh(mesh.devices.reshape(chips, 2, mp), (CHIP, CORE, PAIR))
    ring = chips == 8

    def local(
        inputs, encoded, cotangent, segments, padding, task_ids, token_weights, gain_self, gain_cross, gain_ffn,
        self_query, self_key, self_value, self_out, cross_query, cross_key, cross_value, cross_out, ffn_in, ffn_out,
        gen_down, gen_up, gen_gain, task_table, proj_first, proj_second,
    ):
        rows, length, width = inputs.shape
        half = length // 2
        core = lax.axis_index(CORE)
        chip = lax.axis_index(CHIP)
        z, y = chip // 2, chip % 2
        where = jnp.stack([core, z, y]).astype(jnp.int32)
        first = core == 0
        factor = HD ** (-0.5)
        tasks_all = task_table.shape[0]
        local_rows = self_query.shape[0]
        chip_rows = 2 * local_rows
        quarter = self_query.shape[1] // 2
        heads = quarter // HD
        hidden = ffn_in.shape[1] // 2
        tasks_wide = tasks_all * ADAPT
        both = range(2)

        def order(mine, other, axis=0):
            return jnp.where(
                first, jnp.concatenate([mine, other], axis), jnp.concatenate([other, mine], axis)
            )

        def part_of(value, index, size, axis=0):
            return lax.dynamic_slice_in_dim(value, index * size, size, axis)

        turns = [[(k, (k + 2 * step) % chips) for k in range(chips)] for step in (1, 2, 3)]
        side = [(k, k ^ 1) for k in range(chips)]

        def behind(value, gate):
            return value if gate is None else lax.optimization_barrier((value, gate))[0]

        def gather(weights, soon, after=()):
            total = sum(w.shape[1] // 2 for w in weights)
            if ring:
                keep, send = call(pack_rows, [shape((local_rows, total), LOW)] * 2, where, *weights, after=after)
            else:
                keep = jnp.concatenate([part_of(w, core, w.shape[1] // 2, 1) for w in weights], 1)
                send = jnp.concatenate([part_of(w, 1 - core, w.shape[1] // 2, 1) for w in weights], 1)
            moved = swap_core(send)
            if not (ring and soon):
                shard = order(keep, moved)
                return lax.all_gather(shard, CHIP, axis=0, tiled=True), shard
            shard = jnp.concatenate([keep, moved], 0)
            held = [shard]
            for _ in range(3):
                held.append(lax.ppermute(held[-1], CHIP, turns[0]))
            return Pieces(held, [lax.ppermute(h, CHIP, side) for h in held]), shard

        def sides(full):
            blocks = full.reshape(4, 2, chip_rows, full.shape[1])
            return [lax.dynamic_index_in_dim(blocks, at, 1, keepdims=False) for at in (1 - y, y)]

        def blocks_of(mine, moved):
            def block(step):
                at = (z + step) % 4
                return sum(lax.dynamic_index_in_dim(v, at, 0, keepdims=False).astype(WIDE) for v in (mine, moved))

            return block(0), [block(step).astype(LOW) for step in (1, 2, 3)]

        def away_blocks(sent):
            return [lax.ppermute(b, CHIP, turn) for b, turn in zip(sent, turns, strict=True)]

        def meet(own_block, sent, gate):
            far = away_blocks(sent)
            return own_block + sum(behind(f, gate).astype(WIDE) for f in far)

        def scatter(full):
            return lax.psum_scatter(full, CHIP, scatter_dimension=0, tiled=True)

        def halves(held):
            send = swap_core(part_of(held, 1 - core, local_rows).astype(LOW))
            return part_of(held, core, local_rows), send

        def give(widths, *sums, after=()):
            scale = 1.0 / math.sqrt(rows * dp * length)
            return call(
                functools.partial(emit, widths, scale),
                [shape((local_rows, 2 * w), WIDE) for _ in range(len(sums) // 2) for w in widths], where, *sums, after=after,
            )

        def all_sum(value):
            bit = 1
            while bit < chips:
                value = value + lax.ppermute(value, CHIP, [(k, k ^ bit) for k in range(chips)])
                bit *= 2
            return value

        def project(table, one, two):
            return exact(jax.nn.gelu(exact(table, one)), two)


        w_rest, shard_rest = gather([cross_query, cross_key, cross_value, cross_out, ffn_in, ffn_out], False)
        w_cross = Cols(w_rest, 0, 4 * quarter)
        w_ffn = Cols(w_rest, 4 * quarter, 4 * quarter + 2 * hidden)
        w_self, shard_self = gather([self_query, self_key, self_value, self_out], True, (shard_rest,))
        gate = w_self.blocks[1] if ring else shard_self
        ident_all, project_pull = jax.vjp(project, behind(task_table, gate), proj_first, proj_second)
        ident_low_all = ident_all.astype(LOW)
        gain_all = 1.0 + exact(ident_all, gen_gain)

        def spread(generator):
            made = dot(ident_low_all, generator).astype(LOW)
            made = made.reshape(tasks_all, local_rows, ADAPT).transpose(1, 0, 2)
            return made.reshape(local_rows, tasks_wide)

        down_here, up_here = spread(gen_down), spread(gen_up)
        keep, send = jnp.where(first, down_here, up_here), jnp.where(first, up_here, down_here)
        if ring:
            shard = jnp.concatenate([keep, swap_core(send)], 0)
            held = [shard, *(lax.ppermute(shard, CHIP, turn) for turn in turns)]
            generated = Pieces(held, [lax.ppermute(h, CHIP, side) for h in held])
        else:
            generated = lax.all_gather(order(keep, swap_core(send)), CHIP, axis=0, tiled=True)

        words = jnp.concatenate([segments, padding, jnp.broadcast_to(task_ids[:, None], (1, length))], 0)
        words = behind(words, gate)
        words_other = swap_core(words)
        words = [jnp.where(first, words, words_other), jnp.where(first, words_other, words)]
        own, memory, goal = (v.reshape(length, width) for v in (inputs, encoded, cotangent))
        own_other, memory_other, goal_other = swap_core(own), swap_core(memory), swap_core(goal)
        streams = [Pick(r, own, own_other) for r in both]
        memories = [Pick(r, memory, memory_other) for r in both]
        goals = [Pick(r, goal, goal_other) for r in both]
        weights = token_weights.astype(WIDE)
        onehots = [(w[2, 0] == jnp.arange(tasks_all)).astype(WIDE) for w in words]
        segqs = [w[:1] for w in words]
        segks = [jnp.where(w[1] == 1, w[0], -1)[:, None] for w in words]
        row_weights = [jnp.sum(o * weights) * (tasks_all / jnp.sum(weights)) for o in onehots]
        row_weights = [w.reshape(1, 1) for w in row_weights]
        gains_task = [exact(o[None], gain_all) for o in onehots]
        slots = lax.broadcasted_iota(jnp.int32, (tasks_wide, 2 * ADAPT), 0)
        places = lax.broadcasted_iota(jnp.int32, (tasks_wide, 2 * ADAPT), 1)
        wanted = jnp.where(places < ADAPT, words[0][2, 0], words[1][2, 0]) * ADAPT + places % ADAPT
        select = (slots == wanted).astype(LOW)
        g_self, g_cross, g_ffn = (g[None] for g in (gain_self, gain_cross, gain_ffn))

        ready = (*gains_task, *row_weights, *segks, select, g_self, g_cross, g_ffn)
        sent_early = tuple(generated.blocks[1:4]) if ring else ()
        picked = call(pick, [shape((width, 2 * ADAPT), LOW)], where, generated, select)[0]
        line = shape((1, width), WIDE)
        lse = shape((heads, length), WIDE)
        total_scratch = pltpu.VMEM((length, width), WIDE)
        unit = 2 * length * width

        def low(columns_wide):
            return shape((length, columns_wide), LOW)

        full_low = low(width)
        kept = [dict() for _ in both]
        chain, last = [], []

        def share(part, between=None):
            if last:
                part, _ = lax.optimization_barrier((part, last[0]))
            other = behind(swap_core(part), between)
            here = (part_of(part, core, half).astype(WIDE) + part_of(other, core, half).astype(WIDE)).astype(LOW)
            far = swap_pair(here)
            chain[:], last[:] = [here], [far]
            return part, other, far, swap_core(far)

        def stage(body, outs, *args, extra=(), **options):
            return call(body, outs, where, *args, after=(*chain, *extra), **options)

        def whole(weight):
            return [shape(weight.shape, LOW)] if isinstance(weight, Pieces) else []

        def forward_self(r):
            nonlocal w_self
            k = kept[r]
            k["first"], k["qkv"], k["context"], k["lse"], part, *more = stage(
                functools.partial(self_forward, heads, factor),
                [full_low, low(3 * quarter), low(quarter), lse, Halved(full_low), *whole(w_self)],
                streams[r], g_self, w_self, segqs[r], segks[r], extra=(picked,) if r else (*ready, *sent_early), flops=5 * unit * quarter,
            )
            w_self = (more or [w_self])[0]
            k["y"] = share(part)

        def forward_cross(r):
            k = kept[r]
            k["after_self"], k["second"], k["cq"], k["ckv"], k["c_context"], k["c_lse"], part = stage(
                functools.partial(cross_forward, heads, factor),
                [full_low, full_low, low(quarter), low(2 * quarter), low(quarter), lse, Halved(full_low)],
                memories[r], w_cross, streams[r], *k["y"], g_cross, segqs[r], segks[r], extra=ready if r else (),
                flops=5 * unit * quarter,
            )
            k["y"] = share(part)

        def forward_ffn(r):
            k = kept[r]
            k["after_cross"], k["third"], k["slope"], k["active"], part = stage(
                functools.partial(ffn_forward, hidden), [full_low, full_low, low(hidden), low(hidden), Halved(full_low)],
                k["after_self"], *k["y"], g_ffn, w_ffn, extra=ready,
                flops=2 * unit * hidden,
            )
            k["y"] = share(part)

        def into(r, name):
            return (kept[0][name],) if r else None

        def backward_ffn(r):
            k = kept[r]
            k["ffn_low"], k["grad_inner"], part, k["outputs"], k["grad_down"], k["grad_up"], k["grad_gain"] = stage(
                adapt_backward,
                [full_low, low(hidden), full_low, Owned(r, shape((length, width), WIDE), into(r, "outputs")),
                 shape((width, ADAPT), LOW), shape((ADAPT, width), LOW), line],
                k["after_cross"], *k["y"], gains_task[r], *made[r], goals[r], row_weights[r], segks[r],
                Cols(w_rest, w_ffn.start + hidden, w_ffn.stop), k["slope"], Cols(w_rest, w_ffn.start, w_ffn.start + hidden),
                flops=2 * unit * hidden + 5 * unit * 128, scratch=[total_scratch],
            )
            k["y"] = share(part)

        grads_scratch = [pltpu.VMEM((length, quarter), LOW)] + [pltpu.VMEM((length, quarter), WIDE)] * 2

        def backward_cross(r):
            k = kept[r]
            k["cross_low"], k["g3"], k["gcq"], k["gckv"], part, *k["memory"] = stage(
                functools.partial(cross_backward, heads, factor),
                [full_low, line, low(quarter), low(2 * quarter), full_low, Routed(r, full_low, kept[0]["memory"] if r else None)],
                *k["y"], k["after_cross"], k["ffn_low"], g_ffn, w_cross, k["cq"], k["ckv"], k["c_lse"], segqs[r], segks[r],
                flops=7 * unit * quarter, scratch=grads_scratch,
            )
            k["y"] = share(part)

        def backward_self(r, work=None):
            k = kept[r]
            k["self_low"], k["g2"], k["gqkv"], part = stage(
                functools.partial(self_backward, heads, factor), [full_low, line, low(3 * quarter), Halved(full_low)],
                *k["y"], k["after_self"], k["cross_low"], g_cross, w_self, k["qkv"], k["lse"], segqs[r], segks[r],
                flops=7 * unit * quarter, scratch=grads_scratch,
            )
            if work is not None:
                k["sum"] = work()
            k["y"] = share(part, k.get("sum"))
            k["far"] = k["y"][2]

        def backward_input(r, after):
            k = kept[r]
            k["grad_x"], k["g1"] = call(
                input_backward, [Owned(r, shape((length, width), WIDE), into(r, "grad_x")), line],
                where, *k["y"], streams[r], k["self_low"], g_self, after=after,
            )

        def pairs(*names):
            return [kept[r][name] for name in names for r in both]

        for r in both:
            forward_self(r)

        picked_other = swap_core(picked)
        downs = jnp.where(first, picked, picked_other)
        ups = jnp.where(first, picked_other, picked)
        made = [(downs[:, r * ADAPT : (r + 1) * ADAPT], ups[:, r * ADAPT : (r + 1) * ADAPT].reshape(ADAPT, width)) for r in both]
        ready = tuple(m for pair in made for m in pair)
        for r in both:
            forward_cross(r)
        for r in both:
            forward_ffn(r)
        for r in both:
            backward_ffn(r)
        tasks_here = dot_rows(
            jnp.concatenate([jnp.where(first, kept[r]["grad_down"], kept[r]["grad_up"].reshape(width, ADAPT)) for r in both], 1),
            select,
        ).astype(LOW)
        sum_ffn = call(
            functools.partial(weights_grad, [hidden, hidden]), [shape((width, 2 * hidden + tasks_wide), LOW)], where,
            *pairs("third", "grad_inner", "ffn_low", "active"), tasks_here, after=tuple(chain), flops=4 * unit * hidden,
        )[0]
        held_ffn = scatter(sum_ffn)
        for r in both:
            backward_cross(r)
        sum_cross = (
            call(
                functools.partial(weights_grad, [quarter, 2 * quarter, quarter]), [shape((width, 4 * quarter), LOW)], where,
                *pairs("second", "gcq"), *memories, *pairs("gckv", "cross_low", "c_context"), after=tuple(chain),
                flops=8 * unit * quarter,
            )[0]
        )
        if ring:
            away, mine = sides(sum_cross)
            moved = lax.ppermute(away, CHIP, side)
        chain += [away] if ring else [sum_cross]
        backward_self(0)
        cross = (mine, moved) if ring else ()

        def self_sum():
            return call(
                functools.partial(weights_grad, [3 * quarter, quarter]), [shape((width, 4 * quarter), LOW)], where,
                *pairs("first", "gqkv", "self_low", "context"), after=cross[1:], flops=8 * unit * quarter,
            )[0]

        backward_self(1, self_sum)
        sum_self = kept[1]["sum"]
        if ring:
            away, mine = sides(sum_self)
            own_cross, sent_cross = blocks_of(cross[0], behind(cross[1], away))
            backward_input(0, (*chain, away, *sent_cross))
            moved = behind(lax.ppermute(away, CHIP, side), kept[0]["g1"])
            own_self, sent_self = blocks_of(mine, moved)
            backward_input(1, tuple(sent_self))
            held_cross = meet(own_cross, sent_cross, sent_self[0])
            far_self = away_blocks(sent_self)
            held_self = own_self + sum(behind(f, kept[1]["g1"]).astype(WIDE) for f in far_self)
        else:
            backward_input(0, ())
            backward_input(1, ())
            held_cross, held_self = scatter(sum_cross), scatter(sum_self)
        parts_ffn = halves(behind(held_ffn, sent_self[2] if ring else chain[0]))
        found_mine, found_other = (p[:, 2 * hidden :].astype(WIDE) * (1.0 / math.sqrt(rows * dp * length)) for p in parts_ffn)
        found = order(found_mine, found_other, 1)
        given = give([quarter] * 4, *halves(held_cross), *halves(held_self))
        grads_cross, grads_self = given[:4], given[4:]
        scale = 1.0 / math.sqrt(rows * dp * length)

        keep, send = kept[1]["memory"]
        memory_part = (behind(keep, sum_self).astype(WIDE) + swap_core(send).astype(WIDE)).astype(LOW)
        memory_part = behind(memory_part, kept[0]["far"])
        grad_memory = memory_part.astype(WIDE) + swap_pair(memory_part).astype(WIDE)

        def narrow(value):
            value = value.reshape(local_rows, tasks_all, ADAPT).transpose(1, 0, 2)
            return value.reshape(tasks_all, local_rows * ADAPT).astype(LOW)

        found_down, found_up = narrow(found[:, :tasks_wide]), narrow(found[:, tasks_wide:])
        grad_gen_down = dot_inner(ident_low_all, found_down)
        grad_gen_up = dot_inner(ident_low_all, found_up)
        ident_part = dot_rows(found_down, gen_down) + dot_rows(found_up, gen_up)
        ident_part = ident_part + swap_core(ident_part)
        ident_pad = jnp.pad(ident_part, ((0, 0), (0, width - ident_part.shape[1])))
        grad_in, grad_outer = give([hidden, hidden], *parts_ffn, after=(ident_pad, kept[1]["g1"]))
        gain_part = sum(onehots[r][:, None] * behind(kept[r]["grad_gain"], sum_self) for r in both) * scale
        norms = [sum(kept[r][name] for r in both) for name in ("g1", "g2", "g3")]
        sums = all_sum(jnp.concatenate([gain_part, ident_pad, *norms], 0))
        gain_sum, ident_sum = sums[:tasks_all], sums[tasks_all : 2 * tasks_all, : ident_part.shape[1]]
        norm_sums = sums[2 * tasks_all :] * scale
        grad_gen_gain = exact(ident_all, gain_sum, ((0,), (0,)))
        grad_ident = ident_sum + exact(gain_sum, gen_gain, ((1,), (1,)))
        grad_table, grad_first_m, grad_second_m = project_pull(grad_ident)

        def shaped(value):
            return value.reshape(rows, length, width)

        return (
            shaped(kept[1]["outputs"]), shaped(kept[1]["grad_x"]), shaped(grad_memory), norm_sums[0], norm_sums[1], norm_sums[2],
            *grads_self, *grads_cross, grad_in, grad_outer, grad_gen_down, grad_gen_up,
            grad_gen_gain, grad_table, grad_first_m, grad_second_m,
        )

    data = (CHIP, CORE)
    three, matrix = P(data, None, None), P(data, PAIR)
    in_specs = (
        three, three, three, P(data, None), P(data, None), P(data), P(), P(), P(), P(),
        *(matrix,) * 10, P(None, data), P(None, data), P(), P(), P(), P(),
    )
    out_specs = (
        three, three, three, P(), P(), P(), *(matrix,) * 10, P(None, data), P(None, data), P(), P(), P(), P(),
    )
    return jax.shard_map(local, mesh=grid, in_specs=in_specs, out_specs=out_specs, check_vma=False)
```

```python
import functools
import math

import jax
import jax.numpy as jnp
from jax import lax
from jax.experimental import pallas as pl
from jax.experimental.pallas import tpu as pltpu
from jax.sharding import Mesh
from jax.sharding import PartitionSpec as P

HD = 64
ADAPT = 24
HIGHEST = lax.Precision.HIGHEST
EPSILON = 1e-06
MASKED = -1000000000.0
LOW = jnp.bfloat16
WIDE = jnp.float32
CHIP, CORE, PAIR = "chip", "core", "mp"
ACROSS = [(0, 1), (1, 0)]
SPAN = 128
ROOT = math.sqrt(2.0 / math.pi)


def dot(left, right):
    return lax.dot_general(left, right, (((1,), (0,)), ((), ())), preferred_element_type=WIDE)


def dot_rows(left, right):
    return lax.dot_general(left, right, (((1,), (1,)), ((), ())), preferred_element_type=WIDE)


def dot_inner(left, right):
    return lax.dot_general(left, right, (((0,), (0,)), ((), ())), preferred_element_type=WIDE)


def exact(left, right, dims=((1,), (0,))):
    return lax.dot_general(left, right, (dims, ((), ())), precision=HIGHEST, preferred_element_type=WIDE)


def rstd_of(value):
    return lax.rsqrt(jnp.mean(value * value, axis=-1, keepdims=True) + EPSILON)


def gelu_parts(value):
    square = value * value
    slope = jnp.tanh(ROOT * (value + 0.044715 * square * value))
    half = 0.5 * (1.0 + slope)
    return value * half, half + 0.5 * value * (1.0 - slope * slope) * ROOT * (1.0 + 0.134145 * square)


def shape(dims, dtype):
    return jax.ShapeDtypeStruct(dims, dtype)


class Cols:
    def __init__(self, array, start, stop):
        self.array, self.start, self.stop = array, start, stop


class Pick:
    def __init__(self, row, own, other):
        self.row, self.own, self.other = row, own, other


class Pieces:
    def __init__(self, held, other):
        self.blocks = [*held, *other]
        self.size = held[0].shape[0]
        self.shape = (len(self.blocks) * self.size, held[0].shape[1])
        self.dtype = held[0].dtype

    def places(self, where):
        part = self.size // 2
        for index in range(len(self.blocks)):
            z = lax.rem(where[1] + 4 - index % 4, 4)
            y = where[2] if index < 4 else 1 - where[2]
            for side in range(2):
                turn = where[0] if side == 0 else 1 - where[0]
                at = pl.multiple_of((2 * z + y) * self.size + turn * part, 16)
                yield index, slice(side * part, (side + 1) * part), pl.ds(at, part)


class Owned:
    def __init__(self, row, aval, into):
        self.row, self.aval, self.into = row, aval, into


class Halved:
    def __init__(self, aval):
        self.aval = aval


class Routed:
    def __init__(self, row, aval, into):
        self.row, self.aval, self.into = row, aval, into


class Box:
    def __init__(self, ref, copies):
        self.ref, self.copies, self.pending = ref, copies, False

    def each(self, act):
        for condition, copy in self.copies:
            if condition is None:
                act(copy)
            else:
                pl.when(condition)(functools.partial(act, copy))

    def start(self):
        self.each(lambda copy: copy.start())
        self.pending = True

    def wait(self):
        if self.pending:
            self.each(lambda copy: copy.wait())
            self.pending = False

    def get(self):
        self.wait()
        return self.ref

    def put(self, value):
        self.ref[...] = value
        self.start()

    def put_halves(self, make):
        middle = self.ref.shape[0] // 2
        for index, (_, copy) in enumerate(self.copies):
            rows = slice(index * middle, (index + 1) * middle)
            self.ref[rows, :] = make(rows)
            copy.start()
        self.pending = True


VMEM_LIMIT = 60 * 1024 * 1024


def call(body, outs, where, *args, after=(), flops=0, scratch=()):
    inputs, buffers, loads = [], [], []
    for arg in args:
        if isinstance(arg, Pick):
            loads.append((arg, len(inputs)))
            inputs += [arg.own, arg.other]
            buffers.append((arg.own.shape, arg.own.dtype))
        elif isinstance(arg, Cols):
            loads.append((arg, len(inputs)))
            inputs.append(arg.array)
            buffers.append(((arg.array.shape[0], arg.stop - arg.start), arg.array.dtype))
        elif isinstance(arg, Pieces):
            loads.append((arg, len(inputs)))
            inputs += arg.blocks
            buffers.append((arg.shape, arg.dtype))
        else:
            loads.append((arg, len(inputs)))
            inputs.append(arg)
            buffers.append((arg.shape, arg.dtype))
    avals, stores, aliases = [], [], {}
    for out in outs:
        special = isinstance(out, (Owned, Routed))
        aval = out.aval if special or isinstance(out, Halved) else out
        stores.append((out, len(avals)))
        buffers.append((aval.shape, aval.dtype))
        if special and out.into is not None:
            for array in out.into:
                aliases[1 + len(inputs)] = len(avals)
                inputs.append(array)
                avals.append(aval)
        else:
            avals += [aval] * (2 if isinstance(out, Routed) else 1)
    many = sum(2 * len(a.blocks) for a in args if isinstance(a, Pieces)) + sum(isinstance(o, Halved) for o in outs)
    moved = sum(math.prod(dims) * jnp.dtype(dtype).itemsize for dims, dtype in buffers)
    inputs += after

    def kernel(where_ref, *refs):
        in_refs, refs = refs[: len(inputs)], refs[len(inputs) :]
        out_refs, refs = refs[: len(avals)], refs[len(avals) :]
        own, refs = refs[: len(scratch)], refs[len(scratch) :]
        held, sems = refs[:-1], refs[-1]
        boxes, extra = [], len(buffers)
        for n, (arg, at) in enumerate(loads):
            if isinstance(arg, Pieces):
                copies = []
                for index, rows, place in arg.places(where_ref):
                    source, target = in_refs[at + index].at[rows, :], held[n].at[place, :]
                    copies.append((None, pltpu.make_async_copy(source, target, sems.at[extra])))
                    extra += 1
                boxes.append(Box(held[n], copies))
                boxes[-1].start()
                continue
            if isinstance(arg, Pick):
                mine = where_ref[0] == arg.row
                pairs = [(mine, in_refs[at]), (jnp.logical_not(mine), in_refs[at + 1])]
            elif isinstance(arg, Cols):
                pairs = [(None, in_refs[at].at[:, arg.start : arg.stop])]
            else:
                pairs = [(None, in_refs[at])]
            boxes.append(Box(held[n], [(c, pltpu.make_async_copy(s, held[n], sems.at[n])) for c, s in pairs]))
            boxes[-1].start()
        for n, (out, at) in enumerate(stores, len(loads)):
            pairs = [(None, out_refs[at])]
            if isinstance(out, Halved):
                middle = out.aval.shape[0] // 2
                copies = []
                for rows, sem in ((pl.ds(0, middle), n), (pl.ds(middle, middle), extra)):
                    copies.append((None, pltpu.make_async_copy(held[n].at[rows, :], out_refs[at].at[rows, :], sems.at[sem])))
                extra += 1
                boxes.append(Box(held[n], copies))
                continue
            if isinstance(out, (Owned, Routed)):
                mine = where_ref[0] == out.row
                pairs = [(mine, out_refs[at])]
                if isinstance(out, Routed):
                    pairs.append((jnp.logical_not(mine), out_refs[at + 1]))
            boxes.append(Box(held[n], [(c, pltpu.make_async_copy(held[n], d, sems.at[n])) for c, d in pairs]))
        body(where_ref, *boxes, *own)
        for box in boxes:
            box.wait()

    hbm = pl.BlockSpec(memory_space=pltpu.HBM)
    return pl.pallas_call(
        kernel,
        out_shape=tuple(avals),
        in_specs=[pl.BlockSpec(memory_space=pltpu.SMEM)] + [hbm] * len(inputs),
        out_specs=tuple(hbm for _ in avals),
        scratch_shapes=[*scratch, *(pltpu.VMEM(*b) for b in buffers), pltpu.SemaphoreType.DMA((len(buffers) + many,))],
        input_output_aliases=aliases,
        compiler_params=pltpu.CompilerParams(vmem_limit_bytes=VMEM_LIMIT),
        cost_estimate=pl.CostEstimate(flops=flops, bytes_accessed=moved, transcendentals=0),
    )(where, *inputs)


def at_half(core, half):
    return pl.ds(pl.multiple_of(core * half, half), half)


def windows(length, causal):
    for lo in range(0, length, SPAN):
        yield lo, max(lo - SPAN, 0), lo + SPAN if causal else min(lo + 2 * SPAN, length)


def mask_of(segq_ref, segk_ref, lo, start, stop, causal):
    dims = (stop - start, SPAN)
    keys = start + lax.broadcasted_iota(jnp.int32, dims, 0)
    queries = lo + lax.broadcasted_iota(jnp.int32, dims, 1)
    same = segk_ref[start:stop, :] == segq_ref[:, lo : lo + SPAN]
    if causal:
        same = same & (keys <= queries)
    return same | (keys == queries)


def beside(parts):
    return jnp.concatenate(parts, axis=1)


def lanes(value, count):
    return [value[:, i * SPAN : (i + 1) * SPAN] for i in range(count)]


def attend(q_at, k_at, v_at, segq_ref, segk_ref, context_ref, lse_ref, causal, heads, factor):
    for lo, start, stop in windows(context_ref.shape[0], causal):
        mask = beside([mask_of(segq_ref, segk_ref, lo, start, stop, causal)] * heads)
        scores = beside([dot_rows(k_at(h, start, stop), q_at(h, lo, lo + SPAN) * LOW(factor)) for h in range(heads)])
        scores = jnp.where(mask, scores, MASKED)
        top = jnp.max(scores, axis=0, keepdims=True)
        expos = jnp.exp(scores - top)
        total = jnp.sum(expos, axis=0, keepdims=True)
        probs = (expos * (1.0 / total)).astype(LOW)
        logs = lanes(top + jnp.log(total), heads)
        for h, part in enumerate(lanes(probs, heads)):
            context_ref[lo : lo + SPAN, h * HD : (h + 1) * HD] = dot_inner(part, v_at(h, start, stop)).astype(LOW)
            lse_ref[h : h + 1, lo : lo + SPAN] = logs[h]


def attend_back(q_at, k_at, v_at, g_at, segq_ref, segk_ref, lse_ref, gq_ref, gk_ref, gv_ref, causal, heads, factor):
    gk_ref[...] = jnp.zeros_like(gk_ref)
    gv_ref[...] = jnp.zeros_like(gv_ref)
    for lo, start, stop in windows(lse_ref.shape[1], causal):
        mask = beside([mask_of(segq_ref, segk_ref, lo, start, stop, causal)] * heads)
        queries = [q_at(h, lo, lo + SPAN) * LOW(factor) for h in range(heads)]
        keys = [k_at(h, start, stop) for h in range(heads)]
        grads = [g_at(h, lo, lo + SPAN) for h in range(heads)]
        scores = beside([dot_rows(keys[h], queries[h]) for h in range(heads)])
        logs = beside([lse_ref[h : h + 1, lo : lo + SPAN] for h in range(heads)])
        probs = jnp.exp(jnp.where(mask, scores, MASKED) - logs)
        grad_probs = beside([dot_rows(v_at(h, start, stop), grads[h]) for h in range(heads)])
        centre = jnp.sum(probs * grad_probs, axis=0, keepdims=True)
        grad_scores = lanes((probs * (grad_probs - centre)).astype(LOW), heads)
        for h, part in enumerate(lanes(probs.astype(LOW), heads)):
            cols = slice(h * HD, (h + 1) * HD)
            gv_ref[start:stop, cols] += dot(part, grads[h])
            gk_ref[start:stop, cols] += dot(grad_scores[h], queries[h])
            gq_ref[lo : lo + SPAN, cols] = (dot_inner(grad_scores[h], keys[h]) * factor).astype(LOW)


def columns(ref, at):
    return lambda h, lo, hi: ref[lo:hi, at + h * HD : at + (h + 1) * HD]


def branch(core, pack):
    mine, other, *far = pack
    half = far[0].ref.shape[0]
    for index, box in zip((core, 1 - core), far, strict=True):
        rows = at_half(index, half)
        here = (mine.get()[rows, :].astype(WIDE) + other.get()[rows, :].astype(WIDE)).astype(LOW)
        yield rows, here.astype(WIDE) + box.get()[...].astype(WIDE)


def wide(box):
    return box.get()[...].astype(WIDE)


def norm_next(core, pack, before, gain, after, normed):
    for rows, moved in branch(core, pack):
        value = (moved + before.get()[rows, :].astype(WIDE)).astype(LOW)
        after.ref[rows, :] = value
        value = value.astype(WIDE)
        normed.ref[rows, :] = (value * rstd_of(value) * gain.get()[...]).astype(LOW)
    after.start()
    normed.start()


def self_forward(heads, factor, where, own, gain, w, segq, segk, first, qkv, context, lse, part, *whole):
    third = heads * HD
    value = wide(own)
    first.put((value * rstd_of(value) * gain.get()[...]).astype(LOW))
    w_ref = w.get()
    qkv.put(dot(first.ref[...], w_ref[:, : 3 * third]).astype(LOW))
    attend(columns(qkv.ref, 0), columns(qkv.ref, third), columns(qkv.ref, 2 * third), segq.get(), segk.get(),
           context.ref, lse.ref, True, heads, factor)
    context.start()
    lse.start()
    part.put_halves(lambda rows: dot_rows(context.ref[rows, :], w_ref[:, 3 * third : 4 * third]).astype(LOW))
    hand_on(w, whole)


def cross_forward(heads, factor, where, memory, w, before, mine, theirs, far, far_other, gain, segq, segk,
                  after, second, cq, ckv, context, lse, part):
    third = heads * HD
    memory_ref, w_ref = memory.get(), w.get()
    ckv.put(dot(memory_ref[...], w_ref[:, third : 3 * third]).astype(LOW))
    norm_next(where[0], (mine, theirs, far, far_other), before, gain, after, second)
    cq.put(dot(second.ref[...], w_ref[:, :third]).astype(LOW))
    attend(columns(cq.ref, 0), columns(ckv.ref, 0), columns(ckv.ref, third), segq.get(), segk.get(),
           context.ref, lse.ref, False, heads, factor)
    context.start()
    lse.start()
    part.put_halves(lambda rows: dot_rows(context.ref[rows, :], w_ref[:, 3 * third : 4 * third]).astype(LOW))


def ffn_forward(hidden, where, before, mine, theirs, far, far_other, gain, w, after, third, slope, active, part):
    norm_next(where[0], (mine, theirs, far, far_other), before, gain, after, third)
    w_ref = w.get()
    act, rate = gelu_parts(dot(third.ref[...], w_ref[:, :hidden]))
    active.put(act.astype(LOW))
    slope.put(rate.astype(LOW))
    part.put_halves(lambda rows: dot_rows(active.ref[rows, :], w_ref[:, hidden : 2 * hidden]).astype(LOW))


def adapt_backward(where, before, mine, theirs, far, far_other, gain, down, up, goal, weight, segk, w_out, slope, w_in,
                   low, inner, part, outputs, down_grad, up_grad, gain_grad, total_ref):
    for rows, moved in branch(where[0], (mine, theirs, far, far_other)):
        total_ref[rows, :] = moved + before.get()[rows, :].astype(WIDE)
    value = total_ref[...]
    rstd = rstd_of(value)
    normed = value * rstd
    gain_ref, down_ref, up_ref = gain.get(), down.get(), up.get()
    adapt_in = (normed * gain_ref[...]).astype(LOW)
    act, rate = gelu_parts(dot(adapt_in, down_ref[...]))
    act = act.astype(LOW)
    outputs.put(value + dot(act, up_ref[...]))
    grad_out = wide(goal) * jnp.where(segk.get()[...] >= 0, weight.get()[...], 0.0)
    out_low = grad_out.astype(LOW)
    grad_bottle = (dot_rows(out_low, up_ref[...]) * rate).astype(LOW)
    grad_in = dot_rows(grad_bottle, down_ref[...])
    gain_grad.put(jnp.sum(grad_in * normed, axis=0, keepdims=True))
    scaled = grad_in * gain_ref[...]
    total = grad_out + rstd * (scaled - normed * jnp.mean(scaled * normed, axis=-1, keepdims=True))
    low.put(total.astype(LOW))
    inner.put((dot(low.ref[...], w_out.get()[...]) * wide(slope)).astype(LOW))
    part.put(dot_rows(inner.ref[...], w_in.get()[...]).astype(LOW))
    up_grad.put(dot_inner(act, out_low).astype(LOW))
    down_grad.put(dot_inner(adapt_in, grad_bottle).astype(LOW))


def norm_back(core, pack, value, before, gain, grad, gain_grad):
    total = 0.0
    for rows, moved in branch(core, pack):
        here = value.get()[rows, :].astype(WIDE)
        rstd = rstd_of(here)
        normed = here * rstd
        total = total + jnp.sum(moved * normed, axis=0, keepdims=True)
        scaled = moved * gain.get()[...]
        here = rstd * (scaled - normed * jnp.mean(scaled * normed, axis=-1, keepdims=True))
        grad.ref[rows, :] = (here + before.get()[rows, :].astype(WIDE)).astype(grad.ref.dtype)
    grad.start()
    gain_grad.put(total)


def cross_backward(heads, factor, where, mine, theirs, far, far_other, value, before, gain, w, cq, ckv, lse, segq, segk,
                   low, gain_grad, gq, gkv, part, memory, g_ref, gk_ref, gv_ref):
    third = heads * HD
    norm_back(where[0], (mine, theirs, far, far_other), value, before, gain, low, gain_grad)
    w_ref = w.get()
    g_ref[...] = dot(low.ref[...], w_ref[:, 3 * third : 4 * third]).astype(LOW)
    attend_back(columns(cq.get(), 0), columns(ckv.get(), 0), columns(ckv.get(), third), columns(g_ref, 0), segq.get(), segk.get(),
                lse.get(), gq.ref, gk_ref, gv_ref, False, heads, factor)
    gq.start()
    part.put(dot_rows(gq.ref[...], w_ref[:, :third]).astype(LOW))
    gkv.ref[:, :third] = gk_ref[...].astype(LOW)
    gkv.ref[:, third:] = gv_ref[...].astype(LOW)
    gkv.start()
    memory.put(dot_rows(gkv.ref[...], w_ref[:, third : 3 * third]).astype(LOW))


def self_backward(heads, factor, where, mine, theirs, far, far_other, value, before, gain, w, qkv, lse, segq, segk,
                  low, gain_grad, gqkv, part, g_ref, gk_ref, gv_ref):
    third = heads * HD
    norm_back(where[0], (mine, theirs, far, far_other), value, before, gain, low, gain_grad)
    w_ref = w.get()
    g_ref[...] = dot(low.ref[...], w_ref[:, 3 * third : 4 * third]).astype(LOW)
    qkv_ref = qkv.get()
    attend_back(columns(qkv_ref, 0), columns(qkv_ref, third), columns(qkv_ref, 2 * third), columns(g_ref, 0),
                segq.get(), segk.get(), lse.get(), gqkv.ref, gk_ref, gv_ref, True, heads, factor)
    gqkv.ref[:, third : 2 * third] = gk_ref[...].astype(LOW)
    gqkv.ref[:, 2 * third :] = gv_ref[...].astype(LOW)
    gqkv.start()
    part.put_halves(lambda rows: dot_rows(gqkv.ref[rows, :], w_ref[:, : 3 * third]).astype(LOW))


def input_backward(where, mine, theirs, far, far_other, own, before, gain, grad, gain_grad):
    norm_back(where[0], (mine, theirs, far, far_other), own, before, gain, grad, gain_grad)


def pair_dot(left0, left1, right0, right1):
    return (dot_inner(left0.get()[...], right0.get()[...]) + dot_inner(left1.get()[...], right1.get()[...])).astype(LOW)


def weights_grad(widths, where, *refs):
    *boxes, out = refs
    at = 0
    for index, size in enumerate(widths):
        out.ref[:, at : at + size] = pair_dot(*boxes[4 * index : 4 * index + 4])
        at += size
    for box in boxes[4 * len(widths) :]:
        out.ref[:, at : at + box.ref.shape[1]] = box.get()[...]
    out.start()


def emit(widths, scale, where, *refs):
    count = len(refs) // (2 + len(widths))
    sums, outs = refs[: 2 * count], refs[2 * count :]
    for box in sums:
        box.wait()

    def put_in(index, first, second):
        at = 0
        for size, out in zip(widths, outs[index * len(widths) :], strict=False):
            out.ref[:, :size] = first[:, at : at + size].astype(WIDE) * scale
            out.ref[:, size:] = second[:, at : at + size].astype(WIDE) * scale
            at += size

    @pl.when(where[0] == 0)
    def _():
        for index in range(count):
            put_in(index, sums[2 * index].ref, sums[2 * index + 1].ref)

    @pl.when(where[0] != 0)
    def _():
        for index in range(count):
            put_in(index, sums[2 * index + 1].ref, sums[2 * index].ref)

    for out in outs:
        out.start()


def pick(where, generated, select, out):
    out.put(dot(generated.get()[...], select.get()[...]).astype(LOW))


def hand_on(weight, outs):
    for out in outs:
        out.put(weight.ref[...])


def pack_rows(where, *refs):
    *weights, keep, send = refs
    for weight in weights:
        weight.wait()

    def put_in(core):
        at = 0
        for weight in weights:
            size = weight.ref.shape[1] // 2
            send.ref[:, at : at + size] = weight.ref[:, (1 - core) * size : (2 - core) * size]
            keep.ref[:, at : at + size] = weight.ref[:, core * size : (core + 1) * size]
            at += size

    @pl.when(where[0] == 0)
    def _():
        put_in(0)

    @pl.when(where[0] != 0)
    def _():
        put_in(1)

    send.start()
    keep.start()


def swap_core(value):
    return lax.ppermute(value, CORE, ACROSS)


def swap_pair(value):
    return lax.ppermute(value, PAIR, ACROSS)


def solution(mesh):
    dp, mp = mesh.devices.shape
    chips = dp // 2
    grid = Mesh(mesh.devices.reshape(chips, 2, mp), (CHIP, CORE, PAIR))
    ring = chips == 8

    def local(
        inputs, encoded, cotangent, segments, padding, task_ids, token_weights, gain_self, gain_cross, gain_ffn,
        self_query, self_key, self_value, self_out, cross_query, cross_key, cross_value, cross_out, ffn_in, ffn_out,
        gen_down, gen_up, gen_gain, task_table, proj_first, proj_second,
    ):
        rows, length, width = inputs.shape
        half = length // 2
        core = lax.axis_index(CORE)
        chip = lax.axis_index(CHIP)
        z, y = chip // 2, chip % 2
        where = jnp.stack([core, z, y]).astype(jnp.int32)
        first = core == 0
        factor = HD ** (-0.5)
        tasks_all = task_table.shape[0]
        local_rows = self_query.shape[0]
        chip_rows = 2 * local_rows
        quarter = self_query.shape[1] // 2
        heads = quarter // HD
        hidden = ffn_in.shape[1] // 2
        tasks_wide = tasks_all * ADAPT
        both = range(2)

        def order(mine, other, axis=0):
            return jnp.where(
                first, jnp.concatenate([mine, other], axis), jnp.concatenate([other, mine], axis)
            )

        def part_of(value, index, size, axis=0):
            return lax.dynamic_slice_in_dim(value, index * size, size, axis)

        turns = [[(k, (k + 2 * step) % chips) for k in range(chips)] for step in (1, 2, 3)]
        side = [(k, k ^ 1) for k in range(chips)]

        def behind(value, gate):
            return value if gate is None else lax.optimization_barrier((value, gate))[0]

        def gather(weights, soon, after=()):
            total = sum(w.shape[1] // 2 for w in weights)
            if ring:
                keep, send = call(pack_rows, [shape((local_rows, total), LOW)] * 2, where, *weights, after=after)
            else:
                keep = jnp.concatenate([part_of(w, core, w.shape[1] // 2, 1) for w in weights], 1)
                send = jnp.concatenate([part_of(w, 1 - core, w.shape[1] // 2, 1) for w in weights], 1)
            moved = swap_core(send)
            if not (ring and soon):
                shard = order(keep, moved)
                return lax.all_gather(shard, CHIP, axis=0, tiled=True), shard
            shard = jnp.concatenate([keep, moved], 0)
            held = [shard]
            for _ in range(3):
                held.append(lax.ppermute(held[-1], CHIP, turns[0]))
            return Pieces(held, [lax.ppermute(h, CHIP, side) for h in held]), shard

        def sides(full):
            blocks = full.reshape(4, 2, chip_rows, full.shape[1])
            return [lax.dynamic_index_in_dim(blocks, at, 1, keepdims=False) for at in (1 - y, y)]

        def blocks_of(mine, moved):
            def block(step):
                at = (z + step) % 4
                return sum(lax.dynamic_index_in_dim(v, at, 0, keepdims=False).astype(WIDE) for v in (mine, moved))

            return block(0), [block(step).astype(LOW) for step in (1, 2, 3)]

        def away_blocks(sent):
            return [lax.ppermute(b, CHIP, turn) for b, turn in zip(sent, turns, strict=True)]

        def meet(own_block, sent, gate):
            far = away_blocks(sent)
            return own_block + sum(behind(f, gate).astype(WIDE) for f in far)

        def scatter(full):
            return lax.psum_scatter(full, CHIP, scatter_dimension=0, tiled=True)

        def halves(held):
            send = swap_core(part_of(held, 1 - core, local_rows).astype(LOW))
            return part_of(held, core, local_rows), send

        def give(widths, *sums, after=()):
            scale = 1.0 / math.sqrt(rows * dp * length)
            return call(
                functools.partial(emit, widths, scale),
                [shape((local_rows, 2 * w), WIDE) for _ in range(len(sums) // 2) for w in widths], where, *sums, after=after,
            )

        def all_sum(value):
            bit = 1
            while bit < chips:
                value = value + lax.ppermute(value, CHIP, [(k, k ^ bit) for k in range(chips)])
                bit *= 2
            return value

        def project(table, one, two):
            return exact(jax.nn.gelu(exact(table, one)), two)


        w_rest, shard_rest = gather([cross_query, cross_key, cross_value, cross_out, ffn_in, ffn_out], False)
        w_cross = Cols(w_rest, 0, 4 * quarter)
        w_ffn = Cols(w_rest, 4 * quarter, 4 * quarter + 2 * hidden)
        w_self, shard_self = gather([self_query, self_key, self_value, self_out], True, (shard_rest,))
        gate = w_self.blocks[1] if ring else shard_self
        ident_all, project_pull = jax.vjp(project, behind(task_table, gate), proj_first, proj_second)
        ident_low_all = ident_all.astype(LOW)
        gain_all = 1.0 + exact(ident_all, gen_gain)

        def spread(generator):
            made = dot(ident_low_all, generator).astype(LOW)
            made = made.reshape(tasks_all, local_rows, ADAPT).transpose(1, 0, 2)
            return made.reshape(local_rows, tasks_wide)

        down_here, up_here = spread(gen_down), spread(gen_up)
        keep, send = jnp.where(first, down_here, up_here), jnp.where(first, up_here, down_here)
        if ring:
            shard = jnp.concatenate([keep, swap_core(send)], 0)
            held = [shard, *(lax.ppermute(shard, CHIP, turn) for turn in turns)]
            generated = Pieces(held, [lax.ppermute(h, CHIP, side) for h in held])
        else:
            generated = lax.all_gather(order(keep, swap_core(send)), CHIP, axis=0, tiled=True)

        words = jnp.concatenate([segments, padding, jnp.broadcast_to(task_ids[:, None], (1, length))], 0)
        words = behind(words, gate)
        words_other = swap_core(words)
        words = [jnp.where(first, words, words_other), jnp.where(first, words_other, words)]
        own, memory, goal = (v.reshape(length, width) for v in (inputs, encoded, cotangent))
        own_other, memory_other, goal_other = swap_core(own), swap_core(memory), swap_core(goal)
        streams = [Pick(r, own, own_other) for r in both]
        memories = [Pick(r, memory, memory_other) for r in both]
        goals = [Pick(r, goal, goal_other) for r in both]
        weights = token_weights.astype(WIDE)
        onehots = [(w[2, 0] == jnp.arange(tasks_all)).astype(WIDE) for w in words]
        segqs = [w[:1] for w in words]
        segks = [jnp.where(w[1] == 1, w[0], -1)[:, None] for w in words]
        row_weights = [jnp.sum(o * weights) * (tasks_all / jnp.sum(weights)) for o in onehots]
        row_weights = [w.reshape(1, 1) for w in row_weights]
        gains_task = [exact(o[None], gain_all) for o in onehots]
        slots = lax.broadcasted_iota(jnp.int32, (tasks_wide, 2 * ADAPT), 0)
        places = lax.broadcasted_iota(jnp.int32, (tasks_wide, 2 * ADAPT), 1)
        wanted = jnp.where(places < ADAPT, words[0][2, 0], words[1][2, 0]) * ADAPT + places % ADAPT
        select = (slots == wanted).astype(LOW)
        g_self, g_cross, g_ffn = (g[None] for g in (gain_self, gain_cross, gain_ffn))

        ready = (*gains_task, *row_weights, *segks, select, g_self, g_cross, g_ffn)
        sent_early = tuple(generated.blocks[1:4]) if ring else ()
        picked = call(pick, [shape((width, 2 * ADAPT), LOW)], where, generated, select)[0]
        line = shape((1, width), WIDE)
        lse = shape((heads, length), WIDE)
        total_scratch = pltpu.VMEM((length, width), WIDE)
        unit = 2 * length * width

        def low(columns_wide):
            return shape((length, columns_wide), LOW)

        full_low = low(width)
        kept = [dict() for _ in both]
        chain, last = [], []

        def share(part, between=None):
            if last:
                part, _ = lax.optimization_barrier((part, last[0]))
            other = behind(swap_core(part), between)
            here = (part_of(part, core, half).astype(WIDE) + part_of(other, core, half).astype(WIDE)).astype(LOW)
            far = swap_pair(here)
            chain[:], last[:] = [here], [far]
            return part, other, far, swap_core(far)

        def stage(body, outs, *args, extra=(), **options):
            return call(body, outs, where, *args, after=(*chain, *extra), **options)

        def whole(weight):
            return [shape(weight.shape, LOW)] if isinstance(weight, Pieces) else []

        def forward_self(r):
            nonlocal w_self
            k = kept[r]
            k["first"], k["qkv"], k["context"], k["lse"], part, *more = stage(
                functools.partial(self_forward, heads, factor),
                [full_low, low(3 * quarter), low(quarter), lse, Halved(full_low), *whole(w_self)],
                streams[r], g_self, w_self, segqs[r], segks[r], extra=(picked,) if r else (*ready, *sent_early), flops=5 * unit * quarter,
            )
            w_self = (more or [w_self])[0]
            k["y"] = share(part)

        def forward_cross(r):
            k = kept[r]
            k["after_self"], k["second"], k["cq"], k["ckv"], k["c_context"], k["c_lse"], part = stage(
                functools.partial(cross_forward, heads, factor),
                [full_low, full_low, low(quarter), low(2 * quarter), low(quarter), lse, Halved(full_low)],
                memories[r], w_cross, streams[r], *k["y"], g_cross, segqs[r], segks[r], extra=ready if r else (),
                flops=5 * unit * quarter,
            )
            k["y"] = share(part)

        def forward_ffn(r):
            k = kept[r]
            k["after_cross"], k["third"], k["slope"], k["active"], part = stage(
                functools.partial(ffn_forward, hidden), [full_low, full_low, low(hidden), low(hidden), Halved(full_low)],
                k["after_self"], *k["y"], g_ffn, w_ffn, extra=ready,
                flops=2 * unit * hidden,
            )
            k["y"] = share(part)

        def into(r, name):
            return (kept[0][name],) if r else None

        def backward_ffn(r):
            k = kept[r]
            k["ffn_low"], k["grad_inner"], part, k["outputs"], k["grad_down"], k["grad_up"], k["grad_gain"] = stage(
                adapt_backward,
                [full_low, low(hidden), full_low, Owned(r, shape((length, width), WIDE), into(r, "outputs")),
                 shape((width, ADAPT), LOW), shape((ADAPT, width), LOW), line],
                k["after_cross"], *k["y"], gains_task[r], *made[r], goals[r], row_weights[r], segks[r],
                Cols(w_rest, w_ffn.start + hidden, w_ffn.stop), k["slope"], Cols(w_rest, w_ffn.start, w_ffn.start + hidden),
                flops=2 * unit * hidden + 5 * unit * 128, scratch=[total_scratch],
            )
            k["y"] = share(part)

        grads_scratch = [pltpu.VMEM((length, quarter), LOW)] + [pltpu.VMEM((length, quarter), WIDE)] * 2

        def backward_cross(r):
            k = kept[r]
            k["cross_low"], k["g3"], k["gcq"], k["gckv"], part, *k["memory"] = stage(
                functools.partial(cross_backward, heads, factor),
                [full_low, line, low(quarter), low(2 * quarter), full_low, Routed(r, full_low, kept[0]["memory"] if r else None)],
                *k["y"], k["after_cross"], k["ffn_low"], g_ffn, w_cross, k["cq"], k["ckv"], k["c_lse"], segqs[r], segks[r],
                flops=7 * unit * quarter, scratch=grads_scratch,
            )
            k["y"] = share(part)

        def backward_self(r, work=None):
            k = kept[r]
            k["self_low"], k["g2"], k["gqkv"], part = stage(
                functools.partial(self_backward, heads, factor), [full_low, line, low(3 * quarter), Halved(full_low)],
                *k["y"], k["after_self"], k["cross_low"], g_cross, w_self, k["qkv"], k["lse"], segqs[r], segks[r],
                flops=7 * unit * quarter, scratch=grads_scratch,
            )
            if work is not None:
                k["sum"] = work()
            k["y"] = share(part, k.get("sum"))
            k["far"] = k["y"][2]

        def backward_input(r, after):
            k = kept[r]
            k["grad_x"], k["g1"] = call(
                input_backward, [Owned(r, shape((length, width), WIDE), into(r, "grad_x")), line],
                where, *k["y"], streams[r], k["self_low"], g_self, after=after,
            )

        def pairs(*names):
            return [kept[r][name] for name in names for r in both]

        for r in both:
            forward_self(r)

        picked_other = swap_core(picked)
        downs = jnp.where(first, picked, picked_other)
        ups = jnp.where(first, picked_other, picked)
        made = [(downs[:, r * ADAPT : (r + 1) * ADAPT], ups[:, r * ADAPT : (r + 1) * ADAPT].reshape(ADAPT, width)) for r in both]
        ready = tuple(m for pair in made for m in pair)
        for r in both:
            forward_cross(r)
        for r in both:
            forward_ffn(r)
        for r in both:
            backward_ffn(r)
        tasks_here = dot_rows(
            jnp.concatenate([jnp.where(first, kept[r]["grad_down"], kept[r]["grad_up"].reshape(width, ADAPT)) for r in both], 1),
            select,
        ).astype(LOW)
        sum_ffn = call(
            functools.partial(weights_grad, [hidden, hidden]), [shape((width, 2 * hidden + tasks_wide), LOW)], where,
            *pairs("third", "grad_inner", "ffn_low", "active"), tasks_here, after=tuple(chain), flops=4 * unit * hidden,
        )[0]
        held_ffn = scatter(sum_ffn)
        for r in both:
            backward_cross(r)
        sum_cross = (
            call(
                functools.partial(weights_grad, [quarter, 2 * quarter, quarter]), [shape((width, 4 * quarter), LOW)], where,
                *pairs("second", "gcq"), *memories, *pairs("gckv", "cross_low", "c_context"), after=tuple(chain),
                flops=8 * unit * quarter,
            )[0]
        )
        if ring:
            away, mine = sides(sum_cross)
            moved = lax.ppermute(away, CHIP, side)
        chain += [away] if ring else [sum_cross]
        backward_self(0)
        cross = (mine, moved) if ring else ()

        def self_sum():
            return call(
                functools.partial(weights_grad, [3 * quarter, quarter]), [shape((width, 4 * quarter), LOW)], where,
                *pairs("first", "gqkv", "self_low", "context"), after=cross[1:], flops=8 * unit * quarter,
            )[0]

        backward_self(1, self_sum)
        sum_self = kept[1]["sum"]
        if ring:
            away, mine = sides(sum_self)
            own_cross, sent_cross = blocks_of(cross[0], behind(cross[1], away))
            backward_input(0, (*chain, away, *sent_cross))
            moved = behind(lax.ppermute(away, CHIP, side), kept[0]["g1"])
            own_self, sent_self = blocks_of(mine, moved)
            backward_input(1, tuple(sent_self))
            held_cross = meet(own_cross, sent_cross, kept[1]["g1"])
            far_self = away_blocks(sent_self)
            held_self = own_self + sum(behind(f, kept[1]["g1"]).astype(WIDE) for f in far_self)
        else:
            backward_input(0, ())
            backward_input(1, ())
            held_cross, held_self = scatter(sum_cross), scatter(sum_self)
        parts_ffn = halves(behind(held_ffn, sent_self[2] if ring else chain[0]))
        found_mine, found_other = (p[:, 2 * hidden :].astype(WIDE) * (1.0 / math.sqrt(rows * dp * length)) for p in parts_ffn)
        found = order(found_mine, found_other, 1)
        given = give([quarter] * 4, *halves(held_cross), *halves(held_self))
        grads_cross, grads_self = given[:4], given[4:]
        scale = 1.0 / math.sqrt(rows * dp * length)

        keep, send = kept[1]["memory"]
        memory_part = (behind(keep, sum_self).astype(WIDE) + swap_core(send).astype(WIDE)).astype(LOW)
        memory_part = behind(memory_part, kept[0]["far"])
        grad_memory = memory_part.astype(WIDE) + swap_pair(memory_part).astype(WIDE)

        def narrow(value):
            value = value.reshape(local_rows, tasks_all, ADAPT).transpose(1, 0, 2)
            return value.reshape(tasks_all, local_rows * ADAPT).astype(LOW)

        found_down, found_up = narrow(found[:, :tasks_wide]), narrow(found[:, tasks_wide:])
        ident_last = behind(ident_low_all, kept[1]["g1"])
        grad_gen_down = dot_inner(ident_last, found_down)
        grad_gen_up = dot_inner(ident_last, found_up)
        ident_part = dot_rows(found_down, gen_down) + dot_rows(found_up, gen_up)
        ident_part = ident_part + swap_core(ident_part)
        ident_pad = jnp.pad(ident_part, ((0, 0), (0, width - ident_part.shape[1])))
        grad_in, grad_outer = give([hidden, hidden], *parts_ffn, after=(ident_pad, kept[1]["g1"]))
        gain_part = sum(onehots[r][:, None] * behind(kept[r]["grad_gain"], sum_self) for r in both) * scale
        norms = [sum(kept[r][name] for r in both) for name in ("g1", "g2", "g3")]
        sums = all_sum(jnp.concatenate([gain_part, ident_pad, *norms], 0))
        gain_sum, ident_sum = sums[:tasks_all], sums[tasks_all : 2 * tasks_all, : ident_part.shape[1]]
        norm_sums = sums[2 * tasks_all :] * scale
        grad_gen_gain = exact(ident_all, gain_sum, ((0,), (0,)))
        grad_ident = ident_sum + exact(gain_sum, gen_gain, ((1,), (1,)))
        grad_table, grad_first_m, grad_second_m = project_pull(grad_ident)

        def shaped(value):
            return value.reshape(rows, length, width)

        return (
            shaped(kept[1]["outputs"]), shaped(kept[1]["grad_x"]), shaped(grad_memory), norm_sums[0], norm_sums[1], norm_sums[2],
            *grads_self, *grads_cross, grad_in, grad_outer, grad_gen_down, grad_gen_up,
            grad_gen_gain, grad_table, grad_first_m, grad_second_m,
        )

    data = (CHIP, CORE)
    three, matrix = P(data, None, None), P(data, PAIR)
    in_specs = (
        three, three, three, P(data, None), P(data, None), P(data), P(), P(), P(), P(),
        *(matrix,) * 10, P(None, data), P(None, data), P(), P(), P(), P(),
    )
    out_specs = (
        three, three, three, P(), P(), P(), *(matrix,) * 10, P(None, data), P(None, data), P(), P(), P(), P(),
    )
    return jax.shard_map(local, mesh=grid, in_specs=in_specs, out_specs=out_specs, check_vma=False)
```
